256 devices in a mesh: dp: 32 (over z, y), fsdp: 8 (over x, core).
Axes of the slice: x: 4, y: 4, z: 8, core: 2. Of those that a mesh axis runs over, the one named last changes fastest.
Arguments:
- frames: bfloat16 [8, 768, 32, 1536], P('fsdp', 'dp'), may hold values from -6 to 6
- ln_gain: float32 [1536], replicated, may hold values from 0.5 to 1.5
- w_in: bfloat16 [1536, 3072], P(('dp', 'fsdp')), may hold values from -0.15625 to 0.15625
- depth_kernel: float32 [31, 1536], replicated, may hold values from -1 to 1
- bn_scale: float32 [1536], replicated, may hold values from 0.5 to 1.5
- bn_shift: float32 [1536], replicated, may hold values from -3 to 3
- w_out: bfloat16 [1536, 1536], P(('dp', 'fsdp')), may hold values from -0.15625 to 0.15625
- lengths: int32 [8, 32, 24], P('fsdp'), may hold values from 0 to 32, as said below
- destinations: int32 [8, 32, 24], P('fsdp'), may hold values from 0 to 31, as said below
- offsets: int32 [8, 32, 24], P('fsdp'), may hold values from 0 to 224, as said below
Outputs:
- encoded: bfloat16 [8, 256, 32, 1536], P('fsdp', 'dp')
The draws below stay inside these ranges and needn't reach their ends.
Inputs may be any that keep to these rules, and one draw needn't show every extreme that they name: lengths: live slots come first in a loader and hold half of 32 to 32 frames; 0 marks an empty slot. In each group the busiest loader has all 24 slots live, the group has 256 live utterances, and one of them has 32 frames. destinations: within a group a loader sends at most one live utterance to a device, and every device receives exactly 8 live utterances. Empty slots hold 0. offsets: multiples of 32; the 8 live utterances received by one device have distinct offsets. Empty slots hold 0.
All inputs are finite; a program needn't handle non-finite values.
Results may differ from the reference program's by a relative error of at most 0.003.
Values may be sent and summed in bfloat16 or wider, within the bound.
A program may use at most 128 MiB of HBM per device.

```python
import jax
import jax.numpy as jnp
from jax import lax

D = 1536
KERNEL = 31
MAXLEN = 32
RSLOT = 8
UTT = 24
N_DP = 32
N_FSDP = 8


def group_tables(group_key):
    key_one, key_two, key_three = jax.random.split(group_key, 3)
    base_counts = jnp.full((N_DP,), RSLOT, dtype=jnp.int32)
    base_counts = base_counts.at[0].set(UTT)
    base_counts = base_counts.at[1:1 + 2 * RSLOT].set(RSLOT - 1)
    order = jax.random.permutation(key_one, N_DP)
    counts = base_counts[order]
    slot_ids = jnp.arange(UTT, dtype=jnp.int32)
    live_mask = slot_ids[None, :] < counts[:, None]
    starts = jnp.cumsum(counts) - counts
    stream_index = starts[:, None] + slot_ids[None, :]
    device_order = jax.random.permutation(key_two, N_DP).astype(jnp.int32)
    dest_table = jnp.where(live_mask, device_order[stream_index % N_DP], 0)
    off_table = jnp.where(live_mask, stream_index // N_DP * MAXLEN, 0)
    raw_lengths = jax.random.randint(key_three, (N_DP, UTT), MAXLEN // 2, MAXLEN + 1)
    forced = (counts[:, None] == UTT) & (slot_ids[None, :] == 0)
    raw_lengths = jnp.where(forced, MAXLEN, raw_lengths)
    len_table = jnp.where(live_mask, raw_lengths, 0)
    return (len_table.astype(jnp.int32), dest_table.astype(jnp.int32), off_table.astype(jnp.int32))


def all_tables(key):
    group_keys = jax.random.split(jax.random.fold_in(key, 71), N_FSDP)
    return jax.vmap(group_tables)(group_keys)


def draw_lengths(key, part):
    return all_tables(key)[0]


def draw_destinations(key, part):
    return all_tables(key)[1]


def draw_offsets(key, part):
    return all_tables(key)[2]


def block_scale(stream_key, shape, pieces, smallest, high):
    gain = 1.0
    for position, parts in pieces:
        draws = jax.random.uniform(jax.random.fold_in(jax.random.fold_in(stream_key, 6), position), (parts,), jnp.float32, smallest / len(pieces), high / len(pieces))
        gain = gain * jnp.repeat(jnp.exp(draws), shape[position] // parts).reshape((-1,) + (1,) * (len(shape) - 1 - position))
    return gain


def bell_draw(rng, shape, deviation, reach, cuts=(), kind=jnp.bfloat16):
    loudness = block_scale(rng, shape, cuts, -0.22, 0.18) if cuts else 1.0
    array = jax.random.normal(rng, shape, jnp.float32) * deviation * loudness
    return jnp.minimum(jnp.maximum(array, -reach), reach).astype(kind)


def setup_inputs(seed: int = 0) -> dict:
    keys = jax.random.split(jax.random.key(seed), 11)
    frames = bell_draw(keys[0], (N_FSDP, N_DP * UTT, MAXLEN, D), 1.0, 6.0, ((0, 8), (1, 32)))
    ln_gain = jnp.clip(1.0 + 0.1 * jax.random.normal(keys[1], (D,), jnp.float32), 0.5, 1.5)
    w_in = bell_draw(keys[2], (D, 2 * D), D ** -0.5, 0.15625, ((0, 256),))
    depth_kernel = bell_draw(keys[3], (KERNEL, D), KERNEL ** -0.5, 1.0, (), jnp.float32)
    bn_scale = jnp.clip(1.0 + 0.1 * jax.random.normal(keys[4], (D,), jnp.float32), 0.5, 1.5)
    bn_shift = bell_draw(keys[5], (D,), 0.5, 3.0, (), jnp.float32)
    w_out = bell_draw(keys[6], (D, D), D ** -0.5, 0.15625, ((0, 256),))
    lengths = draw_lengths(jax.random.fold_in(keys[10], 71), 0)
    destinations = draw_destinations(jax.random.fold_in(keys[10], 71), 0)
    offsets = draw_offsets(jax.random.fold_in(keys[10], 71), 0)
    return {"frames": frames, "ln_gain": ln_gain, "w_in": w_in, "depth_kernel": depth_kernel, "bn_scale": bn_scale, "bn_shift": bn_shift, "w_out": w_out, "lengths": lengths, "destinations": destinations, "offsets": offsets}


def conv_module(blocks, utt_lengths, ln_gain, w_in, depth_kernel, bn_scale, bn_shift, w_out):
    block_count, frames_len, feature_width = blocks.shape
    wide_rows = blocks.reshape(block_count * frames_len, feature_width).astype(jnp.float32)
    row_mean = lax.optimization_barrier(jnp.mean(wide_rows, axis=1, keepdims=True))
    centred = wide_rows - row_mean
    row_var = lax.optimization_barrier(jnp.mean(centred * centred, axis=1, keepdims=True))
    normed = (centred * lax.rsqrt(row_var + 1e-05) * ln_gain).astype(jnp.bfloat16)
    glu_in = jnp.dot(normed, w_in, preferred_element_type=jnp.float32)
    gated_units = glu_in[:, :feature_width] * jax.nn.sigmoid(glu_in[:, feature_width:])
    gated_units = gated_units.reshape(block_count, frames_len, feature_width)
    valid_mask = jnp.arange(frames_len, dtype=jnp.int32)[None, :] < utt_lengths[:, None]
    gated_units = jnp.where(valid_mask[:, :, None], gated_units, jnp.zeros((), gated_units.dtype))
    side_reach = (KERNEL - 1) // 2
    padded = jnp.pad(gated_units, ((0, 0), (side_reach, side_reach), (0, 0)))
    convolved = padded[:, 0:frames_len, :] * depth_kernel[0]
    for kernel_tap in range(1, KERNEL):
        convolved = convolved + padded[:, kernel_tap:kernel_tap + frames_len, :] * depth_kernel[kernel_tap]
    shifted = convolved * bn_scale + bn_shift
    activated = (shifted * jax.nn.sigmoid(shifted)).astype(jnp.bfloat16)
    activated = activated.reshape(block_count * frames_len, feature_width)
    mixed_out = wide_rows + jnp.dot(activated, w_out, preferred_element_type=jnp.float32)
    mixed_out = mixed_out.reshape(block_count, frames_len, feature_width)
    mixed_out = jnp.where(valid_mask[:, :, None], mixed_out, jnp.zeros((), mixed_out.dtype))
    return mixed_out.astype(jnp.bfloat16)

def reference(frames, ln_gain, w_in, depth_kernel, bn_scale, bn_shift, w_out, lengths, destinations, offsets):

    def one_group(group_data):
        group_frames, tab_len, tab_dest, tab_off = group_data
        key_table = jnp.where(tab_len > 0, tab_dest * RSLOT + tab_off // MAXLEN, -1).reshape(-1)
        targets = jnp.arange(N_DP * RSLOT, dtype=jnp.int32)
        match_table = (key_table[None, :] == targets[:, None]).astype(jnp.int32)
        slot_numbers = jnp.arange(N_DP * UTT, dtype=jnp.int32)
        source = lax.optimization_barrier(jnp.sum(match_table * slot_numbers[None, :], axis=1)).astype(jnp.int32)
        recv_len = lax.optimization_barrier(jnp.sum(match_table * tab_len.reshape(-1)[None, :], axis=1)).astype(jnp.int32)
        blocks = jnp.take(group_frames, source, axis=0)
        return conv_module(blocks, recv_len, ln_gain, w_in, depth_kernel, bn_scale, bn_shift, w_out)
    return lax.map(one_group, (frames, lengths, destinations, offsets))
```

```python
import jax
import jax.numpy as jnp
from jax import lax
from jax.experimental import pallas as pl
from jax.experimental.pallas import tpu as pltpu
from jax.sharding import PartitionSpec as P

MESH = pl.DeviceIdType.MESH

D = 1536
KERNEL = 31
MAXLEN = 32
RSLOT = 8
NZ, NY, NX, NC = 8, 4, 4, 2
N_DP = NZ * NY
SHARD_ROWS = 6
BLOCK_ROWS = 24
CHUNK = D // NX
BLOCK_COLS = 3 * CHUNK
PAD = 16

OFFSETS = sorted(
    [(dz, dy) for dz in range(NZ) for dy in range(NY) if (dz, dy) != (0, 0)],
    key=lambda o: -(min(o[0], NZ - o[0]) * 8 + min(o[1], NY - o[1])),
)
ISSUE = (6, 8, 12, 16, 20, 26, 31)


def comm_kernel(
    chosen, wp, arr, full, parts, block,
    a2a_send, a2a_recv, part_send, part_recv, block_sem,
    zu_send, zu_recv, zd_send, zd_recv,
    yu_send, yu_recv, yd_send, yd_recv,
    xu_send, xu_recv, xd_send, xd_recv,
    core_send, core_recv,
):
    dp = lax.axis_index("dp")
    fs = lax.axis_index("fsdp")
    z, y = dp // NY, dp % NY
    x, c = fs // NC, fs % NC
    other = 1 - c

    def dev(zz, yy, xx, cc):
        return (lax.rem(zz, NZ) * NY + lax.rem(yy, NY), lax.rem(xx, NX) * NC + cc)

    barrier = pltpu.get_barrier_semaphore()
    for dz, dy in OFFSETS:
        pl.semaphore_signal(barrier, inc=1, device_id=dev(z + dz, y + dy, x, c), device_id_type=MESH)
    for k in range(1, NX * NC):
        peer = lax.rem(fs + k, NX * NC)
        pl.semaphore_signal(barrier, inc=1, device_id=(dp, peer), device_id_type=MESH)
    pl.semaphore_wait(barrier, len(OFFSETS) + NX * NC - 1)

    def remote(src, dst, send, recv, device):
        return pltpu.make_async_remote_copy(
            src_ref=src, dst_ref=dst, send_sem=send, recv_sem=recv, device_id=device, device_id_type=MESH
        )

    started = []

    def start(copy):
        copy.start()
        started.append(copy)

    def frames_until(count):
        for i in range(len(frame_copies), count):
            dz, dy = OFFSETS[i]
            target = dev(z + dz, y + dy, x, c)
            copy = remote(chosen.at[target[0]], arr.at[dp], a2a_send.at[i], a2a_recv.at[i], target)
            copy.start()
            frame_copies.append(copy)

    frame_copies = []

    slot = lax.rem(x, 2) * NC + c
    keeper = x // 2
    for t in range(NX):
        same = jnp.logical_and(x == t, keeper == c)

        @pl.when(jnp.logical_not(same))
        def _():
            remote(wp.at[t], parts.at[slot], part_send.at[t], part_recv.at[slot], (dp, t * NC + keeper)).start()

        @pl.when(same)
        def _():
            pltpu.make_async_copy(wp.at[t], parts.at[slot], block_sem.at[0]).start()

    frames_until(ISSUE[0])

    for k in range(4):
        source = c * 4 + k

        @pl.when(source != fs)
        def _():
            remote(wp.at[0], parts.at[k], part_send.at[0], part_recv.at[k], (dp, fs)).wait_recv()

        @pl.when(source == fs)
        def _():
            pltpu.make_async_copy(wp.at[0], parts.at[k], block_sem.at[0]).wait()

    row = lax.broadcasted_iota(jnp.int32, (BLOCK_ROWS, 32), 0)
    col = lax.broadcasted_iota(jnp.int32, (BLOCK_ROWS, 32), 1)
    pick = (col == (row // SHARD_ROWS) * 8 + lax.rem(row, SHARD_ROWS)).astype(jnp.bfloat16)
    block[...] = jnp.dot(
        pick, parts[...].reshape(32, BLOCK_COLS), preferred_element_type=jnp.float32
    ).astype(jnp.bfloat16)

    own = pltpu.make_async_copy(block, full.at[x, z, y, c], block_sem.at[1])
    own.start()

    up, down = dev(z + 1, y, x, c), dev(z + NZ - 1, y, x, c)

    def z_up(s):
        src = lax.rem(z + NZ - s, NZ)
        return remote(block if s == 0 else full.at[x, src, y, c], full.at[x, src, y, c], zu_send.at[s], zu_recv.at[s], up)

    def z_down(s):
        src = lax.rem(z + s, NZ)
        return remote(block if s == 0 else full.at[x, src, y, c], full.at[x, src, y, c], zd_send.at[s], zd_recv.at[s], down)

    def z_landed(s, sign):
        src = lax.rem(z + NZ + sign * (s + 1), NZ)
        recv = zu_recv if sign < 0 else zd_recv
        ref = full.at[x, src, y, c]
        return remote(ref, ref, zu_send.at[s], recv.at[s], up)

    start(z_up(0))
    start(z_down(0))
    for s in range(4):
        frames_until(ISSUE[1 + s])
        z_landed(s, -1).wait_recv()
        if s < 3:
            start(z_up(s + 1))
            z_landed(s, 1).wait_recv()
            if s < 2:
                start(z_down(s + 1))
    own.wait()

    def piece(xx, yy, half=None):
        rows = slice(None) if half is None else pl.ds(half * 4, 4)
        return full.at[lax.rem(xx, NX), rows, lax.rem(yy, NY), c]

    y_up, y_down = dev(z, y + 1, x, c), dev(z, y + NY - 1, x, c)
    x_up, x_down = dev(z, y, x + 1, c), dev(z, y, x + NX - 1, c)
    sibling = (dp, x * NC + other)

    def send(ref, s_sem, r_sem, device):
        start(remote(ref, ref, s_sem, r_sem, device))

    def landed(ref, r_sem):
        remote(ref, ref, yu_send.at[0], r_sem, sibling).wait_recv()

    def to_core(dx, j, ref):
        send(ref, core_send.at[dx * 5 + j], core_recv.at[dx * 5 + j], sibling)

    def x_start(j, ref):
        send(ref, xu_send.at[j], xu_recv.at[j], x_up)
        send(ref, xd_send.at[j], xd_recv.at[j], x_down)
        to_core(0, j, ref)

    mine = piece(x, y)
    send(mine, yu_send.at[0], yu_recv.at[0], y_up)
    send(mine, yd_send.at[0], yd_recv.at[0], y_down)
    x_start(0, mine)
    frames_until(ISSUE[5])

    landed(piece(x, y + 3), yu_recv.at[0])
    send(piece(x, y + 3, 0), yu_send.at[1], yu_recv.at[1], y_up)
    x_start(1, piece(x, y + 3))
    landed(piece(x, y + 1), yd_recv.at[0])
    send(piece(x, y + 1, 1), yd_send.at[1], yd_recv.at[1], y_down)
    x_start(2, piece(x, y + 1))
    frames_until(ISSUE[6])

    rows_of = [(0, None), (3, None), (1, None), (2, 0), (2, 1)]

    def x_landed(j, first):
        dy, half = rows_of[j]
        lo, hi = (0, 1) if half is None else (half, half)
        landed(piece(x + 3, y + dy, half), xu_recv.at[j])
        landed(piece(x + 1, y + dy, half), xd_recv.at[j])
        if half is None:
            send(piece(x + 3, y + dy, 0), xu_send.at[5 + j], xu_recv.at[5 + j], x_up)
            send(piece(x + 1, y + dy, 1), xd_send.at[5 + j], xd_recv.at[5 + j], x_down)
        elif half == 0:
            send(piece(x + 3, y + dy, 0), xu_send.at[5 + j], xu_recv.at[5 + j], x_up)
        else:
            send(piece(x + 1, y + dy, 1), xd_send.at[5 + j], xd_recv.at[5 + j], x_down)
        to_core(1, j, piece(x + 3, y + dy, half))
        to_core(2, j, piece(x + 1, y + dy, half))

    def x_far_landed(j):
        dy, half = rows_of[j]
        if half in (None, 0):
            landed(piece(x + 2, y + dy, 0), xu_recv.at[5 + j])
        if half in (None, 1):
            landed(piece(x + 2, y + dy, 1), xd_recv.at[5 + j])
        to_core(3, j, piece(x + 2, y + dy, half))

    x_landed(0, True)
    landed(piece(x, y + 2, 0), yu_recv.at[1])
    x_start(3, piece(x, y + 2, 0))
    landed(piece(x, y + 2, 1), yd_recv.at[1])
    x_start(4, piece(x, y + 2, 1))
    for j in range(1, 5):
        x_landed(j, True)
        x_far_landed(j - 1)
    x_far_landed(4)

    for dx in range(NX):
        for j in range(5):
            dy, half = rows_of[j]
            rows = slice(None) if half is None else pl.ds(half * 4, 4)
            xx = lax.rem(x + (0, 3, 1, 2)[dx], NX)
            landed(full.at[xx, rows, lax.rem(y + dy, NY), other], core_recv.at[dx * 5 + j])

    for i, (dz, dy) in enumerate(OFFSETS):
        sender = dev(z + NZ - dz, y + NY - dy, x, c)[0]
        landed(arr.at[sender], a2a_recv.at[i])

    for t in range(NX):
        same = jnp.logical_and(x == t, keeper == c)

        @pl.when(jnp.logical_not(same))
        def _():
            remote(wp.at[t], parts.at[0], part_send.at[t], part_recv.at[0], sibling).wait_send()

    for copy in started + frame_copies:
        copy.wait_send()


def communicate(chosen, wp):
    dma = pltpu.SemaphoreType.DMA
    return pl.pallas_call(
        comm_kernel,
        out_shape=(
            jax.ShapeDtypeStruct((N_DP, MAXLEN, D), jnp.bfloat16),
            jax.ShapeDtypeStruct((NX, NZ, NY, NC, BLOCK_ROWS, BLOCK_COLS), jnp.bfloat16),
        ),
        in_specs=[pl.BlockSpec(memory_space=pl.ANY)] * 2,
        out_specs=(pl.BlockSpec(memory_space=pl.ANY), pl.BlockSpec(memory_space=pl.ANY)),
        scratch_shapes=[
            pltpu.VMEM((4, 8, BLOCK_COLS), jnp.bfloat16),
            pltpu.VMEM((BLOCK_ROWS, BLOCK_COLS), jnp.bfloat16),
            dma((31,)), dma((31,)), dma((4,)), dma((4,)), dma((2,)),
            dma((4,)), dma((4,)), dma((3,)), dma((3,)),
            dma((2,)), dma((2,)), dma((2,)), dma((2,)),
            dma((10,)), dma((10,)), dma((10,)), dma((10,)),
            dma((20,)), dma((20,)),
        ],
        compiler_params=pltpu.CompilerParams(collective_id=0, has_side_effects=True),
        name="exchange",
    )(chosen, wp)


def module_kernel(
    source, length, me, arr, chosen, full, gain, taps, scale, shift, out,
    xbuf, wbuf, normed, hidden, window, act, x_sem, w_sem,
):
    for r in range(RSLOT):
        @pl.when(source[r] != me[0])
        def _():
            pltpu.make_async_copy(arr.at[source[r]], xbuf.at[r], x_sem.at[r]).start()

        @pl.when(source[r] == me[0])
        def _():
            pltpu.make_async_copy(chosen.at[source[r]], xbuf.at[r], x_sem.at[r]).start()
    loads = [pltpu.make_async_copy(full.at[i], wbuf.at[i], w_sem.at[i]) for i in range(NX)]
    for load in loads:
        load.start()

    window[...] = jnp.zeros_like(window)
    for r in range(RSLOT):
        pltpu.make_async_copy(arr.at[0], xbuf.at[r], x_sem.at[r]).wait()

    def norm(r, carry):
        wide = xbuf[r].astype(jnp.float32)
        mean = jnp.mean(wide, axis=1, keepdims=True)
        centred = wide - mean
        var = jnp.mean(centred * centred, axis=1, keepdims=True)
        normed[pl.ds(pl.multiple_of(r * MAXLEN, MAXLEN), MAXLEN), :] = (
            centred * lax.rsqrt(var + 1e-05) * gain[...]
        ).astype(jnp.bfloat16)
        return carry

    lax.fori_loop(0, RSLOT, norm, 0)

    step_ids = lax.broadcasted_iota(jnp.int32, (MAXLEN, 128), 0)
    for i in range(NX):
        loads[i].wait()
        hidden[...] = jnp.dot(normed[...], wbuf[i, :, 0 : 2 * CHUNK], preferred_element_type=jnp.float32)
        for b in range(CHUNK // 128):
            lane = slice(i * CHUNK + b * 128, i * CHUNK + b * 128 + 128)
            tap = [jnp.broadcast_to(taps[k : k + 1, lane], (8, 128)) for k in range(KERNEL)]
            mul = jnp.broadcast_to(scale[:, lane], (16, 128))
            add = jnp.broadcast_to(shift[:, lane], (16, 128))

            def conv(r, carry):
                base = pl.multiple_of(r * MAXLEN, MAXLEN)
                value = hidden[pl.ds(base, MAXLEN), b * 128 : b * 128 + 128]
                gate = hidden[pl.ds(base, MAXLEN), CHUNK + b * 128 : CHUNK + b * 128 + 128]
                gated = jnp.where(step_ids < length[r], value * jax.nn.sigmoid(gate), 0.0)
                window[r, PAD : PAD + MAXLEN, :] = gated
                for pair in range(2):
                    tiles = []
                    for t in (2 * pair, 2 * pair + 1):
                        total = None
                        for k in range(KERNEL):
                            first = 8 * t + k - 15
                            if first + 7 < 0 or first > MAXLEN - 1:
                                continue
                            term = window[r, PAD + first : PAD + first + 8, :] * tap[k]
                            total = term if total is None else total + term
                        tiles.append(total)
                    s = jnp.concatenate(tiles, axis=0) * mul + add
                    act[pl.ds(pl.multiple_of(base + 16 * pair, 16), 16), lane] = (
                        s * jax.nn.sigmoid(s)
                    ).astype(jnp.bfloat16)
                return carry

            lax.fori_loop(0, RSLOT, conv, 0)

    for i in range(NX):
        lane = slice(i * CHUNK, (i + 1) * CHUNK)
        hidden[:, 0:CHUNK] = jnp.dot(
            act[...], wbuf[i, :, 2 * CHUNK : 3 * CHUNK], preferred_element_type=jnp.float32
        )
        ids = lax.broadcasted_iota(jnp.int32, (MAXLEN, CHUNK), 0)

        def close(r, carry):
            mixed = xbuf[r, :, lane].astype(jnp.float32) + hidden[
                pl.ds(pl.multiple_of(r * MAXLEN, MAXLEN), MAXLEN), 0:CHUNK
            ]
            out[r, :, lane] = jnp.where(ids < length[r], mixed, 0.0).astype(jnp.bfloat16)
            return carry

        lax.fori_loop(0, RSLOT, close, 0)


def conv_module(source, length, me, arr, chosen, full, gain, taps, scale, shift):
    smem = pl.BlockSpec(memory_space=pltpu.SMEM)
    vmem = pl.BlockSpec(memory_space=pltpu.VMEM)
    hbm = pl.BlockSpec(memory_space=pl.ANY)
    return pl.pallas_call(
        module_kernel,
        out_shape=jax.ShapeDtypeStruct((RSLOT, MAXLEN, D), jnp.bfloat16),
        in_specs=[smem, smem, smem, hbm, hbm, hbm, vmem, vmem, vmem, vmem],
        out_specs=vmem,
        scratch_shapes=[
            pltpu.VMEM((RSLOT, MAXLEN, D), jnp.bfloat16),
            pltpu.VMEM((NX, D, BLOCK_COLS), jnp.bfloat16),
            pltpu.VMEM((RSLOT * MAXLEN, D), jnp.bfloat16),
            pltpu.VMEM((RSLOT * MAXLEN, 2 * CHUNK), jnp.float32),
            pltpu.VMEM((RSLOT, MAXLEN + 2 * PAD, 128), jnp.float32),
            pltpu.VMEM((RSLOT * MAXLEN, D), jnp.bfloat16),
            pltpu.SemaphoreType.DMA((RSLOT,)),
            pltpu.SemaphoreType.DMA((NX,)),
        ],
        compiler_params=pltpu.CompilerParams(vmem_limit_bytes=48 * 1024 * 1024),
        name="conv_module",
    )(source, length, me, arr, chosen, full, gain, taps, scale, shift)


def shards(frames, ln_gain, w_in, depth_kernel, bn_scale, bn_shift, w_out, lengths, destinations, offsets):
    dp = lax.axis_index("dp")
    tab_len, tab_dest, tab_off = lengths[0], destinations[0], offsets[0]
    slots = tab_len.shape[1]
    own_len = lax.dynamic_index_in_dim(tab_len, dp, 0, keepdims=False)
    own_dest = lax.dynamic_index_in_dim(tab_dest, dp, 0, keepdims=False)
    peers = jnp.arange(N_DP, dtype=jnp.int32)
    sends = ((own_dest[None, :] == peers[:, None]) & (own_len[None, :] > 0)).astype(jnp.int32)
    send_slot = jnp.sum(sends * jnp.arange(slots, dtype=jnp.int32)[None, :], axis=1)
    chosen = jnp.take(frames[0], send_slot, axis=0)

    key = jnp.where(tab_len > 0, tab_dest * RSLOT + tab_off // MAXLEN, -1)
    targets = dp * RSLOT + jnp.arange(RSLOT, dtype=jnp.int32)
    match = (key[None, :, :] == targets[:, None, None]).astype(jnp.int32)
    source = jnp.sum(match * peers[None, :, None], axis=(1, 2))
    length = jnp.sum(match * tab_len[None, :, :], axis=(1, 2))

    w_rows = jnp.concatenate(
        [w_in.reshape(SHARD_ROWS, 2, NX, CHUNK), w_out.reshape(SHARD_ROWS, 1, NX, CHUNK)], axis=1
    )
    wp = jnp.transpose(w_rows, (2, 0, 1, 3)).reshape(NX, SHARD_ROWS, BLOCK_COLS)
    wp = jnp.pad(wp, ((0, 0), (0, 8 - SHARD_ROWS), (0, 0)))

    arr, full = communicate(chosen, wp)
    out = conv_module(
        source, length, dp.reshape(1).astype(jnp.int32), arr, chosen,
        full.reshape(NX, D, BLOCK_COLS), ln_gain[None], depth_kernel, bn_scale[None], bn_shift[None],
    )
    return out[None]


def solution(mesh):
    return jax.shard_map(
        shards,
        mesh=mesh,
        in_specs=(
            P("fsdp", "dp", None, None),
            P(),
            P(("dp", "fsdp"), None),
            P(),
            P(),
            P(),
            P(("dp", "fsdp"), None),
            P("fsdp", None, None),
            P("fsdp", None, None),
            P("fsdp", None, None),
        ),
        out_specs=P("fsdp", "dp", None, None),
        check_vma=False,
    )
```

```python
import jax
import jax.numpy as jnp
from jax import lax
from jax.experimental import pallas as pl
from jax.experimental.pallas import tpu as pltpu
from jax.sharding import PartitionSpec as P

MESH = pl.DeviceIdType.MESH

D = 1536
KERNEL = 31
MAXLEN = 32
RSLOT = 8
NZ, NY, NX, NC = 8, 4, 4, 2
N_DP = NZ * NY
SHARD_ROWS = 6
BLOCK_ROWS = 24
CHUNK = D // NX
BLOCK_COLS = 3 * CHUNK
PAD = 16

HALF = MAXLEN // 2
PIECES = [(3, None), (1, None), (2, 0), (2, 1)]
ARRIVALS = [0, 7, 1, 6, 2, 5, 3, 4]
UP_FORWARD = (0, 1, 2, 3)


def comm_kernel(
    codes, send_slot, frames, w_in, w_out, out, full,
    wp, parts, block, staged,
    far0, far1, up2_0, up2_1, dn2_0, dn2_1, up3_0, up3_1, dn3_0, dn3_1, up4_0, up4_1, dn4_0, dn4_1, last0, last1,
    mu3_0, mu3_1, md3_0, md3_1, mu4_0, mu4_1, md4_0, md4_1,
    fy_send, fy_recv, fz_send, fz_recv,
    part_send, part_recv, local_sem,
    zu_send, zu_recv, zd_send, zd_recv,
    yu_send, yu_recv, yd_send, yd_recv,
    xu_send, xu_recv, xd_send, xd_recv,
    core_send, core_recv,
):
    dp = lax.axis_index("dp")
    fs = lax.axis_index("fsdp")
    z, y = dp // NY, dp % NY
    x, c = fs // NC, fs % NC
    other = 1 - c
    far, last = (far0, far1), (last0, last1)
    two = ((up2_0, up2_1), (dn2_0, dn2_1))
    three = ((up3_0, up3_1), (dn3_0, dn3_1))
    four = ((up4_0, up4_1), (dn4_0, dn4_1))
    merged3 = ((mu3_0, mu3_1), (md3_0, md3_1))
    merged4 = ((mu4_0, mu4_1), (md4_0, md4_1))

    def dev(zz, yy, xx, cc):
        return (lax.rem(zz, NZ) * NY + lax.rem(yy, NY), lax.rem(xx, NX) * NC + cc)

    sibling = (dp, x * NC + other)
    z_next = (dev(z + 1, y, x, c), dev(z + NZ - 1, y, x, c))
    y_next = (dev(z, y + 1, x, c), dev(z, y + NY - 1, x, c))
    x_next = (dev(z, y, x + 1, c), dev(z, y, x + NX - 1, c))

    barrier = pltpu.get_barrier_semaphore()

    def greet(device):
        pl.semaphore_signal(barrier, inc=1, device_id=device, device_id_type=MESH)

    for k in range(1, NX * NC):
        greet((dp, lax.rem(fs + k, NX * NC)))
    for k in range(1, NY):
        greet(dev(z, y + k, x, c))
    for device in z_next:
        greet(device)

    def remote(src, dst, send, recv, device):
        return pltpu.make_async_remote_copy(
            src_ref=src, dst_ref=dst, send_sem=send, recv_sem=recv, device_id=device, device_id_type=MESH
        )

    started = []

    def start(src, dst, s_sem, r_sem, device):
        copy = remote(src, dst, s_sem, r_sem, device)
        copy.start()
        started.append(copy)

    def landed(ref, r_sem):
        remote(ref, ref, fy_send.at[0, 0, 0], r_sem, sibling).wait_recv()

    homes = {
        4: (far, 0), 3: (two[0], 2), 5: (two[1], 2), 2: (three[0], 6), 6: (three[1], 6),
        1: (four[0], 8), 7: (four[1], 8), 0: (last, 16),
    }

    def pick_frames(dz):
        for dy in range(NY):
            slot = send_slot[dev(z + dz, y + dy, x, c)[0]]
            if dy:
                staged[dz, dy - 1] = frames[slot]
            else:
                refs, first = homes[dz]
                for h in range(2):
                    refs[h][first + y] = frames[slot, h * HALF : (h + 1) * HALF, :]

    def send_frames(dz):
        refs, first = homes[dz]
        for h in range(2):
            for dy in (1, 3, 2):
                start(
                    staged.at[dz, dy - 1, pl.ds(h * HALF, HALF)], refs[h].at[first + y],
                    fy_send.at[dz, dy - 1, h], fy_recv.at[dz, dy - 1, h], dev(z, y + dy, x, c),
                )

    def frames_landed(dz, h):
        refs, first = homes[dz]
        for dy in (1, 3, 2):
            landed(refs[h].at[first + lax.rem(y + NY - dy, NY)], fy_recv.at[dz, dy - 1, h])

    wp[...] = jnp.zeros_like(wp)
    for t in range(NX):
        wp[t, 0:SHARD_ROWS, 0:CHUNK] = w_in[:, t * CHUNK : (t + 1) * CHUNK]
        wp[t, 0:SHARD_ROWS, CHUNK : 2 * CHUNK] = w_in[:, D + t * CHUNK : D + (t + 1) * CHUNK]
        wp[t, 0:SHARD_ROWS, 2 * CHUNK : 3 * CHUNK] = w_out[:, t * CHUNK : (t + 1) * CHUNK]
    pick_frames(4)
    pl.semaphore_wait(barrier, NX * NC + NY)

    slot_here = lax.rem(x, 2) * NC + c
    keeper = x // 2
    for t in range(NX):
        same = jnp.logical_and(x == t, keeper == c)

        @pl.when(jnp.logical_not(same))
        def _():
            remote(wp.at[t], parts.at[slot_here], part_send.at[t], part_recv.at[slot_here], (dp, t * NC + keeper)).start()

        @pl.when(same)
        def _():
            pltpu.make_async_copy(wp.at[t], parts.at[slot_here], local_sem.at[0]).start()

    send_frames(4)
    for dz in (3, 5):
        pick_frames(dz)

    for k in range(4):
        source = c * 4 + k

        @pl.when(source != fs)
        def _():
            landed(parts.at[k], part_recv.at[k])

        @pl.when(source == fs)
        def _():
            pltpu.make_async_copy(wp.at[0], parts.at[k], local_sem.at[0]).wait()

    row = lax.broadcasted_iota(jnp.int32, (BLOCK_ROWS, 32), 0)
    col = lax.broadcasted_iota(jnp.int32, (BLOCK_ROWS, 32), 1)
    pick = (col == (row // SHARD_ROWS) * 8 + lax.rem(row, SHARD_ROWS)).astype(jnp.bfloat16)
    block[...] = jnp.dot(
        pick, parts[...].reshape(32, BLOCK_COLS), preferred_element_type=jnp.float32
    ).astype(jnp.bfloat16)

    own = pltpu.make_async_copy(block, full.at[x, z, y, c], local_sem.at[1])
    own.start()

    def z_block(xx, dz, yy):
        return full.at[lax.rem(xx, NX), lax.rem(z + dz, NZ), lax.rem(yy, NY), c]

    def piece(xx, yy, half=None, cc=None):
        rows = slice(None) if half is None else pl.ds(half * 4, 4)
        return full.at[lax.rem(xx, NX), rows, lax.rem(yy, NY), c if cc is None else cc]

    def spread(i):
        dz = ARRIVALS[i]
        ref = block if i == 0 else z_block(x, dz, y)
        dst = z_block(x, dz, y)
        step = (i + 1) // 2
        if i == 0 or (dz > 4 and step < 4):
            start(ref, dst, zu_send.at[step], zu_recv.at[step], z_next[0])
        if i == 0 or (dz < 4 and step < 3):
            start(ref, dst, zd_send.at[step], zd_recv.at[step], z_next[1])
        start(ref, dst, xu_send.at[i], xu_recv.at[i], x_next[0])
        start(ref, dst, xd_send.at[i], xd_recv.at[i], x_next[1])
        start(ref, dst, yu_send.at[i], yu_recv.at[i], y_next[0])
        start(ref, dst, yd_send.at[i], yd_recv.at[i], y_next[1])

    def z_landed(i):
        dz = ARRIVALS[i]
        step = (i - 1) // 2
        recv = zu_recv if dz >= 4 else zd_recv
        landed(z_block(x, dz, y), recv.at[step])

    def hop(step, h):
        for way in range(2):
            if step == 1:
                src, dst = far[h].at[pl.ds(2 * way, 2)], two[way][h].at[pl.ds(0, 2)]
            elif step == 2:
                src, dst = two[way][h], three[way][h].at[pl.ds(0, 6)]
            elif step == 3:
                src, dst = merged3[way][h], four[way][h].at[pl.ds(0, 8)]
            else:
                src, dst = merged4[way][h], last[h].at[pl.ds(8 * way, 8)]
            start(src, dst, fz_send.at[step - 1, way, h], fz_recv.at[step - 1, way, h], z_next[way])

    def hop_landed(step, h):
        for way in range(2):
            dst = (two[way][h].at[pl.ds(0, 2)], three[way][h].at[pl.ds(0, 6)],
                   four[way][h].at[pl.ds(0, 8)], last[h].at[pl.ds(8 * way, 8)])[step - 1]
            landed(dst, fz_recv.at[step - 1, way, h])

    def merge(step, h):
        for way in range(2):
            index = (1 if step == 3 else 2) if way == 0 else (4 if step == 3 else 5)
            for r in range(RSLOT):
                source = codes[index * RSLOT + r] // 64
                zs, ys = source // NY, lax.rem(source, NY)
                away = lax.rem((z - zs if way == 0 else zs - z) + NZ, NZ)
                if step == 3:
                    early = ys - 2 * way
                    early = jnp.where(jnp.logical_and(early >= 0, early < 2), early, 0)
                    at = jnp.where(away == 0, 6 + ys, jnp.where(away == 1, 2 + ys, early))
                    merged3[way][h][r] = three[way][h][at]
                else:
                    at = jnp.where(away == 0, 8 + ys, r)
                    merged4[way][h][r] = four[way][h][at]

    def to_core(sem, ref):
        start(ref, ref, core_send.at[sem], core_recv.at[sem], sibling)

    spread(0)
    for dz in (3, 5):
        send_frames(dz)
    own.wait()
    for i in range(1, 8):
        z_landed(i)
        spread(i)
        if i == 2:
            frames_landed(4, 0)
            hop(1, 0)
        if i == 4:
            frames_landed(4, 1)
            hop(1, 1)
        if i in (5, 6):
            pick_frames((2, 6)[i - 5])
    to_core(0, piece(x, y))
    for dz in (2, 6):
        send_frames(dz)

    for h in range(2):
        hop_landed(1, h)
        frames_landed(3, h)
        frames_landed(5, h)
        hop(2, h)
    for dz in (1, 7, 0):
        pick_frames(dz)

    def x_start(j, ref):
        start(ref, ref, xu_send.at[8 + j], xu_recv.at[8 + j], x_next[0])
        start(ref, ref, xd_send.at[8 + j], xd_recv.at[8 + j], x_next[1])
        to_core(1 + j, ref)

    for i in range(8):
        landed(z_block(x, ARRIVALS[i], y + 3), yu_recv.at[i])
    ref = piece(x, y + 3, 0)
    start(ref, ref, yu_send.at[8], yu_recv.at[8], y_next[0])
    x_start(0, piece(x, y + 3))
    for i in range(8):
        landed(z_block(x, ARRIVALS[i], y + 1), yd_recv.at[i])
    ref = piece(x, y + 1, 1)
    start(ref, ref, yd_send.at[8], yd_recv.at[8], y_next[1])
    x_start(1, piece(x, y + 1))
    for dz in (1, 7, 0):
        send_frames(dz)

    for i in range(8):
        below, above = z_block(x + 3, ARRIVALS[i], y), z_block(x + 1, ARRIVALS[i], y)
        landed(below, xu_recv.at[i])
        landed(above, xd_recv.at[i])
        if i % 2 == 0:
            start(below, below, xu_send.at[12 + i // 2], xu_recv.at[12 + i // 2], x_next[0])
        else:
            start(above, above, xd_send.at[12 + i // 2], xd_recv.at[12 + i // 2], x_next[1])
    to_core(5, piece(x + 3, y))
    to_core(6, piece(x + 1, y))

    for h in range(2):
        hop_landed(2, h)
        frames_landed(2, h)
        frames_landed(6, h)
        merge(3, h)
        hop(3, h)

    landed(piece(x, y + 2, 0), yu_recv.at[8])
    x_start(2, piece(x, y + 2, 0))
    landed(piece(x, y + 2, 1), yd_recv.at[8])
    x_start(3, piece(x, y + 2, 1))

    def x_landed(j):
        dy, half = PIECES[j]
        below, above = piece(x + 3, y + dy, half), piece(x + 1, y + dy, half)
        landed(below, xu_recv.at[8 + j])
        landed(above, xd_recv.at[8 + j])
        if half in (None, 0):
            ref = piece(x + 3, y + dy, 0)
            start(ref, ref, xu_send.at[16 + j], xu_recv.at[16 + j], x_next[0])
        if half in (None, 1):
            ref = piece(x + 1, y + dy, 1)
            start(ref, ref, xd_send.at[16 + j], xd_recv.at[16 + j], x_next[1])
        to_core(7 + j, below)
        to_core(11 + j, above)

    def x_far_landed(j):
        dy, half = PIECES[j]
        if half in (None, 0):
            landed(piece(x + 2, y + dy, 0), xu_recv.at[16 + j])
        if half in (None, 1):
            landed(piece(x + 2, y + dy, 1), xd_recv.at[16 + j])
        to_core(15 + j, piece(x + 2, y + dy, half))

    x_landed(0)
    for i in range(8):
        recv = xu_recv if i % 2 == 0 else xd_recv
        landed(z_block(x + 2, ARRIVALS[i], y), recv.at[12 + i // 2])
    to_core(19, piece(x + 2, y))

    for h in range(2):
        hop_landed(3, h)
        frames_landed(1, h)
        frames_landed(7, h)
        merge(4, h)
        hop(4, h)
    x_landed(1)
    x_far_landed(0)
    x_landed(2)
    x_far_landed(1)
    x_landed(3)
    x_far_landed(2)
    x_far_landed(3)

    for h in range(2):
        hop_landed(4, h)
        frames_landed(0, h)
        for r in range(RSLOT):
            source = codes[3 * RSLOT + r] // 64
            zs, ys = source // NY, lax.rem(source, NY)
            away = lax.rem(z - zs + NZ, NZ)
            above = jnp.logical_or(away > 4, jnp.logical_and(away == 4, ys >= 2))
            at = jnp.where(away == 0, 16 + ys, jnp.where(above, 8 + r, r))
            out[r, h * HALF : (h + 1) * HALF, :] = last[h][at]

    landed(piece(x, y, None, other), core_recv.at[0])
    for j, (dy, half) in enumerate(PIECES):
        landed(piece(x, y + dy, half, other), core_recv.at[1 + j])
        landed(piece(x + 3, y + dy, half, other), core_recv.at[7 + j])
        landed(piece(x + 1, y + dy, half, other), core_recv.at[11 + j])
        landed(piece(x + 2, y + dy, half, other), core_recv.at[15 + j])
    landed(piece(x + 3, y, None, other), core_recv.at[5])
    landed(piece(x + 1, y, None, other), core_recv.at[6])
    landed(piece(x + 2, y, None, other), core_recv.at[19])

    for t in range(NX):
        same = jnp.logical_and(x == t, keeper == c)

        @pl.when(jnp.logical_not(same))
        def _():
            remote(wp.at[t], parts.at[0], part_send.at[t], part_recv.at[0], sibling).wait_send()

    for copy in started:
        copy.wait_send()


def communicate(codes, send_slot, frames, w_in, w_out):
    dma = pltpu.SemaphoreType.DMA
    smem = pl.BlockSpec(memory_space=pltpu.SMEM)
    vmem = pl.BlockSpec(memory_space=pltpu.VMEM)

    def slots(n):
        return [pltpu.VMEM((n, HALF, D), jnp.bfloat16)]

    return pl.pallas_call(
        comm_kernel,
        out_shape=(
            jax.ShapeDtypeStruct((RSLOT, MAXLEN, D), jnp.bfloat16),
            jax.ShapeDtypeStruct((NX, NZ, NY, NC, BLOCK_ROWS, BLOCK_COLS), jnp.bfloat16),
        ),
        in_specs=[smem, smem, vmem, vmem, vmem],
        out_specs=(vmem, pl.BlockSpec(memory_space=pl.ANY)),
        scratch_shapes=[
            pltpu.VMEM((NX, 8, BLOCK_COLS), jnp.bfloat16),
            pltpu.VMEM((4, 8, BLOCK_COLS), jnp.bfloat16),
            pltpu.VMEM((BLOCK_ROWS, BLOCK_COLS), jnp.bfloat16),
            pltpu.VMEM((NZ, NY - 1, MAXLEN, D), jnp.bfloat16),
            *(slots(4) * 2 + slots(6) * 4 + slots(10) * 4 + slots(12) * 4 + slots(20) * 2 + slots(8) * 8),
            dma((NZ, NY - 1, 2)), dma((NZ, NY - 1, 2)), dma((4, 2, 2)), dma((4, 2, 2)),
            dma((4,)), dma((4,)), dma((2,)),
            dma((4,)), dma((4,)), dma((3,)), dma((3,)),
            dma((9,)), dma((9,)), dma((9,)), dma((9,)),
            dma((20,)), dma((20,)), dma((20,)), dma((20,)),
            dma((20,)), dma((20,)),
        ],
        compiler_params=pltpu.CompilerParams(
            collective_id=0, has_side_effects=True, vmem_limit_bytes=40 * 1024 * 1024
        ),
        name="exchange",
    )(codes, send_slot, frames, w_in, w_out)


def module_kernel(
    codes, xbuf, full, gain, taps, scale, shift, out,
    wbuf, normed, hidden, window, act, w_sem,
):
    loads = [pltpu.make_async_copy(full.at[i], wbuf.at[i], w_sem.at[i]) for i in range(NX)]
    for load in loads:
        load.start()

    window[...] = jnp.zeros_like(window)
    def norm(r, carry):
        wide = xbuf[r].astype(jnp.float32)
        mean = jnp.mean(wide, axis=1, keepdims=True)
        centred = wide - mean
        var = jnp.mean(centred * centred, axis=1, keepdims=True)
        normed[pl.ds(pl.multiple_of(r * MAXLEN, MAXLEN), MAXLEN), :] = (
            centred * lax.rsqrt(var + 1e-05) * gain[...]
        ).astype(jnp.bfloat16)
        return carry

    lax.fori_loop(0, RSLOT, norm, 0)

    step_ids = lax.broadcasted_iota(jnp.int32, (MAXLEN, 128), 0)
    for i in range(NX):
        loads[i].wait()
        hidden[...] = jnp.dot(normed[...], wbuf[i, :, 0 : 2 * CHUNK], preferred_element_type=jnp.float32)
        for b in range(CHUNK // 128):
            lane = slice(i * CHUNK + b * 128, i * CHUNK + b * 128 + 128)
            tap = [jnp.broadcast_to(taps[k : k + 1, lane], (8, 128)) for k in range(KERNEL)]
            mul = jnp.broadcast_to(scale[:, lane], (16, 128))
            add = jnp.broadcast_to(shift[:, lane], (16, 128))

            def conv(r, carry):
                base = pl.multiple_of(r * MAXLEN, MAXLEN)
                value = hidden[pl.ds(base, MAXLEN), b * 128 : b * 128 + 128]
                gate = hidden[pl.ds(base, MAXLEN), CHUNK + b * 128 : CHUNK + b * 128 + 128]
                gated = jnp.where(step_ids < lax.rem(codes[3 * RSLOT + r], 64), value * jax.nn.sigmoid(gate), 0.0)
                window[r, PAD : PAD + MAXLEN, :] = gated
                for pair in range(2):
                    tiles = []
                    for t in (2 * pair, 2 * pair + 1):
                        total = None
                        for k in range(KERNEL):
                            first = 8 * t + k - 15
                            if first + 7 < 0 or first > MAXLEN - 1:
                                continue
                            term = window[r, PAD + first : PAD + first + 8, :] * tap[k]
                            total = term if total is None else total + term
                        tiles.append(total)
                    s = jnp.concatenate(tiles, axis=0) * mul + add
                    act[pl.ds(pl.multiple_of(base + 16 * pair, 16), 16), lane] = (
                        s * jax.nn.sigmoid(s)
                    ).astype(jnp.bfloat16)
                return carry

            lax.fori_loop(0, RSLOT, conv, 0)

    for i in range(NX):
        lane = slice(i * CHUNK, (i + 1) * CHUNK)
        hidden[:, 0:CHUNK] = jnp.dot(
            act[...], wbuf[i, :, 2 * CHUNK : 3 * CHUNK], preferred_element_type=jnp.float32
        )
        ids = lax.broadcasted_iota(jnp.int32, (MAXLEN, CHUNK), 0)

        def close(r, carry):
            mixed = xbuf[r, :, lane].astype(jnp.float32) + hidden[
                pl.ds(pl.multiple_of(r * MAXLEN, MAXLEN), MAXLEN), 0:CHUNK
            ]
            out[r, :, lane] = jnp.where(ids < lax.rem(codes[3 * RSLOT + r], 64), mixed, 0.0).astype(jnp.bfloat16)
            return carry

        lax.fori_loop(0, RSLOT, close, 0)


def conv_module(codes, xbuf, full, gain, taps, scale, shift):
    smem = pl.BlockSpec(memory_space=pltpu.SMEM)
    vmem = pl.BlockSpec(memory_space=pltpu.VMEM)
    hbm = pl.BlockSpec(memory_space=pl.ANY)
    return pl.pallas_call(
        module_kernel,
        out_shape=jax.ShapeDtypeStruct((RSLOT, MAXLEN, D), jnp.bfloat16),
        in_specs=[smem, vmem, hbm, vmem, vmem, vmem, vmem],
        out_specs=vmem,
        scratch_shapes=[
            pltpu.VMEM((NX, D, BLOCK_COLS), jnp.bfloat16),
            pltpu.VMEM((RSLOT * MAXLEN, D), jnp.bfloat16),
            pltpu.VMEM((RSLOT * MAXLEN, 2 * CHUNK), jnp.float32),
            pltpu.VMEM((RSLOT, MAXLEN + 2 * PAD, 128), jnp.float32),
            pltpu.VMEM((RSLOT * MAXLEN, D), jnp.bfloat16),
            pltpu.SemaphoreType.DMA((NX,)),
        ],
        compiler_params=pltpu.CompilerParams(vmem_limit_bytes=48 * 1024 * 1024),
        name="conv_module",
    )(codes, xbuf, full, gain, taps, scale, shift)


def shards(frames, ln_gain, w_in, depth_kernel, bn_scale, bn_shift, w_out, lengths, destinations, offsets):
    dp = lax.axis_index("dp")
    tab_len, tab_dest, tab_off = lengths[0], destinations[0], offsets[0]
    slots = tab_len.shape[1]
    peers = jnp.arange(N_DP, dtype=jnp.int32)
    own_len = lax.dynamic_index_in_dim(tab_len, dp, 0, keepdims=False)
    own_dest = lax.dynamic_index_in_dim(tab_dest, dp, 0, keepdims=False)
    sends = ((own_dest[None, :] == peers[:, None]) & (own_len[None, :] > 0)).astype(jnp.int32)
    send_slot = jnp.sum(sends * jnp.arange(slots, dtype=jnp.int32)[None, :], axis=1)

    rows = jnp.array([0, 2, 1, 0, NZ - 2, NZ - 1], dtype=jnp.int32)
    dests = lax.rem(dp // NY + rows, NZ) * NY + dp % NY
    targets = (dests[:, None] * RSLOT + jnp.arange(RSLOT, dtype=jnp.int32)[None, :]).reshape(-1)
    key = jnp.where(tab_len > 0, tab_dest * RSLOT + tab_off // MAXLEN, -1)
    code = peers[:, None] * 64 + tab_len
    codes = jnp.sum(jnp.where(key[None] == targets[:, None, None], code[None], 0), axis=(1, 2))

    xbuf, full = communicate(codes, send_slot, frames[0], w_in, w_out)
    out = conv_module(
        codes, xbuf, full.reshape(NX, D, BLOCK_COLS),
        ln_gain[None], depth_kernel, bn_scale[None], bn_shift[None],
    )
    return out[None]


def solution(mesh):
    return jax.shard_map(
        shards,
        mesh=mesh,
        in_specs=(
            P("fsdp", "dp", None, None),
            P(),
            P(("dp", "fsdp"), None),
            P(),
            P(),
            P(),
            P(("dp", "fsdp"), None),
            P("fsdp", None, None),
            P("fsdp", None, None),
            P("fsdp", None, None),
        ),
        out_specs=P("fsdp", "dp", None, None),
        check_vma=False,
    )
```

```python
import jax
import jax.numpy as jnp
from jax import lax
from jax.experimental import pallas as pl
from jax.experimental.pallas import tpu as pltpu
from jax.sharding import PartitionSpec as P

MESH = pl.DeviceIdType.MESH

D = 1536
KERNEL = 31
MAXLEN = 32
RSLOT = 8
NZ, NY, NX, NC = 8, 4, 4, 2
N_DP = NZ * NY
SHARD_ROWS = 6
BLOCK_ROWS = 24
CHUNK = D // NX
BLOCK_COLS = 3 * CHUNK
PAD = 16

HALF = MAXLEN // 2
PIECES = [(3, None), (1, None), (2, 0), (2, 1)]
ARRIVALS = [0, 7, 1, 6, 2, 5, 3, 4]
UP_FORWARD = (0, 1, 2, 3)


def comm_kernel(
    codes, frames_hbm, w_in_hbm, w_out_hbm, out, full,
    frames, w_in, w_out, wp, parts, block, staged,
    far0, far1, up2_0, up2_1, dn2_0, dn2_1, up3_0, up3_1, dn3_0, dn3_1, up4_0, up4_1, dn4_0, dn4_1, last0, last1,
    mu3_0, mu3_1, md3_0, md3_1, mu4_0, mu4_1, md4_0, md4_1,
    fy_send, fy_recv, fz_send, fz_recv,
    part_send, part_recv, local_sem,
    zu_send, zu_recv, zd_send, zd_recv,
    yu_send, yu_recv, yd_send, yd_recv,
    xu_send, xu_recv, xd_send, xd_recv,
    core_send, core_recv,
):
    dp = lax.axis_index("dp")
    fs = lax.axis_index("fsdp")
    z, y = dp // NY, dp % NY
    x, c = fs // NC, fs % NC
    other = 1 - c
    far, last = (far0, far1), (last0, last1)
    two = ((up2_0, up2_1), (dn2_0, dn2_1))
    three = ((up3_0, up3_1), (dn3_0, dn3_1))
    four = ((up4_0, up4_1), (dn4_0, dn4_1))
    merged3 = ((mu3_0, mu3_1), (md3_0, md3_1))
    merged4 = ((mu4_0, mu4_1), (md4_0, md4_1))

    def dev(zz, yy, xx, cc):
        return (lax.rem(zz, NZ) * NY + lax.rem(yy, NY), lax.rem(xx, NX) * NC + cc)

    sibling = (dp, x * NC + other)
    z_next = (dev(z + 1, y, x, c), dev(z + NZ - 1, y, x, c))
    y_next = (dev(z, y + 1, x, c), dev(z, y + NY - 1, x, c))
    x_next = (dev(z, y, x + 1, c), dev(z, y, x + NX - 1, c))

    barrier = pltpu.get_barrier_semaphore()

    def greet(device):
        pl.semaphore_signal(barrier, inc=1, device_id=device, device_id_type=MESH)

    for k in range(1, NX * NC):
        greet((dp, lax.rem(fs + k, NX * NC)))
    for k in range(1, NY):
        greet(dev(z, y + k, x, c))
    for device in z_next:
        greet(device)

    loads = [
        pltpu.make_async_copy(w_in_hbm, w_in, local_sem.at[2]),
        pltpu.make_async_copy(w_out_hbm, w_out, local_sem.at[3]),
        pltpu.make_async_copy(frames_hbm, frames, local_sem.at[4]),
    ]
    for load in loads:
        load.start()

    def remote(src, dst, send, recv, device):
        return pltpu.make_async_remote_copy(
            src_ref=src, dst_ref=dst, send_sem=send, recv_sem=recv, device_id=device, device_id_type=MESH
        )

    started = []

    def start(src, dst, s_sem, r_sem, device):
        copy = remote(src, dst, s_sem, r_sem, device)
        copy.start()
        started.append(copy)

    def landed(ref, r_sem):
        remote(ref, ref, fy_send.at[0, 0, 0], r_sem, sibling).wait_recv()

    homes = {
        4: (far, 0), 3: (two[0], 2), 5: (two[1], 2), 2: (three[0], 6), 6: (three[1], 6),
        1: (four[0], 8), 7: (four[1], 8), 0: (last, 16),
    }

    def pick_frames(dz):
        for dy in range(NY):
            slot = codes[6 * RSLOT + dev(z + dz, y + dy, x, c)[0]]
            if dy:
                staged[dz, dy - 1] = frames[slot]
            else:
                refs, first = homes[dz]
                for h in range(2):
                    refs[h][first + y] = frames[slot, h * HALF : (h + 1) * HALF, :]

    def send_frames(dz):
        refs, first = homes[dz]
        for h in range(2):
            for dy in (1, 3, 2):
                start(
                    staged.at[dz, dy - 1, pl.ds(h * HALF, HALF)], refs[h].at[first + y],
                    fy_send.at[dz, dy - 1, h], fy_recv.at[dz, dy - 1, h], dev(z, y + dy, x, c),
                )

    def frames_landed(dz, h):
        refs, first = homes[dz]
        for dy in (1, 3, 2):
            landed(refs[h].at[first + lax.rem(y + NY - dy, NY)], fy_recv.at[dz, dy - 1, h])

    wp[...] = jnp.zeros_like(wp)
    for load in loads[:2]:
        load.wait()
    for t in range(NX):
        wp[t, 0:SHARD_ROWS, 0:CHUNK] = w_in[:, t * CHUNK : (t + 1) * CHUNK]
        wp[t, 0:SHARD_ROWS, CHUNK : 2 * CHUNK] = w_in[:, D + t * CHUNK : D + (t + 1) * CHUNK]
        wp[t, 0:SHARD_ROWS, 2 * CHUNK : 3 * CHUNK] = w_out[:, t * CHUNK : (t + 1) * CHUNK]
    loads[2].wait()
    pick_frames(4)
    pl.semaphore_wait(barrier, NX * NC + NY)

    slot_here = lax.rem(x, 2) * NC + c
    keeper = x // 2
    for t in range(NX):
        same = jnp.logical_and(x == t, keeper == c)

        @pl.when(jnp.logical_not(same))
        def _():
            remote(wp.at[t], parts.at[slot_here], part_send.at[t], part_recv.at[slot_here], (dp, t * NC + keeper)).start()

        @pl.when(same)
        def _():
            pltpu.make_async_copy(wp.at[t], parts.at[slot_here], local_sem.at[0]).start()

    send_frames(4)
    for dz in (3, 5):
        pick_frames(dz)

    for k in range(4):
        source = c * 4 + k

        @pl.when(source != fs)
        def _():
            landed(parts.at[k], part_recv.at[k])

        @pl.when(source == fs)
        def _():
            pltpu.make_async_copy(wp.at[0], parts.at[k], local_sem.at[0]).wait()

    row = lax.broadcasted_iota(jnp.int32, (BLOCK_ROWS, 32), 0)
    col = lax.broadcasted_iota(jnp.int32, (BLOCK_ROWS, 32), 1)
    pick = (col == (row // SHARD_ROWS) * 8 + lax.rem(row, SHARD_ROWS)).astype(jnp.bfloat16)
    block[...] = jnp.dot(
        pick, parts[...].reshape(32, BLOCK_COLS), preferred_element_type=jnp.float32
    ).astype(jnp.bfloat16)

    own = pltpu.make_async_copy(block, full.at[x, z, y, c], local_sem.at[1])
    own.start()

    def z_block(xx, dz, yy):
        return full.at[lax.rem(xx, NX), lax.rem(z + dz, NZ), lax.rem(yy, NY), c]

    def piece(xx, yy, half=None, cc=None):
        rows = slice(None) if half is None else pl.ds(half * 4, 4)
        return full.at[lax.rem(xx, NX), rows, lax.rem(yy, NY), c if cc is None else cc]

    def spread(i):
        dz = ARRIVALS[i]
        ref = block if i == 0 else z_block(x, dz, y)
        dst = z_block(x, dz, y)
        step = (i + 1) // 2
        if i == 0 or (dz > 4 and step < 4):
            start(ref, dst, zu_send.at[step], zu_recv.at[step], z_next[0])
        if i == 0 or (dz < 4 and step < 3):
            start(ref, dst, zd_send.at[step], zd_recv.at[step], z_next[1])
        start(ref, dst, xu_send.at[i], xu_recv.at[i], x_next[0])
        start(ref, dst, xd_send.at[i], xd_recv.at[i], x_next[1])
        start(ref, dst, yu_send.at[i], yu_recv.at[i], y_next[0])
        start(ref, dst, yd_send.at[i], yd_recv.at[i], y_next[1])

    def z_landed(i):
        dz = ARRIVALS[i]
        step = (i - 1) // 2
        recv = zu_recv if dz >= 4 else zd_recv
        landed(z_block(x, dz, y), recv.at[step])

    def hop(step, h):
        for way in range(2):
            if step == 1:
                src, dst = far[h].at[pl.ds(2 * way, 2)], two[way][h].at[pl.ds(0, 2)]
            elif step == 2:
                src, dst = two[way][h], three[way][h].at[pl.ds(0, 6)]
            elif step == 3:
                src, dst = merged3[way][h], four[way][h].at[pl.ds(0, 8)]
            else:
                src, dst = merged4[way][h], last[h].at[pl.ds(8 * way, 8)]
            start(src, dst, fz_send.at[step - 1, way, h], fz_recv.at[step - 1, way, h], z_next[way])

    def hop_landed(step, h):
        for way in range(2):
            dst = (two[way][h].at[pl.ds(0, 2)], three[way][h].at[pl.ds(0, 6)],
                   four[way][h].at[pl.ds(0, 8)], last[h].at[pl.ds(8 * way, 8)])[step - 1]
            landed(dst, fz_recv.at[step - 1, way, h])

    def merge(step, h):
        for way in range(2):
            index = (1 if step == 3 else 2) if way == 0 else (4 if step == 3 else 5)
            for r in range(RSLOT):
                source = codes[index * RSLOT + r] // 64
                zs, ys = source // NY, lax.rem(source, NY)
                away = lax.rem((z - zs if way == 0 else zs - z) + NZ, NZ)
                if step == 3:
                    early = ys - 2 * way
                    early = jnp.where(jnp.logical_and(early >= 0, early < 2), early, 0)
                    at = jnp.where(away == 0, 6 + ys, jnp.where(away == 1, 2 + ys, early))
                    merged3[way][h][r] = three[way][h][at]
                else:
                    at = jnp.where(away == 0, 8 + ys, r)
                    merged4[way][h][r] = four[way][h][at]

    def to_core(sem, ref):
        start(ref, ref, core_send.at[sem], core_recv.at[sem], sibling)

    spread(0)
    for dz in (3, 5):
        send_frames(dz)
    own.wait()
    for i in range(1, 8):
        z_landed(i)
        spread(i)
        if i == 2:
            frames_landed(4, 0)
            hop(1, 0)
        if i == 4:
            frames_landed(4, 1)
            hop(1, 1)
        if i in (5, 6):
            pick_frames((2, 6)[i - 5])
    to_core(0, piece(x, y))
    for dz in (2, 6):
        send_frames(dz)

    for h in range(2):
        hop_landed(1, h)
        frames_landed(3, h)
        frames_landed(5, h)
        hop(2, h)
    for dz in (1, 7, 0):
        pick_frames(dz)

    def x_start(j, ref):
        start(ref, ref, xu_send.at[8 + j], xu_recv.at[8 + j], x_next[0])
        start(ref, ref, xd_send.at[8 + j], xd_recv.at[8 + j], x_next[1])
        to_core(1 + j, ref)

    for i in range(8):
        landed(z_block(x, ARRIVALS[i], y + 3), yu_recv.at[i])
    ref = piece(x, y + 3, 0)
    start(ref, ref, yu_send.at[8], yu_recv.at[8], y_next[0])
    x_start(0, piece(x, y + 3))
    for i in range(8):
        landed(z_block(x, ARRIVALS[i], y + 1), yd_recv.at[i])
    ref = piece(x, y + 1, 1)
    start(ref, ref, yd_send.at[8], yd_recv.at[8], y_next[1])
    x_start(1, piece(x, y + 1))
    for dz in (1, 7, 0):
        send_frames(dz)

    for i in range(8):
        below, above = z_block(x + 3, ARRIVALS[i], y), z_block(x + 1, ARRIVALS[i], y)
        landed(below, xu_recv.at[i])
        landed(above, xd_recv.at[i])
        if i % 2 == 0:
            start(below, below, xu_send.at[12 + i // 2], xu_recv.at[12 + i // 2], x_next[0])
        else:
            start(above, above, xd_send.at[12 + i // 2], xd_recv.at[12 + i // 2], x_next[1])
    to_core(5, piece(x + 3, y))
    to_core(6, piece(x + 1, y))

    for h in range(2):
        hop_landed(2, h)
        frames_landed(2, h)
        frames_landed(6, h)
        merge(3, h)
        hop(3, h)

    landed(piece(x, y + 2, 0), yu_recv.at[8])
    x_start(2, piece(x, y + 2, 0))
    landed(piece(x, y + 2, 1), yd_recv.at[8])
    x_start(3, piece(x, y + 2, 1))

    def x_landed(j):
        dy, half = PIECES[j]
        below, above = piece(x + 3, y + dy, half), piece(x + 1, y + dy, half)
        landed(below, xu_recv.at[8 + j])
        landed(above, xd_recv.at[8 + j])
        if half in (None, 0):
            ref = piece(x + 3, y + dy, 0)
            start(ref, ref, xu_send.at[16 + j], xu_recv.at[16 + j], x_next[0])
        if half in (None, 1):
            ref = piece(x + 1, y + dy, 1)
            start(ref, ref, xd_send.at[16 + j], xd_recv.at[16 + j], x_next[1])
        to_core(7 + j, below)
        to_core(11 + j, above)

    def x_far_landed(j):
        dy, half = PIECES[j]
        if half in (None, 0):
            landed(piece(x + 2, y + dy, 0), xu_recv.at[16 + j])
        if half in (None, 1):
            landed(piece(x + 2, y + dy, 1), xd_recv.at[16 + j])
        to_core(15 + j, piece(x + 2, y + dy, half))

    x_landed(0)
    for i in range(8):
        recv = xu_recv if i % 2 == 0 else xd_recv
        landed(z_block(x + 2, ARRIVALS[i], y), recv.at[12 + i // 2])
    to_core(19, piece(x + 2, y))

    for h in range(2):
        hop_landed(3, h)
        frames_landed(1, h)
        frames_landed(7, h)
        merge(4, h)
        hop(4, h)
    x_landed(1)
    x_far_landed(0)
    x_landed(2)
    x_far_landed(1)
    x_landed(3)
    x_far_landed(2)
    x_far_landed(3)

    for h in range(2):
        hop_landed(4, h)
        frames_landed(0, h)
        for r in range(RSLOT):
            source = codes[3 * RSLOT + r] // 64
            zs, ys = source // NY, lax.rem(source, NY)
            away = lax.rem(z - zs + NZ, NZ)
            above = jnp.logical_or(away > 4, jnp.logical_and(away == 4, ys >= 2))
            at = jnp.where(away == 0, 16 + ys, jnp.where(above, 8 + r, r))
            out[r, h * HALF : (h + 1) * HALF, :] = last[h][at]

    landed(piece(x, y, None, other), core_recv.at[0])
    for j, (dy, half) in enumerate(PIECES):
        landed(piece(x, y + dy, half, other), core_recv.at[1 + j])
        landed(piece(x + 3, y + dy, half, other), core_recv.at[7 + j])
        landed(piece(x + 1, y + dy, half, other), core_recv.at[11 + j])
        landed(piece(x + 2, y + dy, half, other), core_recv.at[15 + j])
    landed(piece(x + 3, y, None, other), core_recv.at[5])
    landed(piece(x + 1, y, None, other), core_recv.at[6])
    landed(piece(x + 2, y, None, other), core_recv.at[19])

    for t in range(NX):
        same = jnp.logical_and(x == t, keeper == c)

        @pl.when(jnp.logical_not(same))
        def _():
            remote(wp.at[t], parts.at[0], part_send.at[t], part_recv.at[0], sibling).wait_send()

    for copy in started:
        copy.wait_send()


def communicate(codes, frames, w_in, w_out):
    dma = pltpu.SemaphoreType.DMA
    smem = pl.BlockSpec(memory_space=pltpu.SMEM)
    vmem = pl.BlockSpec(memory_space=pltpu.VMEM)
    hbm = pl.BlockSpec(memory_space=pltpu.HBM)

    def slots(n):
        return [pltpu.VMEM((n, HALF, D), jnp.bfloat16)]

    return pl.pallas_call(
        comm_kernel,
        out_shape=(
            jax.ShapeDtypeStruct((RSLOT, MAXLEN, D), jnp.bfloat16),
            jax.ShapeDtypeStruct((NX, NZ, NY, NC, BLOCK_ROWS, BLOCK_COLS), jnp.bfloat16),
        ),
        in_specs=[smem, hbm, hbm, hbm],
        out_specs=(vmem, pl.BlockSpec(memory_space=pl.ANY)),
        scratch_shapes=[
            pltpu.VMEM(frames.shape, jnp.bfloat16),
            pltpu.VMEM(w_in.shape, jnp.bfloat16),
            pltpu.VMEM(w_out.shape, jnp.bfloat16),
            pltpu.VMEM((NX, 8, BLOCK_COLS), jnp.bfloat16),
            pltpu.VMEM((4, 8, BLOCK_COLS), jnp.bfloat16),
            pltpu.VMEM((BLOCK_ROWS, BLOCK_COLS), jnp.bfloat16),
            pltpu.VMEM((NZ, NY - 1, MAXLEN, D), jnp.bfloat16),
            *(slots(4) * 2 + slots(6) * 4 + slots(10) * 4 + slots(12) * 4 + slots(20) * 2 + slots(8) * 8),
            dma((NZ, NY - 1, 2)), dma((NZ, NY - 1, 2)), dma((4, 2, 2)), dma((4, 2, 2)),
            dma((4,)), dma((4,)), dma((5,)),
            dma((4,)), dma((4,)), dma((3,)), dma((3,)),
            dma((9,)), dma((9,)), dma((9,)), dma((9,)),
            dma((20,)), dma((20,)), dma((20,)), dma((20,)),
            dma((20,)), dma((20,)),
        ],
        compiler_params=pltpu.CompilerParams(
            collective_id=0, has_side_effects=True, vmem_limit_bytes=67043328
        ),
        name="exchange",
    )(codes, frames, w_in, w_out)


def module_kernel(
    codes, xbuf, full, gain, taps, scale, shift, out,
    wbuf, normed, hidden, window, act, w_sem,
):
    loads = [pltpu.make_async_copy(full.at[i], wbuf.at[i], w_sem.at[i]) for i in range(NX)]
    for load in loads:
        load.start()

    window[...] = jnp.zeros_like(window)
    def norm(i, carry):
        for h in range(2):
            wide = xbuf[i, h * HALF : (h + 1) * HALF, :].astype(jnp.float32)
            mean = jnp.mean(wide, axis=1, keepdims=True)
            centred = wide - mean
            var = jnp.mean(centred * centred, axis=1, keepdims=True)
            normed[pl.ds(pl.multiple_of(i * MAXLEN + h * HALF, HALF), HALF), :] = (
                centred * lax.rsqrt(var + 1e-05) * gain[...].reshape(1, D)
            ).astype(jnp.bfloat16)
        return carry

    lax.fori_loop(0, RSLOT, norm, 0)

    step_ids = lax.broadcasted_iota(jnp.int32, (MAXLEN, 128), 0)
    for i in range(NX):
        loads[i].wait()
        hidden[...] = jnp.dot(normed[...], wbuf[i, :, 0 : 2 * CHUNK], preferred_element_type=jnp.float32)
        for b in range(CHUNK // 128):
            lane = slice(i * CHUNK + b * 128, i * CHUNK + b * 128 + 128)
            tap = [jnp.broadcast_to(taps[k : k + 1, lane], (8, 128)) for k in range(KERNEL)]
            mul = jnp.broadcast_to(scale[lane].reshape(1, 128), (16, 128))
            add = jnp.broadcast_to(shift[lane].reshape(1, 128), (16, 128))

            def conv(r, carry):
                base = pl.multiple_of(r * MAXLEN, MAXLEN)
                value = hidden[pl.ds(base, MAXLEN), b * 128 : b * 128 + 128]
                gate = hidden[pl.ds(base, MAXLEN), CHUNK + b * 128 : CHUNK + b * 128 + 128]
                gated = jnp.where(step_ids < lax.rem(codes[3 * RSLOT + r], 64), value * jax.nn.sigmoid(gate), 0.0)
                window[r, PAD : PAD + MAXLEN, :] = gated
                total = [None] * 4
                for first in range(-7, MAXLEN):
                    rows = window[r, PAD + first : PAD + first + 8, :]
                    for t in range(4):
                        k = first + 15 - 8 * t
                        if 0 <= k < KERNEL:
                            term = rows * tap[k]
                            total[t] = term if total[t] is None else total[t] + term
                for pair in range(2):
                    s = jnp.concatenate(total[2 * pair : 2 * pair + 2], axis=0) * mul + add
                    act[pl.ds(pl.multiple_of(base + 16 * pair, 16), 16), lane] = (
                        s * jax.nn.sigmoid(s)
                    ).astype(jnp.bfloat16)
                return carry

            lax.fori_loop(0, RSLOT, conv, 0, unroll=4)

    for i in range(NX):
        lane = slice(i * CHUNK, (i + 1) * CHUNK)
        hidden[:, 0:CHUNK] = jnp.dot(
            act[...], wbuf[i, :, 2 * CHUNK : 3 * CHUNK], preferred_element_type=jnp.float32
        )
        ids = lax.broadcasted_iota(jnp.int32, (MAXLEN, CHUNK), 0)

        def close(r, carry):
            mixed = xbuf[r, :, lane].astype(jnp.float32) + hidden[
                pl.ds(pl.multiple_of(r * MAXLEN, MAXLEN), MAXLEN), 0:CHUNK
            ]
            out[r, :, lane] = jnp.where(ids < lax.rem(codes[3 * RSLOT + r], 64), mixed, 0.0).astype(jnp.bfloat16)
            return carry

        lax.fori_loop(0, RSLOT, close, 0)


def conv_module(codes, xbuf, full, gain, taps, scale, shift):
    smem = pl.BlockSpec(memory_space=pltpu.SMEM)
    vmem = pl.BlockSpec(memory_space=pltpu.VMEM)
    hbm = pl.BlockSpec(memory_space=pltpu.HBM)
    return pl.pallas_call(
        module_kernel,
        out_shape=jax.ShapeDtypeStruct((RSLOT, MAXLEN, D), jnp.bfloat16),
        in_specs=[smem, vmem, hbm, vmem, vmem, vmem, vmem],
        out_specs=vmem,
        scratch_shapes=[
            pltpu.VMEM((NX, D, BLOCK_COLS), jnp.bfloat16),
            pltpu.VMEM((RSLOT * MAXLEN, D), jnp.bfloat16),
            pltpu.VMEM((RSLOT * MAXLEN, 2 * CHUNK), jnp.float32),
            pltpu.VMEM((RSLOT, MAXLEN + 2 * PAD, 128), jnp.float32),
            pltpu.VMEM((RSLOT * MAXLEN, D), jnp.bfloat16),
            pltpu.SemaphoreType.DMA((NX,)),
        ],
        compiler_params=pltpu.CompilerParams(vmem_limit_bytes=67043328),
        name="conv_module",
    )(codes, xbuf, full, gain, taps, scale, shift)


def shards(frames, ln_gain, w_in, depth_kernel, bn_scale, bn_shift, w_out, lengths, destinations, offsets):
    dp = lax.axis_index("dp")
    tab_len, tab_dest, tab_off = lengths[0], destinations[0], offsets[0]
    slots = tab_len.shape[1]
    peers = jnp.arange(N_DP, dtype=jnp.int32)
    entry = jnp.arange(6 * RSLOT + N_DP, dtype=jnp.int32)
    ahead = jnp.array([0, 2, 1, 0, NZ - 2, NZ - 1] + [0] * 4, dtype=jnp.int32)[:, None] * jnp.ones((1, RSLOT), jnp.int32)
    dests = lax.rem(dp // NY + ahead.reshape(-1), NZ) * NY + dp % NY
    incoming = entry < 6 * RSLOT
    targets = jnp.where(incoming, dests * RSLOT + entry % RSLOT, entry - 6 * RSLOT)[:, None, None]
    incoming = incoming[:, None, None]
    live = tab_len > 0
    key_in = jnp.where(live, tab_dest * RSLOT + tab_off // MAXLEN, -1)
    key_out = jnp.where(live & (peers[:, None] == dp), tab_dest, -1)
    code_in = peers[:, None] * 64 + tab_len
    code_out = jnp.broadcast_to(jnp.arange(slots, dtype=jnp.int32)[None, :], tab_len.shape)
    key = jnp.where(incoming, key_in[None], key_out[None])
    value = jnp.where(incoming, code_in[None], code_out[None])
    codes = jnp.sum(jnp.where(key == targets, value, 0), axis=(1, 2))

    xbuf, full = communicate(codes, frames[0], w_in, w_out)
    out = conv_module(
        codes, xbuf, full.reshape(NX, D, BLOCK_COLS),
        ln_gain, depth_kernel, bn_scale, bn_shift,
    )
    return out[None]


def solution(mesh):
    return jax.shard_map(
        shards,
        mesh=mesh,
        in_specs=(
            P("fsdp", "dp", None, None),
            P(),
            P(("dp", "fsdp"), None),
            P(),
            P(),
            P(),
            P(("dp", "fsdp"), None),
            P("fsdp", None, None),
            P("fsdp", None, None),
            P("fsdp", None, None),
        ),
        out_specs=P("fsdp", "dp", None, None),
        check_vma=False,
    )
```

```python
import jax
import jax.numpy as jnp
from jax import lax
from jax.experimental import pallas as pl
from jax.experimental.pallas import tpu as pltpu
from jax.sharding import PartitionSpec as P

MESH = pl.DeviceIdType.MESH

D = 1536
KERNEL = 31
MAXLEN = 32
RSLOT = 8
NZ, NY, NX, NC = 8, 4, 4, 2
N_DP = NZ * NY
SHARD_ROWS = 6
BLOCK_ROWS = 24
CHUNK = D // NX
BLOCK_COLS = 3 * CHUNK
PAD = 16

HALF = MAXLEN // 2
PIECES = [(3, None), (1, None), (2, 0), (2, 1)]
ARRIVALS = [0, 7, 1, 6, 2, 5, 3, 4]
ORDER = (0, 3, 1, 2)


def comm_kernel(
    codes, frames_hbm, w_in_hbm, w_out_hbm, gain_hbm, taps_hbm, scale_hbm, shift_hbm, out, full,
    xbuf, wbuf, normed, hidden, window, act, gain, taps, scale, shift, w_sem,
    frames, w_in, w_out, wp, parts, block, staged,
    far0, far1, up2_0, up2_1, dn2_0, dn2_1, up3_0, up3_1, dn3_0, dn3_1, up4_0, up4_1, dn4_0, dn4_1, last0, last1,
    mu3_0, mu3_1, md3_0, md3_1, mu4_0, mu4_1, md4_0, md4_1,
    fy_send, fy_recv, fz_send, fz_recv,
    part_send, part_recv, local_sem,
    zu_send, zu_recv, zd_send, zd_recv,
    yu_send, yu_recv, yd_send, yd_recv,
    xu_send, xu_recv, xd_send, xd_recv,
    core_send, core_recv,
):
    dp = lax.axis_index("dp")
    fs = lax.axis_index("fsdp")
    z, y = dp // NY, dp % NY
    x, c = fs // NC, fs % NC
    other = 1 - c
    far, last = (far0, far1), (last0, last1)
    two = ((up2_0, up2_1), (dn2_0, dn2_1))
    three = ((up3_0, up3_1), (dn3_0, dn3_1))
    four = ((up4_0, up4_1), (dn4_0, dn4_1))
    merged3 = ((mu3_0, mu3_1), (md3_0, md3_1))
    merged4 = ((mu4_0, mu4_1), (md4_0, md4_1))

    def kept(cc):
        return pl.ds(pl.multiple_of(cc * BLOCK_ROWS, 8), BLOCK_ROWS)

    def dev(zz, yy, xx, cc):
        return (lax.rem(zz, NZ) * NY + lax.rem(yy, NY), lax.rem(xx, NX) * NC + cc)

    sibling = (dp, x * NC + other)
    z_next = (dev(z + 1, y, x, c), dev(z + NZ - 1, y, x, c))
    y_next = (dev(z, y + 1, x, c), dev(z, y + NY - 1, x, c))
    x_next = (dev(z, y, x + 1, c), dev(z, y, x + NX - 1, c))

    barrier = pltpu.get_barrier_semaphore()

    def greet(device):
        pl.semaphore_signal(barrier, inc=1, device_id=device, device_id_type=MESH)

    for k in range(1, NX * NC):
        greet((dp, lax.rem(fs + k, NX * NC)))
    for k in range(1, NY):
        greet(dev(z, y + k, x, c))
    for device in z_next:
        greet(device)

    loads = [
        pltpu.make_async_copy(w_in_hbm, w_in, local_sem.at[2]),
        pltpu.make_async_copy(w_out_hbm, w_out, local_sem.at[3]),
        pltpu.make_async_copy(frames_hbm, frames, local_sem.at[4]),
        pltpu.make_async_copy(gain_hbm, gain, local_sem.at[5]),
        pltpu.make_async_copy(taps_hbm, taps, local_sem.at[6]),
        pltpu.make_async_copy(scale_hbm, scale, local_sem.at[7]),
        pltpu.make_async_copy(shift_hbm, shift, local_sem.at[8]),
    ]
    for load in loads:
        load.start()

    def remote(src, dst, send, recv, device):
        return pltpu.make_async_remote_copy(
            src_ref=src, dst_ref=dst, send_sem=send, recv_sem=recv, device_id=device, device_id_type=MESH
        )

    started = []

    def start(src, dst, s_sem, r_sem, device):
        copy = remote(src, dst, s_sem, r_sem, device)
        copy.start()
        started.append(copy)

    def landed(ref, r_sem):
        remote(ref, ref, fy_send.at[0, 0, 0], r_sem, sibling).wait_recv()

    homes = {
        4: (far, 0), 3: (two[0], 2), 5: (two[1], 2), 2: (three[0], 6), 6: (three[1], 6),
        1: (four[0], 8), 7: (four[1], 8), 0: (last, 16),
    }

    def pick_frames(dz):
        for dy in range(NY):
            slot = codes[6 * RSLOT + dev(z + dz, y + dy, x, c)[0]]
            if dy:
                staged[dz, dy - 1] = frames[slot]
            else:
                refs, first = homes[dz]
                for h in range(2):
                    refs[h][first + y] = frames[slot, h * HALF : (h + 1) * HALF, :]

    def send_frames(dz):
        refs, first = homes[dz]
        for h in range(2):
            for dy in (1, 3, 2):
                start(
                    staged.at[dz, dy - 1, pl.ds(h * HALF, HALF)], refs[h].at[first + y],
                    fy_send.at[dz, dy - 1, h], fy_recv.at[dz, dy - 1, h], dev(z, y + dy, x, c),
                )

    def frames_landed(dz, h):
        refs, first = homes[dz]
        for dy in (1, 3, 2):
            landed(refs[h].at[first + lax.rem(y + NY - dy, NY)], fy_recv.at[dz, dy - 1, h])

    wp[...] = jnp.zeros_like(wp)
    window[...] = jnp.zeros_like(window)
    for load in loads[:2]:
        load.wait()
    for t in range(NX):
        wp[t, 0:SHARD_ROWS, 0:CHUNK] = w_in[:, t * CHUNK : (t + 1) * CHUNK]
        wp[t, 0:SHARD_ROWS, CHUNK : 2 * CHUNK] = w_in[:, D + t * CHUNK : D + (t + 1) * CHUNK]
        wp[t, 0:SHARD_ROWS, 2 * CHUNK : 3 * CHUNK] = w_out[:, t * CHUNK : (t + 1) * CHUNK]
    loads[2].wait()
    pick_frames(4)
    pl.semaphore_wait(barrier, NX * NC + NY)

    slot_here = lax.rem(x, 2) * NC + c
    keeper = x // 2
    for t in range(NX):
        same = jnp.logical_and(x == t, keeper == c)

        @pl.when(jnp.logical_not(same))
        def _():
            remote(wp.at[t], parts.at[slot_here], part_send.at[t], part_recv.at[slot_here], (dp, t * NC + keeper)).start()

        @pl.when(same)
        def _():
            pltpu.make_async_copy(wp.at[t], parts.at[slot_here], local_sem.at[0]).start()

    send_frames(4)
    for dz in (3, 5):
        pick_frames(dz)

    for k in range(4):
        source = c * 4 + k

        @pl.when(source != fs)
        def _():
            landed(parts.at[k], part_recv.at[k])

        @pl.when(source == fs)
        def _():
            pltpu.make_async_copy(wp.at[0], parts.at[k], local_sem.at[0]).wait()

    row = lax.broadcasted_iota(jnp.int32, (BLOCK_ROWS, 32), 0)
    col = lax.broadcasted_iota(jnp.int32, (BLOCK_ROWS, 32), 1)
    pick = (col == (row // SHARD_ROWS) * 8 + lax.rem(row, SHARD_ROWS)).astype(jnp.bfloat16)
    block[...] = jnp.dot(
        pick, parts[...].reshape(32, BLOCK_COLS), preferred_element_type=jnp.float32
    ).astype(jnp.bfloat16)

    own = pltpu.make_async_copy(block, full.at[x, z, y, kept(c)], local_sem.at[1])
    own.start()

    def z_block(xx, dz, yy):
        return full.at[lax.rem(xx, NX), lax.rem(z + dz, NZ), lax.rem(yy, NY), kept(c)]

    def piece(xx, yy, half=None, cc=None):
        rows = slice(None) if half is None else pl.ds(half * 4, 4)
        return full.at[lax.rem(xx, NX), rows, lax.rem(yy, NY), kept(c if cc is None else cc)]

    def spread(i):
        dz = ARRIVALS[i]
        ref = block if i == 0 else z_block(x, dz, y)
        dst = z_block(x, dz, y)
        step = (i + 1) // 2
        if i == 0 or (dz > 4 and step < 4):
            start(ref, dst, zu_send.at[step], zu_recv.at[step], z_next[0])
        if i == 0 or (dz < 4 and step < 3):
            start(ref, dst, zd_send.at[step], zd_recv.at[step], z_next[1])
        start(ref, dst, xu_send.at[i], xu_recv.at[i], x_next[0])
        start(ref, dst, xd_send.at[i], xd_recv.at[i], x_next[1])
        start(ref, dst, yu_send.at[i], yu_recv.at[i], y_next[0])
        start(ref, dst, yd_send.at[i], yd_recv.at[i], y_next[1])

    def z_landed(i):
        dz = ARRIVALS[i]
        step = (i - 1) // 2
        recv = zu_recv if dz >= 4 else zd_recv
        landed(z_block(x, dz, y), recv.at[step])

    def hop(step, h):
        for way in range(2):
            if step == 1:
                src, dst = far[h].at[pl.ds(2 * way, 2)], two[way][h].at[pl.ds(0, 2)]
            elif step == 2:
                src, dst = two[way][h], three[way][h].at[pl.ds(0, 6)]
            elif step == 3:
                src, dst = merged3[way][h], four[way][h].at[pl.ds(0, 8)]
            else:
                src, dst = merged4[way][h], last[h].at[pl.ds(8 * way, 8)]
            start(src, dst, fz_send.at[step - 1, way, h], fz_recv.at[step - 1, way, h], z_next[way])

    def hop_landed(step, h):
        for way in range(2):
            dst = (two[way][h].at[pl.ds(0, 2)], three[way][h].at[pl.ds(0, 6)],
                   four[way][h].at[pl.ds(0, 8)], last[h].at[pl.ds(8 * way, 8)])[step - 1]
            landed(dst, fz_recv.at[step - 1, way, h])

    def merge(step, h):
        for way in range(2):
            index = (1 if step == 3 else 2) if way == 0 else (4 if step == 3 else 5)
            for r in range(RSLOT):
                source = codes[index * RSLOT + r] // 64
                zs, ys = source // NY, lax.rem(source, NY)
                away = lax.rem((z - zs if way == 0 else zs - z) + NZ, NZ)
                if step == 3:
                    early = ys - 2 * way
                    early = jnp.where(jnp.logical_and(early >= 0, early < 2), early, 0)
                    at = jnp.where(away == 0, 6 + ys, jnp.where(away == 1, 2 + ys, early))
                    merged3[way][h][r] = three[way][h][at]
                else:
                    at = jnp.where(away == 0, 8 + ys, r)
                    merged4[way][h][r] = four[way][h][at]

    def to_core(sem, ref):
        start(ref, ref, core_send.at[sem], core_recv.at[sem], sibling)

    step_ids = lax.broadcasted_iota(jnp.int32, (MAXLEN, 128), 0)

    def norm(i, carry):
        for h in range(2):
            wide = xbuf[i, h * HALF : (h + 1) * HALF, :].astype(jnp.float32)
            mean = jnp.mean(wide, axis=1, keepdims=True)
            centred = wide - mean
            var = jnp.mean(centred * centred, axis=1, keepdims=True)
            normed[pl.ds(pl.multiple_of(i * MAXLEN + h * HALF, HALF), HALF), :] = (
                centred * lax.rsqrt(var + 1e-05) * gain[...].reshape(1, D)
            ).astype(jnp.bfloat16)
        return carry

    def load_chunk(i):
        return pltpu.make_async_copy(
            full.at[lax.rem(x + ORDER[i], NX)], wbuf.at[i], w_sem.at[i]
        )

    def chunk(i):
        column = lax.rem(x + ORDER[i], NX) * CHUNK
        load_chunk(i).wait()
        hidden[...] = jnp.dot(normed[...], wbuf[i, :, :, :, 0 : 2 * CHUNK].reshape(D, 2 * CHUNK), preferred_element_type=jnp.float32)
        for b in range(CHUNK // 128):
            lane = pl.ds(pl.multiple_of(column + b * 128, 128), 128)
            tap = [jnp.broadcast_to(taps[k : k + 1, lane], (8, 128)) for k in range(KERNEL)]
            mul = jnp.broadcast_to(scale[lane].reshape(1, 128), (16, 128))
            add = jnp.broadcast_to(shift[lane].reshape(1, 128), (16, 128))

            def conv(r, carry):
                base = pl.multiple_of(r * MAXLEN, MAXLEN)
                value = hidden[pl.ds(base, MAXLEN), b * 128 : b * 128 + 128]
                gate = hidden[pl.ds(base, MAXLEN), CHUNK + b * 128 : CHUNK + b * 128 + 128]
                gated = jnp.where(step_ids < lax.rem(codes[3 * RSLOT + r], 64), value * jax.nn.sigmoid(gate), 0.0)
                window[r, PAD : PAD + MAXLEN, :] = gated
                total = [None] * 4
                for first in range(-7, MAXLEN):
                    rows = window[r, PAD + first : PAD + first + 8, :]
                    for t in range(4):
                        k = first + 15 - 8 * t
                        if 0 <= k < KERNEL:
                            term = rows * tap[k]
                            total[t] = term if total[t] is None else total[t] + term
                for pair in range(2):
                    s = jnp.concatenate(total[2 * pair : 2 * pair + 2], axis=0) * mul + add
                    act[pl.ds(pl.multiple_of(base + 16 * pair, 16), 16), lane] = (
                        s * jax.nn.sigmoid(s)
                    ).astype(jnp.bfloat16)
                return carry

            lax.fori_loop(0, RSLOT, conv, 0, unroll=4)

    spread(0)
    for dz in (3, 5):
        send_frames(dz)
    own.wait()
    for i in range(1, 8):
        z_landed(i)
        spread(i)
        if i == 2:
            frames_landed(4, 0)
            hop(1, 0)
        if i == 4:
            frames_landed(4, 1)
            hop(1, 1)
        if i in (5, 6):
            pick_frames((2, 6)[i - 5])
    to_core(0, piece(x, y))
    for dz in (2, 6):
        send_frames(dz)

    for h in range(2):
        hop_landed(1, h)
        frames_landed(3, h)
        frames_landed(5, h)
        hop(2, h)
    for dz in (1, 7, 0):
        pick_frames(dz)

    def x_start(j, ref):
        start(ref, ref, xu_send.at[8 + j], xu_recv.at[8 + j], x_next[0])
        start(ref, ref, xd_send.at[8 + j], xd_recv.at[8 + j], x_next[1])
        to_core(1 + j, ref)

    for i in range(8):
        landed(z_block(x, ARRIVALS[i], y + 3), yu_recv.at[i])
    ref = piece(x, y + 3, 0)
    start(ref, ref, yu_send.at[8], yu_recv.at[8], y_next[0])
    x_start(0, piece(x, y + 3))
    for i in range(8):
        landed(z_block(x, ARRIVALS[i], y + 1), yd_recv.at[i])
    ref = piece(x, y + 1, 1)
    start(ref, ref, yd_send.at[8], yd_recv.at[8], y_next[1])
    x_start(1, piece(x, y + 1))
    for dz in (1, 7, 0):
        send_frames(dz)

    for i in range(8):
        below, above = z_block(x + 3, ARRIVALS[i], y), z_block(x + 1, ARRIVALS[i], y)
        landed(below, xu_recv.at[i])
        landed(above, xd_recv.at[i])
        if i % 2 == 0:
            start(below, below, xu_send.at[12 + i // 2], xu_recv.at[12 + i // 2], x_next[0])
        else:
            start(above, above, xd_send.at[12 + i // 2], xd_recv.at[12 + i // 2], x_next[1])
    to_core(5, piece(x + 3, y))
    to_core(6, piece(x + 1, y))

    for h in range(2):
        hop_landed(2, h)
        frames_landed(2, h)
        frames_landed(6, h)
        merge(3, h)
        hop(3, h)

    landed(piece(x, y + 2, 0), yu_recv.at[8])
    x_start(2, piece(x, y + 2, 0))
    landed(piece(x, y + 2, 1), yd_recv.at[8])
    x_start(3, piece(x, y + 2, 1))

    def x_landed(j):
        dy, half = PIECES[j]
        below, above = piece(x + 3, y + dy, half), piece(x + 1, y + dy, half)
        landed(below, xu_recv.at[8 + j])
        landed(above, xd_recv.at[8 + j])
        if half in (None, 0):
            ref = piece(x + 3, y + dy, 0)
            start(ref, ref, xu_send.at[16 + j], xu_recv.at[16 + j], x_next[0])
        if half in (None, 1):
            ref = piece(x + 1, y + dy, 1)
            start(ref, ref, xd_send.at[16 + j], xd_recv.at[16 + j], x_next[1])
        to_core(7 + j, below)
        to_core(11 + j, above)

    def x_far_landed(j):
        dy, half = PIECES[j]
        if half in (None, 0):
            landed(piece(x + 2, y + dy, 0), xu_recv.at[16 + j])
        if half in (None, 1):
            landed(piece(x + 2, y + dy, 1), xd_recv.at[16 + j])
        to_core(15 + j, piece(x + 2, y + dy, half))

    x_landed(0)
    for i in range(8):
        recv = xu_recv if i % 2 == 0 else xd_recv
        landed(z_block(x + 2, ARRIVALS[i], y), recv.at[12 + i // 2])
    to_core(19, piece(x + 2, y))

    for h in range(2):
        hop_landed(3, h)
        frames_landed(1, h)
        frames_landed(7, h)
        merge(4, h)
        hop(4, h)
    landed(piece(x, y, None, other), core_recv.at[0])
    for j, (dy, half) in enumerate(PIECES):
        landed(piece(x, y + dy, half, other), core_recv.at[1 + j])
    load_chunk(0).start()
    x_landed(1)
    x_far_landed(0)
    x_landed(2)
    x_far_landed(1)
    x_landed(3)

    for load in loads[3:]:
        load.wait()
    for h in range(2):
        hop_landed(4, h)
        frames_landed(0, h)
        for r in range(RSLOT):
            source = codes[3 * RSLOT + r] // 64
            zs, ys = source // NY, lax.rem(source, NY)
            away = lax.rem(z - zs + NZ, NZ)
            above = jnp.logical_or(away > 4, jnp.logical_and(away == 4, ys >= 2))
            at = jnp.where(away == 0, 16 + ys, jnp.where(above, 8 + r, r))
            xbuf[r, h * HALF : (h + 1) * HALF, :] = last[h][at]
    x_far_landed(2)
    lax.fori_loop(0, RSLOT, norm, 0)

    for i, (first, whole) in ((1, (7, 5)), (2, (11, 6))):
        landed(piece(x + ORDER[i], y, None, other), core_recv.at[whole])
        for j, (dy, half) in enumerate(PIECES):
            landed(piece(x + ORDER[i], y + dy, half, other), core_recv.at[first + j])
        load_chunk(i).start()
    chunk(0)
    x_far_landed(3)
    chunk(1)
    landed(piece(x + 2, y, None, other), core_recv.at[19])
    for j, (dy, half) in enumerate(PIECES):
        landed(piece(x + 2, y + dy, half, other), core_recv.at[15 + j])
    load_chunk(3).start()
    chunk(2)
    chunk(3)
    for i in range(NX):
        lane = pl.ds(pl.multiple_of(lax.rem(x + ORDER[i], NX) * CHUNK, 128), CHUNK)
        hidden[:, 0:CHUNK] = jnp.dot(
            act[...], wbuf[i, :, :, :, 2 * CHUNK : 3 * CHUNK].reshape(D, CHUNK), preferred_element_type=jnp.float32
        )

        ids = lax.broadcasted_iota(jnp.int32, (MAXLEN, CHUNK), 0)

        def close(r, carry):
            mixed = xbuf[r, :, lane].astype(jnp.float32) + hidden[
                pl.ds(pl.multiple_of(r * MAXLEN, MAXLEN), MAXLEN), 0:CHUNK
            ]
            out[r, :, lane] = jnp.where(ids < lax.rem(codes[3 * RSLOT + r], 64), mixed, 0.0).astype(jnp.bfloat16)
            return carry

        lax.fori_loop(0, RSLOT, close, 0)

    for t in range(NX):
        same = jnp.logical_and(x == t, keeper == c)

        @pl.when(jnp.logical_not(same))
        def _():
            remote(wp.at[t], parts.at[0], part_send.at[t], part_recv.at[0], sibling).wait_send()

    for copy in started:
        copy.wait_send()


def communicate(codes, frames, w_in, w_out, gain, taps, scale, shift):
    dma = pltpu.SemaphoreType.DMA
    smem = pl.BlockSpec(memory_space=pltpu.SMEM)
    vmem = pl.BlockSpec(memory_space=pltpu.VMEM)
    hbm = pl.BlockSpec(memory_space=pltpu.HBM)

    def slots(n):
        return [pltpu.VMEM((n, HALF, D), jnp.bfloat16)]

    return pl.pallas_call(
        comm_kernel,
        out_shape=(
            jax.ShapeDtypeStruct((RSLOT, MAXLEN, D), jnp.bfloat16),
            jax.ShapeDtypeStruct((NX, NZ, NY, NC * BLOCK_ROWS, BLOCK_COLS), jnp.bfloat16),
        ),
        in_specs=[smem] + [hbm] * 7,
        out_specs=(vmem, pl.BlockSpec(memory_space=pl.ANY)),
        scratch_shapes=[
            pltpu.VMEM((RSLOT, MAXLEN, D), jnp.bfloat16),
            pltpu.VMEM((NX, NZ, NY, NC * BLOCK_ROWS, BLOCK_COLS), jnp.bfloat16),
            pltpu.VMEM((RSLOT * MAXLEN, D), jnp.bfloat16),
            pltpu.VMEM((RSLOT * MAXLEN, 2 * CHUNK), jnp.float32),
            pltpu.VMEM((RSLOT, MAXLEN + 2 * PAD, 128), jnp.float32),
            pltpu.VMEM((RSLOT * MAXLEN, D), jnp.bfloat16),
            pltpu.VMEM((D,), jnp.float32),
            pltpu.VMEM((KERNEL, D), jnp.float32),
            pltpu.VMEM((D,), jnp.float32),
            pltpu.VMEM((D,), jnp.float32),
            dma((NX,)),
            pltpu.VMEM(frames.shape, jnp.bfloat16),
            pltpu.VMEM(w_in.shape, jnp.bfloat16),
            pltpu.VMEM(w_out.shape, jnp.bfloat16),
            pltpu.VMEM((NX, 8, BLOCK_COLS), jnp.bfloat16),
            pltpu.VMEM((4, 8, BLOCK_COLS), jnp.bfloat16),
            pltpu.VMEM((BLOCK_ROWS, BLOCK_COLS), jnp.bfloat16),
            pltpu.VMEM((NZ, NY - 1, MAXLEN, D), jnp.bfloat16),
            *(slots(4) * 2 + slots(6) * 4 + slots(10) * 4 + slots(12) * 4 + slots(20) * 2 + slots(8) * 8),
            dma((NZ, NY - 1, 2)), dma((NZ, NY - 1, 2)), dma((4, 2, 2)), dma((4, 2, 2)),
            dma((4,)), dma((4,)), dma((9,)),
            dma((4,)), dma((4,)), dma((3,)), dma((3,)),
            dma((9,)), dma((9,)), dma((9,)), dma((9,)),
            dma((20,)), dma((20,)), dma((20,)), dma((20,)),
            dma((20,)), dma((20,)),
        ],
        compiler_params=pltpu.CompilerParams(
            collective_id=0, has_side_effects=True, vmem_limit_bytes=67043328
        ),
        name="exchange",
    )(codes, frames, w_in, w_out, gain, taps, scale, shift)


def shards(frames, ln_gain, w_in, depth_kernel, bn_scale, bn_shift, w_out, lengths, destinations, offsets):
    dp = lax.axis_index("dp")
    tab_len, tab_dest, tab_off = lengths[0], destinations[0], offsets[0]
    slots = tab_len.shape[1]
    peers = jnp.arange(N_DP, dtype=jnp.int32)
    entry = jnp.arange(6 * RSLOT + N_DP, dtype=jnp.int32)
    ahead = jnp.array([0, 2, 1, 0, NZ - 2, NZ - 1] + [0] * 4, dtype=jnp.int32)[:, None] * jnp.ones((1, RSLOT), jnp.int32)
    dests = lax.rem(dp // NY + ahead.reshape(-1), NZ) * NY + dp % NY
    incoming = entry < 6 * RSLOT
    targets = jnp.where(incoming, dests * RSLOT + entry % RSLOT, entry - 6 * RSLOT)[:, None, None]
    incoming = incoming[:, None, None]
    live = tab_len > 0
    key_in = jnp.where(live, tab_dest * RSLOT + tab_off // MAXLEN, -1)
    key_out = jnp.where(live & (peers[:, None] == dp), tab_dest, -1)
    code_in = peers[:, None] * 64 + tab_len
    code_out = jnp.broadcast_to(jnp.arange(slots, dtype=jnp.int32)[None, :], tab_len.shape)
    key = jnp.where(incoming, key_in[None], key_out[None])
    value = jnp.where(incoming, code_in[None], code_out[None])
    codes = jnp.sum(jnp.where(key == targets, value, 0), axis=(1, 2))

    out, _ = communicate(codes, frames[0], w_in, w_out, ln_gain, depth_kernel, bn_scale, bn_shift)
    return out[None]


def solution(mesh):
    return jax.shard_map(
        shards,
        mesh=mesh,
        in_specs=(
            P("fsdp", "dp", None, None),
            P(),
            P(("dp", "fsdp"), None),
            P(),
            P(),
            P(),
            P(("dp", "fsdp"), None),
            P("fsdp", None, None),
            P("fsdp", None, None),
            P("fsdp", None, None),
        ),
        out_specs=P("fsdp", "dp", None, None),
        check_vma=False,
    )
```

```python
import jax
import jax.numpy as jnp
from jax import lax
from jax.experimental import pallas as pl
from jax.experimental.pallas import tpu as pltpu
from jax.sharding import PartitionSpec as P

MESH = pl.DeviceIdType.MESH

D = 1536
KERNEL = 31
MAXLEN = 32
RSLOT = 8
NZ, NY, NX, NC = 8, 4, 4, 2
N_DP = NZ * NY
SHARD_ROWS = 6
BLOCK_ROWS = 24
CHUNK = D // NX
BLOCK_COLS = 3 * CHUNK
PAD = 16

HALF = MAXLEN // 2
PIECES = [(3, None), (1, None), (2, 0), (2, 1)]
ARRIVALS = [0, 7, 1, 6, 2, 5, 3, 4]
ORDER = (0, 3, 1, 2)


def comm_kernel(
    codes, frames_hbm, w_in_hbm, w_out_hbm, gain_hbm, taps_hbm, scale_hbm, shift_hbm, out, full,
    xbuf, wbuf, normed, hidden, window, act, gain, taps, scale, shift, w_sem,
    frames, w_in, w_out, wp, parts, block, staged,
    far0, far1, up2_0, up2_1, dn2_0, dn2_1, up3_0, up3_1, dn3_0, dn3_1, up4_0, up4_1, dn4_0, dn4_1, last0, last1,
    mu3_0, mu3_1, md3_0, md3_1, mu4_0, mu4_1, md4_0, md4_1,
    fy_send, fy_recv, fz_send, fz_recv,
    part_send, part_recv, local_sem,
    zu_send, zu_recv, zd_send, zd_recv,
    yu_send, yu_recv, yd_send, yd_recv,
    xu_send, xu_recv, xd_send, xd_recv,
    core_send, core_recv, lu_send, lu_recv, ld_send, ld_recv,
):
    dp = lax.axis_index("dp")
    fs = lax.axis_index("fsdp")
    z, y = dp // NY, dp % NY
    x, c = fs // NC, fs % NC
    other = 1 - c
    far, last = (far0, far1), (last0, last1)
    two = ((up2_0, up2_1), (dn2_0, dn2_1))
    three = ((up3_0, up3_1), (dn3_0, dn3_1))
    four = ((up4_0, up4_1), (dn4_0, dn4_1))
    merged3 = ((mu3_0, mu3_1), (md3_0, md3_1))
    merged4 = ((mu4_0, mu4_1), (md4_0, md4_1))

    def kept(cc):
        return pl.ds(pl.multiple_of(cc * BLOCK_ROWS, 8), BLOCK_ROWS)

    def dev(zz, yy, xx, cc):
        return (lax.rem(zz, NZ) * NY + lax.rem(yy, NY), lax.rem(xx, NX) * NC + cc)

    sibling = (dp, x * NC + other)
    z_next = (dev(z + 1, y, x, c), dev(z + NZ - 1, y, x, c))
    y_next = (dev(z, y + 1, x, c), dev(z, y + NY - 1, x, c))
    x_next = (dev(z, y, x + 1, c), dev(z, y, x + NX - 1, c))

    barrier = pltpu.get_barrier_semaphore()

    def greet(device):
        pl.semaphore_signal(barrier, inc=1, device_id=device, device_id_type=MESH)

    for k in range(1, NX * NC):
        greet((dp, lax.rem(fs + k, NX * NC)))
    for k in range(1, NY):
        greet(dev(z, y + k, x, c))
    for device in z_next:
        greet(device)

    loads = [
        pltpu.make_async_copy(w_in_hbm, w_in, local_sem.at[2]),
        pltpu.make_async_copy(w_out_hbm, w_out, local_sem.at[3]),
        pltpu.make_async_copy(frames_hbm, frames, local_sem.at[4]),
        pltpu.make_async_copy(gain_hbm, gain, local_sem.at[5]),
        pltpu.make_async_copy(taps_hbm, taps, local_sem.at[6]),
        pltpu.make_async_copy(scale_hbm, scale, local_sem.at[7]),
        pltpu.make_async_copy(shift_hbm, shift, local_sem.at[8]),
    ]
    for load in loads:
        load.start()

    def remote(src, dst, send, recv, device):
        return pltpu.make_async_remote_copy(
            src_ref=src, dst_ref=dst, send_sem=send, recv_sem=recv, device_id=device, device_id_type=MESH
        )

    started = []

    def start(src, dst, s_sem, r_sem, device):
        copy = remote(src, dst, s_sem, r_sem, device)
        copy.start()
        started.append(copy)

    def landed(ref, r_sem):
        remote(ref, ref, fy_send.at[0, 0, 0], r_sem, sibling).wait_recv()

    homes = {
        4: (far, 0), 3: (two[0], 2), 5: (two[1], 2), 2: (three[0], 6), 6: (three[1], 6),
        1: (four[0], 8), 7: (four[1], 8), 0: (last, 16),
    }

    def pick_frames(dz):
        for dy in range(NY):
            slot = codes[6 * RSLOT + dev(z + dz, y + dy, x, c)[0]]
            if dy:
                staged[dz, dy - 1] = frames[slot]
            else:
                refs, first = homes[dz]
                for h in range(2):
                    refs[h][first + y] = frames[slot, h * HALF : (h + 1) * HALF, :]

    def send_frames(dz):
        refs, first = homes[dz]
        for h in range(2):
            for dy in (1, 3, 2):
                start(
                    staged.at[dz, dy - 1, pl.ds(h * HALF, HALF)], refs[h].at[first + y],
                    fy_send.at[dz, dy - 1, h], fy_recv.at[dz, dy - 1, h], dev(z, y + dy, x, c),
                )

    def frames_landed(dz, h):
        refs, first = homes[dz]
        for dy in (1, 3, 2):
            landed(refs[h].at[first + lax.rem(y + NY - dy, NY)], fy_recv.at[dz, dy - 1, h])

    wp[...] = jnp.zeros_like(wp)
    window[...] = jnp.zeros_like(window)
    for load in loads[:2]:
        load.wait()
    for t in range(NX):
        wp[t, 0:SHARD_ROWS, 0:CHUNK] = w_in[:, t * CHUNK : (t + 1) * CHUNK]
        wp[t, 0:SHARD_ROWS, CHUNK : 2 * CHUNK] = w_in[:, D + t * CHUNK : D + (t + 1) * CHUNK]
        wp[t, 0:SHARD_ROWS, 2 * CHUNK : 3 * CHUNK] = w_out[:, t * CHUNK : (t + 1) * CHUNK]
    loads[2].wait()
    pick_frames(4)
    pl.semaphore_wait(barrier, NX * NC + NY)

    slot_here = lax.rem(x, 2) * NC + c
    keeper = x // 2
    for t in range(NX):
        same = jnp.logical_and(x == t, keeper == c)

        @pl.when(jnp.logical_not(same))
        def _():
            remote(wp.at[t], parts.at[slot_here], part_send.at[t], part_recv.at[slot_here], (dp, t * NC + keeper)).start()

        @pl.when(same)
        def _():
            pltpu.make_async_copy(wp.at[t], parts.at[slot_here], local_sem.at[0]).start()

    send_frames(4)
    for dz in (3, 5):
        pick_frames(dz)

    for k in range(4):
        source = c * 4 + k

        @pl.when(source != fs)
        def _():
            landed(parts.at[k], part_recv.at[k])

        @pl.when(source == fs)
        def _():
            pltpu.make_async_copy(wp.at[0], parts.at[k], local_sem.at[0]).wait()

    row = lax.broadcasted_iota(jnp.int32, (BLOCK_ROWS, 32), 0)
    col = lax.broadcasted_iota(jnp.int32, (BLOCK_ROWS, 32), 1)
    pick = (col == (row // SHARD_ROWS) * 8 + lax.rem(row, SHARD_ROWS)).astype(jnp.bfloat16)
    block[...] = jnp.dot(
        pick, parts[...].reshape(32, BLOCK_COLS), preferred_element_type=jnp.float32
    ).astype(jnp.bfloat16)

    own = pltpu.make_async_copy(block, full.at[x, z, y, kept(c)], local_sem.at[1])
    own.start()

    def z_block(xx, dz, yy):
        return full.at[lax.rem(xx, NX), lax.rem(z + dz, NZ), lax.rem(yy, NY), kept(c)]

    def piece(xx, yy, half=None, cc=None):
        rows = slice(None) if half is None else pl.ds(half * 4, 4)
        return full.at[lax.rem(xx, NX), rows, lax.rem(yy, NY), kept(c if cc is None else cc)]

    def most(xx, yy, half=None, cc=None):
        rows = pl.ds(0, NZ - 1) if half is None else pl.ds(half * 4, 4 - half)
        return full.at[lax.rem(xx, NX), rows, lax.rem(yy, NY), kept(c if cc is None else cc)]

    def late(xx, yy, cc=None):
        return full.at[lax.rem(xx, NX), NZ - 1, lax.rem(yy, NY), kept(c if cc is None else cc)]

    def late_start(k):
        ref = late(x + ORDER[k + 1], y)
        start(ref, ref, lu_send.at[k], lu_recv.at[k], y_next[0])
        start(ref, ref, ld_send.at[k], ld_recv.at[k], y_next[1])

    def late_landed(k):
        below, above = late(x + ORDER[k + 1], y + 3), late(x + ORDER[k + 1], y + 1)
        landed(below, lu_recv.at[k])
        landed(above, ld_recv.at[k])
        if k == 1:
            start(above, above, ld_send.at[3], ld_recv.at[3], y_next[1])
        else:
            start(below, below, lu_send.at[3 + k // 2], lu_recv.at[3 + k // 2], y_next[0])
        to_core(20 + 3 * k, below)
        to_core(21 + 3 * k, above)

    def late_far_landed(k):
        ref = late(x + ORDER[k + 1], y + 2)
        landed(ref, ld_recv.at[3] if k == 1 else lu_recv.at[3 + k // 2])
        to_core(22 + 3 * k, ref)

    def spread(i):
        dz = ARRIVALS[i]
        ref = block if i == 0 else z_block(x, dz, y)
        dst = z_block(x, dz, y)
        step = (i + 1) // 2
        if i == 0 or (dz > 4 and step < 4):
            start(ref, dst, zu_send.at[step], zu_recv.at[step], z_next[0])
        if i == 0 or (dz < 4 and step < 3):
            start(ref, dst, zd_send.at[step], zd_recv.at[step], z_next[1])
        start(ref, dst, xu_send.at[i], xu_recv.at[i], x_next[0])
        start(ref, dst, xd_send.at[i], xd_recv.at[i], x_next[1])
        start(ref, dst, yu_send.at[i], yu_recv.at[i], y_next[0])
        start(ref, dst, yd_send.at[i], yd_recv.at[i], y_next[1])

    def z_landed(i):
        dz = ARRIVALS[i]
        step = (i - 1) // 2
        recv = zu_recv if dz >= 4 else zd_recv
        landed(z_block(x, dz, y), recv.at[step])

    def hop(step, h):
        for way in range(2):
            if step == 1:
                src, dst = far[h].at[pl.ds(2 * way, 2)], two[way][h].at[pl.ds(0, 2)]
            elif step == 2:
                src, dst = two[way][h], three[way][h].at[pl.ds(0, 6)]
            elif step == 3:
                src, dst = merged3[way][h], four[way][h].at[pl.ds(0, 8)]
            else:
                src, dst = merged4[way][h], last[h].at[pl.ds(8 * way, 8)]
            start(src, dst, fz_send.at[step - 1, way, h], fz_recv.at[step - 1, way, h], z_next[way])

    def hop_landed(step, h):
        for way in range(2):
            dst = (two[way][h].at[pl.ds(0, 2)], three[way][h].at[pl.ds(0, 6)],
                   four[way][h].at[pl.ds(0, 8)], last[h].at[pl.ds(8 * way, 8)])[step - 1]
            landed(dst, fz_recv.at[step - 1, way, h])

    def merge(step, h):
        for way in range(2):
            index = (1 if step == 3 else 2) if way == 0 else (4 if step == 3 else 5)
            for r in range(RSLOT):
                source = codes[index * RSLOT + r] // 64
                zs, ys = source // NY, lax.rem(source, NY)
                away = lax.rem((z - zs if way == 0 else zs - z) + NZ, NZ)
                if step == 3:
                    early = ys - 2 * way
                    early = jnp.where(jnp.logical_and(early >= 0, early < 2), early, 0)
                    at = jnp.where(away == 0, 6 + ys, jnp.where(away == 1, 2 + ys, early))
                    merged3[way][h][r] = three[way][h][at]
                else:
                    at = jnp.where(away == 0, 8 + ys, r)
                    merged4[way][h][r] = four[way][h][at]

    def to_core(sem, ref):
        start(ref, ref, core_send.at[sem], core_recv.at[sem], sibling)

    step_ids = lax.broadcasted_iota(jnp.int32, (MAXLEN, 128), 0)

    def norm(i, carry):
        for h in range(2):
            wide = xbuf[i, h * HALF : (h + 1) * HALF, :].astype(jnp.float32)
            mean = jnp.mean(wide, axis=1, keepdims=True)
            centred = wide - mean
            var = jnp.mean(centred * centred, axis=1, keepdims=True)
            normed[pl.ds(pl.multiple_of(i * MAXLEN + h * HALF, HALF), HALF), :] = (
                centred * lax.rsqrt(var + 1e-05) * gain[...].reshape(1, D)
            ).astype(jnp.bfloat16)
        return carry

    def load_chunk(i):
        return pltpu.make_async_copy(
            full.at[lax.rem(x + ORDER[i], NX)], wbuf.at[i], w_sem.at[i]
        )

    def chunk(i):
        column = lax.rem(x + ORDER[i], NX) * CHUNK
        load_chunk(i).wait()
        hidden[...] = jnp.dot(normed[...], wbuf[i, :, :, :, 0 : 2 * CHUNK].reshape(D, 2 * CHUNK), preferred_element_type=jnp.float32)
        for b in range(CHUNK // 128):
            lane = pl.ds(pl.multiple_of(column + b * 128, 128), 128)
            tap = [jnp.broadcast_to(taps[k : k + 1, lane], (8, 128)) for k in range(KERNEL)]
            mul = jnp.broadcast_to(scale[lane].reshape(1, 128), (16, 128))
            add = jnp.broadcast_to(shift[lane].reshape(1, 128), (16, 128))

            def conv(r, carry):
                base = pl.multiple_of(r * MAXLEN, MAXLEN)
                value = hidden[pl.ds(base, MAXLEN), b * 128 : b * 128 + 128]
                gate = hidden[pl.ds(base, MAXLEN), CHUNK + b * 128 : CHUNK + b * 128 + 128]
                gated = jnp.where(step_ids < lax.rem(codes[3 * RSLOT + r], 64), value * jax.nn.sigmoid(gate), 0.0)
                window[r, PAD : PAD + MAXLEN, :] = gated
                total = [None] * 4
                for first in range(-7, MAXLEN):
                    rows = window[r, PAD + first : PAD + first + 8, :]
                    for t in range(4):
                        k = first + 15 - 8 * t
                        if 0 <= k < KERNEL:
                            term = rows * tap[k]
                            total[t] = term if total[t] is None else total[t] + term
                for pair in range(2):
                    s = jnp.concatenate(total[2 * pair : 2 * pair + 2], axis=0) * mul + add
                    act[pl.ds(pl.multiple_of(base + 16 * pair, 16), 16), lane] = (
                        s * jax.nn.sigmoid(s)
                    ).astype(jnp.bfloat16)
                return carry

            lax.fori_loop(0, RSLOT, conv, 0, unroll=4)

    spread(0)
    for dz in (3, 5):
        send_frames(dz)
    own.wait()
    for i in range(1, 8):
        z_landed(i)
        spread(i)
        if i == 2:
            frames_landed(4, 0)
            hop(1, 0)
        if i == 4:
            frames_landed(4, 1)
            hop(1, 1)
        if i in (5, 6):
            pick_frames((2, 6)[i - 5])
    to_core(0, piece(x, y))
    for dz in (2, 6):
        send_frames(dz)

    for h in range(2):
        hop_landed(1, h)
        frames_landed(3, h)
        frames_landed(5, h)
        hop(2, h)
    for dz in (1, 7, 0):
        pick_frames(dz)

    def x_start(j):
        dy, half = PIECES[j]
        ref = most(x, y + dy, half)
        start(ref, ref, xu_send.at[8 + j], xu_recv.at[8 + j], x_next[0])
        start(ref, ref, xd_send.at[8 + j], xd_recv.at[8 + j], x_next[1])
        to_core(1 + j, piece(x, y + dy, half))

    for i in range(8):
        landed(z_block(x, ARRIVALS[i], y + 3), yu_recv.at[i])
    ref = piece(x, y + 3, 0)
    start(ref, ref, yu_send.at[8], yu_recv.at[8], y_next[0])
    x_start(0)
    for i in range(8):
        landed(z_block(x, ARRIVALS[i], y + 1), yd_recv.at[i])
    ref = piece(x, y + 1, 1)
    start(ref, ref, yd_send.at[8], yd_recv.at[8], y_next[1])
    x_start(1)
    for dz in (1, 7):
        send_frames(dz)

    for i in range(8):
        below, above = z_block(x + 3, ARRIVALS[i], y), z_block(x + 1, ARRIVALS[i], y)
        landed(below, xu_recv.at[i])
        landed(above, xd_recv.at[i])
        if i % 2 == 0:
            start(below, below, xu_send.at[12 + i // 2], xu_recv.at[12 + i // 2], x_next[0])
        else:
            start(above, above, xd_send.at[12 + i // 2], xd_recv.at[12 + i // 2], x_next[1])
    to_core(5, piece(x + 3, y))
    to_core(6, piece(x + 1, y))
    late_start(0)
    late_start(1)
    send_frames(0)

    for h in range(2):
        hop_landed(2, h)
        frames_landed(2, h)
        frames_landed(6, h)
        merge(3, h)
        hop(3, h)

    landed(piece(x, y + 2, 0), yu_recv.at[8])
    x_start(2)
    landed(piece(x, y + 2, 1), yd_recv.at[8])
    x_start(3)

    def x_landed(j):
        dy, half = PIECES[j]
        below, above = most(x + 3, y + dy, half), most(x + 1, y + dy, half)
        landed(below, xu_recv.at[8 + j])
        landed(above, xd_recv.at[8 + j])
        if half in (None, 0):
            ref = most(x + 3, y + dy, 0)
            start(ref, ref, xu_send.at[16 + j], xu_recv.at[16 + j], x_next[0])
        if half in (None, 1):
            ref = most(x + 1, y + dy, 1)
            start(ref, ref, xd_send.at[16 + j], xd_recv.at[16 + j], x_next[1])
        to_core(7 + j, below)
        to_core(11 + j, above)

    def x_far_landed(j):
        dy, half = PIECES[j]
        if half in (None, 0):
            landed(most(x + 2, y + dy, 0), xu_recv.at[16 + j])
        if half in (None, 1):
            landed(most(x + 2, y + dy, 1), xd_recv.at[16 + j])
        to_core(15 + j, most(x + 2, y + dy, half))

    x_landed(0)
    for i in range(8):
        recv = xu_recv if i % 2 == 0 else xd_recv
        landed(z_block(x + 2, ARRIVALS[i], y), recv.at[12 + i // 2])
    to_core(19, piece(x + 2, y))
    late_start(2)

    for h in range(2):
        hop_landed(3, h)
        frames_landed(1, h)
        frames_landed(7, h)
        merge(4, h)
        hop(4, h)
    landed(piece(x, y, None, other), core_recv.at[0])
    for j, (dy, half) in enumerate(PIECES):
        landed(piece(x, y + dy, half, other), core_recv.at[1 + j])
    load_chunk(0).start()
    for k in range(3):
        late_landed(k)
    x_landed(1)
    x_far_landed(0)
    x_landed(2)
    x_far_landed(1)
    for k in range(3):
        late_far_landed(k)
    x_landed(3)

    for load in loads[3:]:
        load.wait()
    for h in range(2):
        hop_landed(4, h)
        frames_landed(0, h)
        for r in range(RSLOT):
            source = codes[3 * RSLOT + r] // 64
            zs, ys = source // NY, lax.rem(source, NY)
            away = lax.rem(z - zs + NZ, NZ)
            above = jnp.logical_or(away > 4, jnp.logical_and(away == 4, ys >= 2))
            at = jnp.where(away == 0, 16 + ys, jnp.where(above, 8 + r, r))
            xbuf[r, h * HALF : (h + 1) * HALF, :] = last[h][at]
    x_far_landed(2)
    lax.fori_loop(0, RSLOT, norm, 0)

    for i, (first, whole) in ((1, (7, 5)), (2, (11, 6))):
        landed(piece(x + ORDER[i], y, None, other), core_recv.at[whole])
        for j, (dy, half) in enumerate(PIECES):
            landed(most(x + ORDER[i], y + dy, half, other), core_recv.at[first + j])
        for j, dy in enumerate((3, 1, 2)):
            landed(late(x + ORDER[i], y + dy, other), core_recv.at[17 + 3 * i + j])
        load_chunk(i).start()
    chunk(0)
    x_far_landed(3)
    chunk(1)
    landed(piece(x + 2, y, None, other), core_recv.at[19])
    for j, (dy, half) in enumerate(PIECES):
        landed(most(x + 2, y + dy, half, other), core_recv.at[15 + j])
    for j, dy in enumerate((3, 1, 2)):
        landed(late(x + 2, y + dy, other), core_recv.at[26 + j])
    load_chunk(3).start()
    chunk(2)
    chunk(3)
    for i in range(NX):
        lane = pl.ds(pl.multiple_of(lax.rem(x + ORDER[i], NX) * CHUNK, 128), CHUNK)
        hidden[:, 0:CHUNK] = jnp.dot(
            act[...], wbuf[i, :, :, :, 2 * CHUNK : 3 * CHUNK].reshape(D, CHUNK), preferred_element_type=jnp.float32
        )

        ids = lax.broadcasted_iota(jnp.int32, (MAXLEN, CHUNK), 0)

        def close(r, carry):
            mixed = xbuf[r, :, lane].astype(jnp.float32) + hidden[
                pl.ds(pl.multiple_of(r * MAXLEN, MAXLEN), MAXLEN), 0:CHUNK
            ]
            out[r, :, lane] = jnp.where(ids < lax.rem(codes[3 * RSLOT + r], 64), mixed, 0.0).astype(jnp.bfloat16)
            return carry

        lax.fori_loop(0, RSLOT, close, 0)

    for t in range(NX):
        same = jnp.logical_and(x == t, keeper == c)

        @pl.when(jnp.logical_not(same))
        def _():
            remote(wp.at[t], parts.at[0], part_send.at[t], part_recv.at[0], sibling).wait_send()

    for copy in started:
        copy.wait_send()


def communicate(codes, frames, w_in, w_out, gain, taps, scale, shift):
    dma = pltpu.SemaphoreType.DMA
    smem = pl.BlockSpec(memory_space=pltpu.SMEM)
    vmem = pl.BlockSpec(memory_space=pltpu.VMEM)
    hbm = pl.BlockSpec(memory_space=pltpu.HBM)

    def slots(n):
        return [pltpu.VMEM((n, HALF, D), jnp.bfloat16)]

    return pl.pallas_call(
        comm_kernel,
        out_shape=(
            jax.ShapeDtypeStruct((RSLOT, MAXLEN, D), jnp.bfloat16),
            jax.ShapeDtypeStruct((NX, NZ, NY, NC * BLOCK_ROWS, BLOCK_COLS), jnp.bfloat16),
        ),
        in_specs=[smem] + [hbm] * 7,
        out_specs=(vmem, pl.BlockSpec(memory_space=pl.ANY)),
        scratch_shapes=[
            pltpu.VMEM((RSLOT, MAXLEN, D), jnp.bfloat16),
            pltpu.VMEM((NX, NZ, NY, NC * BLOCK_ROWS, BLOCK_COLS), jnp.bfloat16),
            pltpu.VMEM((RSLOT * MAXLEN, D), jnp.bfloat16),
            pltpu.VMEM((RSLOT * MAXLEN, 2 * CHUNK), jnp.float32),
            pltpu.VMEM((RSLOT, MAXLEN + 2 * PAD, 128), jnp.float32),
            pltpu.VMEM((RSLOT * MAXLEN, D), jnp.bfloat16),
            pltpu.VMEM((D,), jnp.float32),
            pltpu.VMEM((KERNEL, D), jnp.float32),
            pltpu.VMEM((D,), jnp.float32),
            pltpu.VMEM((D,), jnp.float32),
            dma((NX,)),
            pltpu.VMEM(frames.shape, jnp.bfloat16),
            pltpu.VMEM(w_in.shape, jnp.bfloat16),
            pltpu.VMEM(w_out.shape, jnp.bfloat16),
            pltpu.VMEM((NX, 8, BLOCK_COLS), jnp.bfloat16),
            pltpu.VMEM((4, 8, BLOCK_COLS), jnp.bfloat16),
            pltpu.VMEM((BLOCK_ROWS, BLOCK_COLS), jnp.bfloat16),
            pltpu.VMEM((NZ, NY - 1, MAXLEN, D), jnp.bfloat16),
            *(slots(4) * 2 + slots(6) * 4 + slots(10) * 4 + slots(12) * 4 + slots(20) * 2 + slots(8) * 8),
            dma((NZ, NY - 1, 2)), dma((NZ, NY - 1, 2)), dma((4, 2, 2)), dma((4, 2, 2)),
            dma((4,)), dma((4,)), dma((9,)),
            dma((4,)), dma((4,)), dma((3,)), dma((3,)),
            dma((9,)), dma((9,)), dma((9,)), dma((9,)),
            dma((20,)), dma((20,)), dma((20,)), dma((20,)),
            dma((29,)), dma((29,)), dma((5,)), dma((5,)), dma((4,)), dma((4,)),
        ],
        compiler_params=pltpu.CompilerParams(
            collective_id=0, has_side_effects=True, vmem_limit_bytes=67043328
        ),
        name="exchange",
    )(codes, frames, w_in, w_out, gain, taps, scale, shift)


def shards(frames, ln_gain, w_in, depth_kernel, bn_scale, bn_shift, w_out, lengths, destinations, offsets):
    dp = lax.axis_index("dp")
    tab_len, tab_dest, tab_off = lengths[0], destinations[0], offsets[0]
    slots = tab_len.shape[1]
    peers = jnp.arange(N_DP, dtype=jnp.int32)
    entry = jnp.arange(6 * RSLOT + N_DP, dtype=jnp.int32)
    ahead = jnp.array([0, 2, 1, 0, NZ - 2, NZ - 1] + [0] * 4, dtype=jnp.int32)[:, None] * jnp.ones((1, RSLOT), jnp.int32)
    dests = lax.rem(dp // NY + ahead.reshape(-1), NZ) * NY + dp % NY
    incoming = entry < 6 * RSLOT
    targets = jnp.where(incoming, dests * RSLOT + entry % RSLOT, entry - 6 * RSLOT)[:, None, None]
    incoming = incoming[:, None, None]
    live = tab_len > 0
    key_in = jnp.where(live, tab_dest * RSLOT + tab_off // MAXLEN, -1)
    key_out = jnp.where(live & (peers[:, None] == dp), tab_dest, -1)
    code_in = peers[:, None] * 64 + tab_len
    code_out = jnp.broadcast_to(jnp.arange(slots, dtype=jnp.int32)[None, :], tab_len.shape)
    key = jnp.where(incoming, key_in[None], key_out[None])
    value = jnp.where(incoming, code_in[None], code_out[None])
    codes = jnp.sum(jnp.where(key == targets, value, 0), axis=(1, 2))

    out, _ = communicate(codes, frames[0], w_in, w_out, ln_gain, depth_kernel, bn_scale, bn_shift)
    return out[None]


def solution(mesh):
    return jax.shard_map(
        shards,
        mesh=mesh,
        in_specs=(
            P("fsdp", "dp", None, None),
            P(),
            P(("dp", "fsdp"), None),
            P(),
            P(),
            P(),
            P(("dp", "fsdp"), None),
            P("fsdp", None, None),
            P("fsdp", None, None),
            P("fsdp", None, None),
        ),
        out_specs=P("fsdp", "dp", None, None),
        check_vma=False,
    )
```

```python
import jax
import jax.numpy as jnp
from jax import lax
from jax.experimental import pallas as pl
from jax.experimental.pallas import tpu as pltpu
from jax.sharding import PartitionSpec as P

MESH = pl.DeviceIdType.MESH

D = 1536
KERNEL = 31
MAXLEN = 32
RSLOT = 8
NZ, NY, NX, NC = 8, 4, 4, 2
N_DP = NZ * NY
SHARD_ROWS = 6
BLOCK_ROWS = 24
CHUNK = D // NX
BLOCK_COLS = 3 * CHUNK
PAD = 16

HALF = MAXLEN // 2
PIECES = [(3, None), (1, None), (2, 0), (2, 1)]
ARRIVALS = [0, 7, 1, 6, 2, 5, 3, 4]
ORDER = (0, 3, 1, 2)


def comm_kernel(
    codes, frames_hbm, w_in_hbm, w_out_hbm, gain_hbm, taps_hbm, scale_hbm, shift_hbm, out, full,
    xbuf, wbuf, normed, hidden, window, act, gain, taps, scale, shift, w_sem,
    frames, w_in, w_out, wp, parts, block, staged,
    far0, far1, up2_0, up2_1, dn2_0, dn2_1, up3_0, up3_1, dn3_0, dn3_1, up4_0, up4_1, dn4_0, dn4_1, last0, last1,
    mu3_0, mu3_1, md3_0, md3_1, mu4_0, mu4_1, md4_0, md4_1,
    fy_send, fy_recv, fz_send, fz_recv,
    part_send, part_recv, local_sem,
    zu_send, zu_recv, zd_send, zd_recv,
    yu_send, yu_recv, yd_send, yd_recv,
    xu_send, xu_recv, xd_send, xd_recv,
    core_send, core_recv, lu_send, lu_recv, ld_send, ld_recv,
):
    dp = lax.axis_index("dp")
    fs = lax.axis_index("fsdp")
    z, y = dp // NY, dp % NY
    x, c = fs // NC, fs % NC
    other = 1 - c
    far, last = (far0, far1), (last0, last1)
    two = ((up2_0, up2_1), (dn2_0, dn2_1))
    three = ((up3_0, up3_1), (dn3_0, dn3_1))
    four = ((up4_0, up4_1), (dn4_0, dn4_1))
    merged3 = ((mu3_0, mu3_1), (md3_0, md3_1))
    merged4 = ((mu4_0, mu4_1), (md4_0, md4_1))

    def kept(cc):
        return pl.ds(pl.multiple_of(cc * BLOCK_ROWS, 8), BLOCK_ROWS)

    def dev(zz, yy, xx, cc):
        return (lax.rem(zz, NZ) * NY + lax.rem(yy, NY), lax.rem(xx, NX) * NC + cc)

    sibling = (dp, x * NC + other)
    z_next = (dev(z + 1, y, x, c), dev(z + NZ - 1, y, x, c))
    y_next = (dev(z, y + 1, x, c), dev(z, y + NY - 1, x, c))
    x_next = (dev(z, y, x + 1, c), dev(z, y, x + NX - 1, c))

    barrier = pltpu.get_barrier_semaphore()

    def greet(device):
        pl.semaphore_signal(barrier, inc=1, device_id=device, device_id_type=MESH)

    for k in range(1, NX * NC):
        greet((dp, lax.rem(fs + k, NX * NC)))
    for k in range(1, NY):
        greet(dev(z, y + k, x, c))
    for device in z_next:
        greet(device)

    loads = [
        pltpu.make_async_copy(w_in_hbm, w_in, local_sem.at[2]),
        pltpu.make_async_copy(w_out_hbm, w_out, local_sem.at[3]),
        pltpu.make_async_copy(frames_hbm, frames, local_sem.at[4]),
        pltpu.make_async_copy(gain_hbm, gain, local_sem.at[5]),
        pltpu.make_async_copy(taps_hbm, taps, local_sem.at[6]),
        pltpu.make_async_copy(scale_hbm, scale, local_sem.at[7]),
        pltpu.make_async_copy(shift_hbm, shift, local_sem.at[8]),
    ]
    for load in loads:
        load.start()

    def remote(src, dst, send, recv, device):
        return pltpu.make_async_remote_copy(
            src_ref=src, dst_ref=dst, send_sem=send, recv_sem=recv, device_id=device, device_id_type=MESH
        )

    started = []

    def start(src, dst, s_sem, r_sem, device):
        copy = remote(src, dst, s_sem, r_sem, device)
        copy.start()
        started.append(copy)

    def landed(ref, r_sem):
        remote(ref, ref, fy_send.at[0, 0, 0], r_sem, sibling).wait_recv()

    homes = {
        4: (far, 0), 3: (two[0], 2), 5: (two[1], 2), 2: (three[0], 6), 6: (three[1], 6),
        1: (four[0], 8), 7: (four[1], 8), 0: (last, 16),
    }

    def pick_frames(dz):
        for dy in range(NY):
            slot = codes[0, 6 * RSLOT + dev(z + dz, y + dy, x, c)[0]]
            if dy:
                staged[dz, dy - 1] = frames[slot]
            else:
                refs, first = homes[dz]
                for h in range(2):
                    refs[h][first + y] = frames[slot, h * HALF : (h + 1) * HALF, :]

    def send_frames(dz):
        refs, first = homes[dz]
        for h in range(2):
            for dy in (1, 3, 2):
                start(
                    staged.at[dz, dy - 1, pl.ds(h * HALF, HALF)], refs[h].at[first + y],
                    fy_send.at[dz, dy - 1, h], fy_recv.at[dz, dy - 1, h], dev(z, y + dy, x, c),
                )

    def frames_landed(dz, h):
        refs, first = homes[dz]
        for dy in (1, 3, 2):
            landed(refs[h].at[first + lax.rem(y + NY - dy, NY)], fy_recv.at[dz, dy - 1, h])

    wp[...] = jnp.zeros_like(wp)
    window[...] = jnp.zeros_like(window)
    for load in loads[:2]:
        load.wait()
    for t in range(NX):
        wp[t, 0:SHARD_ROWS, 0:CHUNK] = w_in[:, t * CHUNK : (t + 1) * CHUNK]
        wp[t, 0:SHARD_ROWS, CHUNK : 2 * CHUNK] = w_in[:, D + t * CHUNK : D + (t + 1) * CHUNK]
        wp[t, 0:SHARD_ROWS, 2 * CHUNK : 3 * CHUNK] = w_out[:, t * CHUNK : (t + 1) * CHUNK]
    loads[2].wait()
    pick_frames(4)
    pl.semaphore_wait(barrier, NX * NC + NY)

    slot_here = lax.rem(x, 2) * NC + c
    keeper = x // 2
    for t in range(NX):
        same = jnp.logical_and(x == t, keeper == c)

        @pl.when(jnp.logical_not(same))
        def _():
            remote(wp.at[t], parts.at[slot_here], part_send.at[t], part_recv.at[slot_here], (dp, t * NC + keeper)).start()

        @pl.when(same)
        def _():
            pltpu.make_async_copy(wp.at[t], parts.at[slot_here], local_sem.at[0]).start()

    send_frames(4)
    for dz in (3, 5):
        pick_frames(dz)

    for k in range(4):
        source = c * 4 + k

        @pl.when(source != fs)
        def _():
            landed(parts.at[k], part_recv.at[k])

        @pl.when(source == fs)
        def _():
            pltpu.make_async_copy(wp.at[0], parts.at[k], local_sem.at[0]).wait()

    row = lax.broadcasted_iota(jnp.int32, (BLOCK_ROWS, 32), 0)
    col = lax.broadcasted_iota(jnp.int32, (BLOCK_ROWS, 32), 1)
    pick = (col == (row // SHARD_ROWS) * 8 + lax.rem(row, SHARD_ROWS)).astype(jnp.bfloat16)
    block[...] = jnp.dot(
        pick, parts[...].reshape(32, BLOCK_COLS), preferred_element_type=jnp.float32
    ).astype(jnp.bfloat16)

    own = pltpu.make_async_copy(block, full.at[x, z, y, kept(c)], local_sem.at[1])
    own.start()

    def z_block(xx, dz, yy):
        return full.at[lax.rem(xx, NX), lax.rem(z + dz, NZ), lax.rem(yy, NY), kept(c)]

    def piece(xx, yy, half=None, cc=None):
        rows = slice(None) if half is None else pl.ds(half * 4, 4)
        return full.at[lax.rem(xx, NX), rows, lax.rem(yy, NY), kept(c if cc is None else cc)]

    def most(xx, yy, half=None, cc=None):
        rows = pl.ds(0, NZ - 1) if half is None else pl.ds(half * 4, 4 - half)
        return full.at[lax.rem(xx, NX), rows, lax.rem(yy, NY), kept(c if cc is None else cc)]

    def late(xx, yy, cc=None):
        return full.at[lax.rem(xx, NX), NZ - 1, lax.rem(yy, NY), kept(c if cc is None else cc)]

    def late_start(k):
        ref = late(x + ORDER[k + 1], y)
        start(ref, ref, lu_send.at[k], lu_recv.at[k], y_next[0])
        start(ref, ref, ld_send.at[k], ld_recv.at[k], y_next[1])

    def late_landed(k):
        below, above = late(x + ORDER[k + 1], y + 3), late(x + ORDER[k + 1], y + 1)
        landed(below, lu_recv.at[k])
        landed(above, ld_recv.at[k])
        if k == 1:
            start(above, above, ld_send.at[3], ld_recv.at[3], y_next[1])
        else:
            start(below, below, lu_send.at[3 + k // 2], lu_recv.at[3 + k // 2], y_next[0])
        to_core(20 + 3 * k, below)
        to_core(21 + 3 * k, above)

    def late_far_landed(k):
        ref = late(x + ORDER[k + 1], y + 2)
        landed(ref, ld_recv.at[3] if k == 1 else lu_recv.at[3 + k // 2])
        to_core(22 + 3 * k, ref)

    def spread(i):
        dz = ARRIVALS[i]
        ref = block if i == 0 else z_block(x, dz, y)
        dst = z_block(x, dz, y)
        step = (i + 1) // 2
        if i == 0 or (dz > 4 and step < 4):
            start(ref, dst, zu_send.at[step], zu_recv.at[step], z_next[0])
        if i == 0 or (dz < 4 and step < 3):
            start(ref, dst, zd_send.at[step], zd_recv.at[step], z_next[1])
        start(ref, dst, xu_send.at[i], xu_recv.at[i], x_next[0])
        start(ref, dst, xd_send.at[i], xd_recv.at[i], x_next[1])
        start(ref, dst, yu_send.at[i], yu_recv.at[i], y_next[0])
        start(ref, dst, yd_send.at[i], yd_recv.at[i], y_next[1])

    def z_landed(i):
        dz = ARRIVALS[i]
        step = (i - 1) // 2
        recv = zu_recv if dz >= 4 else zd_recv
        landed(z_block(x, dz, y), recv.at[step])

    def hop(step, h):
        for way in range(2):
            if step == 1:
                src, dst = far[h].at[pl.ds(2 * way, 2)], two[way][h].at[pl.ds(0, 2)]
            elif step == 2:
                src, dst = two[way][h], three[way][h].at[pl.ds(0, 6)]
            elif step == 3:
                src, dst = merged3[way][h], four[way][h].at[pl.ds(0, 8)]
            else:
                src, dst = merged4[way][h], last[h].at[pl.ds(8 * way, 8)]
            start(src, dst, fz_send.at[step - 1, way, h], fz_recv.at[step - 1, way, h], z_next[way])

    def hop_landed(step, h):
        for way in range(2):
            dst = (two[way][h].at[pl.ds(0, 2)], three[way][h].at[pl.ds(0, 6)],
                   four[way][h].at[pl.ds(0, 8)], last[h].at[pl.ds(8 * way, 8)])[step - 1]
            landed(dst, fz_recv.at[step - 1, way, h])

    def merge(step, h):
        for way in range(2):
            index = (1 if step == 3 else 2) if way == 0 else (5 if step == 3 else 4)
            for r in range(RSLOT):
                source = codes[0, index * RSLOT + r] // 64
                zs, ys = source // NY, lax.rem(source, NY)
                away = lax.rem((z - zs if way == 0 else zs - z) + NZ, NZ)
                if step == 3:
                    early = ys - 2 * way
                    early = jnp.where(jnp.logical_and(early >= 0, early < 2), early, 0)
                    at = jnp.where(away == 0, 6 + ys, jnp.where(away == 1, 2 + ys, early))
                    merged3[way][h][r] = three[way][h][at]
                else:
                    at = jnp.where(away == 0, 8 + ys, r)
                    merged4[way][h][r] = four[way][h][at]

    def to_core(sem, ref):
        start(ref, ref, core_send.at[sem], core_recv.at[sem], sibling)

    step_ids = lax.broadcasted_iota(jnp.int32, (MAXLEN, 128), 0)

    def norm(i, carry):
        for h in range(2):
            wide = xbuf[i, h * HALF : (h + 1) * HALF, :].astype(jnp.float32)
            mean = jnp.mean(wide, axis=1, keepdims=True)
            centred = wide - mean
            var = jnp.mean(centred * centred, axis=1, keepdims=True)
            normed[pl.ds(pl.multiple_of(i * MAXLEN + h * HALF, HALF), HALF), :] = (
                centred * lax.rsqrt(var + 1e-05) * gain[...].reshape(1, D)
            ).astype(jnp.bfloat16)
        return carry

    def load_row(dy):
        rows = lax.rem(y + dy, NY)
        far_chunk = full.at[lax.rem(x + ORDER[3], NX)]
        return pltpu.make_async_copy(far_chunk.at[:, rows], wbuf.at[3, :, rows], w_sem.at[3 + dy])

    def load_chunk(i):
        return pltpu.make_async_copy(
            full.at[lax.rem(x + ORDER[i], NX)], wbuf.at[i], w_sem.at[i]
        )

    def chunk(i):
        column = lax.rem(x + ORDER[i], NX) * CHUNK
        if i < 3:
            load_chunk(i).wait()
        else:
            for dy in range(NY):
                load_row(dy).wait()
        hidden[...] = jnp.dot(normed[...], wbuf[i, :, :, :, 0 : 2 * CHUNK].reshape(D, 2 * CHUNK), preferred_element_type=jnp.float32)
        for b in range(CHUNK // 128):
            lane = pl.ds(pl.multiple_of(column + b * 128, 128), 128)
            tap = [jnp.broadcast_to(taps[k : k + 1, lane], (8, 128)) for k in range(KERNEL)]
            mul = jnp.broadcast_to(scale[lane].reshape(1, 128), (16, 128))
            add = jnp.broadcast_to(shift[lane].reshape(1, 128), (16, 128))

            def conv(r, carry):
                base = pl.multiple_of(r * MAXLEN, MAXLEN)
                value = hidden[pl.ds(base, MAXLEN), b * 128 : b * 128 + 128]
                gate = hidden[pl.ds(base, MAXLEN), CHUNK + b * 128 : CHUNK + b * 128 + 128]
                gated = jnp.where(step_ids < lax.rem(codes[0, 3 * RSLOT + r], 64), value * jax.nn.sigmoid(gate), 0.0)
                window[r, PAD : PAD + MAXLEN, :] = gated
                total = [None] * 4
                for first in range(-7, MAXLEN):
                    rows = window[r, PAD + first : PAD + first + 8, :]
                    for t in range(4):
                        k = first + 15 - 8 * t
                        if 0 <= k < KERNEL:
                            term = rows * tap[k]
                            total[t] = term if total[t] is None else total[t] + term
                for pair in range(2):
                    s = jnp.concatenate(total[2 * pair : 2 * pair + 2], axis=0) * mul + add
                    act[pl.ds(pl.multiple_of(base + 16 * pair, 16), 16), lane] = (
                        s * jax.nn.sigmoid(s)
                    ).astype(jnp.bfloat16)
                return carry

            lax.fori_loop(0, RSLOT, conv, 0, unroll=4)

    spread(0)
    for dz in (3, 5):
        send_frames(dz)
    own.wait()
    for i in range(1, 8):
        z_landed(i)
        spread(i)
        if i == 2:
            frames_landed(4, 0)
            hop(1, 0)
        if i == 4:
            frames_landed(4, 1)
            hop(1, 1)
        if i in (5, 6):
            pick_frames((2, 6)[i - 5])
    to_core(0, piece(x, y))
    for dz in (2, 6):
        send_frames(dz)

    for h in range(2):
        hop_landed(1, h)
        frames_landed(3, h)
        frames_landed(5, h)
        hop(2, h)
    for dz in (1, 7, 0):
        pick_frames(dz)

    def x_start(j):
        dy, half = PIECES[j]
        ref = most(x, y + dy, half)
        start(ref, ref, xu_send.at[8 + j], xu_recv.at[8 + j], x_next[0])
        start(ref, ref, xd_send.at[8 + j], xd_recv.at[8 + j], x_next[1])
        to_core(1 + j, piece(x, y + dy, half))

    for i in range(8):
        landed(z_block(x, ARRIVALS[i], y + 3), yu_recv.at[i])
    ref = piece(x, y + 3, 0)
    start(ref, ref, yu_send.at[8], yu_recv.at[8], y_next[0])
    x_start(0)
    for i in range(8):
        landed(z_block(x, ARRIVALS[i], y + 1), yd_recv.at[i])
    ref = piece(x, y + 1, 1)
    start(ref, ref, yd_send.at[8], yd_recv.at[8], y_next[1])
    x_start(1)
    for dz in (1, 7):
        send_frames(dz)

    for i in range(8):
        below, above = z_block(x + 3, ARRIVALS[i], y), z_block(x + 1, ARRIVALS[i], y)
        landed(below, xu_recv.at[i])
        landed(above, xd_recv.at[i])
        if i % 2 == 0:
            start(below, below, xu_send.at[12 + i // 2], xu_recv.at[12 + i // 2], x_next[0])
        else:
            start(above, above, xd_send.at[12 + i // 2], xd_recv.at[12 + i // 2], x_next[1])
    to_core(5, piece(x + 3, y))
    to_core(6, piece(x + 1, y))
    late_start(0)
    late_start(1)
    send_frames(0)

    for h in range(2):
        hop_landed(2, h)
        frames_landed(2, h)
        frames_landed(6, h)
        merge(3, h)
        hop(3, h)

    landed(piece(x, y + 2, 0), yu_recv.at[8])
    x_start(2)
    landed(piece(x, y + 2, 1), yd_recv.at[8])
    x_start(3)

    def x_landed(j):
        dy, half = PIECES[j]
        below, above = most(x + 3, y + dy, half), most(x + 1, y + dy, half)
        landed(below, xu_recv.at[8 + j])
        landed(above, xd_recv.at[8 + j])
        if half in (None, 0):
            ref = most(x + 3, y + dy, 0)
            start(ref, ref, xu_send.at[16 + j], xu_recv.at[16 + j], x_next[0])
        if half in (None, 1):
            ref = most(x + 1, y + dy, 1)
            start(ref, ref, xd_send.at[16 + j], xd_recv.at[16 + j], x_next[1])
        to_core(7 + j, below)
        to_core(11 + j, above)

    def x_far_landed(j):
        dy, half = PIECES[j]
        if half in (None, 0):
            landed(most(x + 2, y + dy, 0), xu_recv.at[16 + j])
        if half in (None, 1):
            landed(most(x + 2, y + dy, 1), xd_recv.at[16 + j])
        to_core(15 + j, most(x + 2, y + dy, half))

    x_landed(0)
    for i in range(8):
        recv = xu_recv if i % 2 == 0 else xd_recv
        landed(z_block(x + 2, ARRIVALS[i], y), recv.at[12 + i // 2])
    to_core(19, piece(x + 2, y))
    late_start(2)

    for h in range(2):
        hop_landed(3, h)
        frames_landed(1, h)
        frames_landed(7, h)
        merge(4, h)
        hop(4, h)
    landed(piece(x, y, None, other), core_recv.at[0])
    for j, (dy, half) in enumerate(PIECES):
        landed(piece(x, y + dy, half, other), core_recv.at[1 + j])
    load_chunk(0).start()
    for k in range(3):
        late_landed(k)
    x_landed(1)
    x_far_landed(0)
    x_landed(2)
    x_far_landed(1)
    for k in range(3):
        late_far_landed(k)
    x_landed(3)

    for load in loads[3:]:
        load.wait()
    for h in range(2):
        hop_landed(4, h)
        frames_landed(0, h)
        for r in range(RSLOT):
            source = codes[0, 3 * RSLOT + r] // 64
            zs, ys = source // NY, lax.rem(source, NY)
            away = lax.rem(z - zs + NZ, NZ)
            above = jnp.logical_or(away > 4, jnp.logical_and(away == 4, ys >= 2))
            at = jnp.where(away == 0, 16 + ys, jnp.where(above, 8 + r, r))
            xbuf[r, h * HALF : (h + 1) * HALF, :] = last[h][at]
    x_far_landed(2)
    lax.fori_loop(0, RSLOT, norm, 0)

    for i, (first, whole) in ((1, (7, 5)), (2, (11, 6))):
        landed(piece(x + ORDER[i], y, None, other), core_recv.at[whole])
        for j, (dy, half) in enumerate(PIECES):
            landed(most(x + ORDER[i], y + dy, half, other), core_recv.at[first + j])
        for j, dy in enumerate((3, 1, 2)):
            landed(late(x + ORDER[i], y + dy, other), core_recv.at[17 + 3 * i + j])
        load_chunk(i).start()
    chunk(0)
    x_far_landed(3)
    chunk(1)
    for j, dy in enumerate((3, 1, 2)):
        landed(late(x + 2, y + dy, other), core_recv.at[26 + j])
    landed(piece(x + 2, y, None, other), core_recv.at[19])
    load_row(0).start()
    for j in range(2):
        dy = PIECES[j][0]
        landed(most(x + 2, y + dy, None, other), core_recv.at[15 + j])
        load_row(dy).start()
    chunk(2)
    for j in range(2, 4):
        landed(most(x + 2, y + 2, PIECES[j][1], other), core_recv.at[15 + j])
    load_row(2).start()
    chunk(3)
    for i in range(NX):
        lane = pl.ds(pl.multiple_of(lax.rem(x + ORDER[i], NX) * CHUNK, 128), CHUNK)
        hidden[:, 0:CHUNK] = jnp.dot(
            act[...], wbuf[i, :, :, :, 2 * CHUNK : 3 * CHUNK].reshape(D, CHUNK), preferred_element_type=jnp.float32
        )

        ids = lax.broadcasted_iota(jnp.int32, (MAXLEN, CHUNK), 0)

        def close(r, carry):
            mixed = xbuf[r, :, lane].astype(jnp.float32) + hidden[
                pl.ds(pl.multiple_of(r * MAXLEN, MAXLEN), MAXLEN), 0:CHUNK
            ]
            out[r, :, lane] = jnp.where(ids < lax.rem(codes[0, 3 * RSLOT + r], 64), mixed, 0.0).astype(jnp.bfloat16)
            return carry

        lax.fori_loop(0, RSLOT, close, 0)

    for t in range(NX):
        same = jnp.logical_and(x == t, keeper == c)

        @pl.when(jnp.logical_not(same))
        def _():
            remote(wp.at[t], parts.at[0], part_send.at[t], part_recv.at[0], sibling).wait_send()

    for copy in started:
        copy.wait_send()


def communicate(codes, frames, w_in, w_out, gain, taps, scale, shift):
    dma = pltpu.SemaphoreType.DMA
    smem = pl.BlockSpec(memory_space=pltpu.SMEM)
    vmem = pl.BlockSpec(memory_space=pltpu.VMEM)
    hbm = pl.BlockSpec(memory_space=pltpu.HBM)

    def slots(n):
        return [pltpu.VMEM((n, HALF, D), jnp.bfloat16)]

    return pl.pallas_call(
        comm_kernel,
        out_shape=(
            jax.ShapeDtypeStruct((RSLOT, MAXLEN, D), jnp.bfloat16),
            jax.ShapeDtypeStruct((NX, NZ, NY, NC * BLOCK_ROWS, BLOCK_COLS), jnp.bfloat16),
        ),
        in_specs=[smem] + [hbm] * 7,
        out_specs=(vmem, pl.BlockSpec(memory_space=pl.ANY)),
        scratch_shapes=[
            pltpu.VMEM((RSLOT, MAXLEN, D), jnp.bfloat16),
            pltpu.VMEM((NX, NZ, NY, NC * BLOCK_ROWS, BLOCK_COLS), jnp.bfloat16),
            pltpu.VMEM((RSLOT * MAXLEN, D), jnp.bfloat16),
            pltpu.VMEM((RSLOT * MAXLEN, 2 * CHUNK), jnp.float32),
            pltpu.VMEM((RSLOT, MAXLEN + 2 * PAD, 128), jnp.float32),
            pltpu.VMEM((RSLOT * MAXLEN, D), jnp.bfloat16),
            pltpu.VMEM((D,), jnp.float32),
            pltpu.VMEM((KERNEL, D), jnp.float32),
            pltpu.VMEM((D,), jnp.float32),
            pltpu.VMEM((D,), jnp.float32),
            dma((NX + 3,)),
            pltpu.VMEM(frames.shape, jnp.bfloat16),
            pltpu.VMEM(w_in.shape, jnp.bfloat16),
            pltpu.VMEM(w_out.shape, jnp.bfloat16),
            pltpu.VMEM((NX, 8, BLOCK_COLS), jnp.bfloat16),
            pltpu.VMEM((4, 8, BLOCK_COLS), jnp.bfloat16),
            pltpu.VMEM((BLOCK_ROWS, BLOCK_COLS), jnp.bfloat16),
            pltpu.VMEM((NZ, NY - 1, MAXLEN, D), jnp.bfloat16),
            *(slots(4) * 2 + slots(6) * 4 + slots(10) * 4 + slots(12) * 4 + slots(20) * 2 + slots(8) * 8),
            dma((NZ, NY - 1, 2)), dma((NZ, NY - 1, 2)), dma((4, 2, 2)), dma((4, 2, 2)),
            dma((4,)), dma((4,)), dma((9,)),
            dma((4,)), dma((4,)), dma((3,)), dma((3,)),
            dma((9,)), dma((9,)), dma((9,)), dma((9,)),
            dma((20,)), dma((20,)), dma((20,)), dma((20,)),
            dma((29,)), dma((29,)), dma((5,)), dma((5,)), dma((4,)), dma((4,)),
        ],
        compiler_params=pltpu.CompilerParams(
            collective_id=0, has_side_effects=True, vmem_limit_bytes=67043328
        ),
        name="exchange",
    )(codes, frames, w_in, w_out, gain, taps, scale, shift)


def table_kernel(tab_len, tab_dest, tab_off, codes, rows):
    dp = lax.axis_index("dp")
    length, dest = tab_len[...], tab_dest[...]
    live = length > 0
    loader = lax.broadcasted_iota(jnp.int32, length.shape, 1)
    slot = lax.broadcasted_iota(jnp.int32, length.shape, 0).astype(jnp.float32)
    key_in = jnp.where(live, dest * RSLOT + tab_off[...] // MAXLEN, -1)
    key_out = jnp.where(jnp.logical_and(live, loader == dp), dest, -1)
    code = (loader * 64 + length).astype(jnp.float32)
    rows[...] = jnp.zeros_like(rows)
    for entry in range(6 * RSLOT + N_DP):
        if entry < 6 * RSLOT:
            target = lax.rem(dp // NY + 3 + NZ - entry // RSLOT, NZ) * NY + dp % NY
            picked = jnp.where(key_in == target * RSLOT + entry % RSLOT, code, 0.0)
        else:
            picked = jnp.where(key_out == entry - 6 * RSLOT, slot, 0.0)
        rows[entry : entry + 1, :] = jnp.sum(picked, axis=0, keepdims=True)
    total = lax.dot_general(
        jnp.ones((8, rows.shape[1]), jnp.float32), rows[...], (((1,), (1,)), ((), ())),
        precision=lax.Precision.HIGHEST, preferred_element_type=jnp.float32,
    )
    codes[...] = (total[0:1] + 0.5).astype(jnp.int32)


def table(tab_len, tab_dest, tab_off):
    vmem = pl.BlockSpec(memory_space=pltpu.VMEM)
    return pl.pallas_call(
        table_kernel,
        out_shape=jax.ShapeDtypeStruct((1, 128), jnp.int32),
        in_specs=[vmem] * 3,
        out_specs=vmem,
        scratch_shapes=[pltpu.VMEM((128, tab_len.shape[1]), jnp.float32)],
        name="table",
    )(tab_len, tab_dest, tab_off)


def shards(frames, ln_gain, w_in, depth_kernel, bn_scale, bn_shift, w_out, lengths, destinations, offsets):
    tab_len, tab_dest, tab_off = lengths[0], destinations[0], offsets[0]
    codes = table(tab_len.T, tab_dest.T, tab_off.T)
    out, _ = communicate(codes, frames[0], w_in, w_out, ln_gain, depth_kernel, bn_scale, bn_shift)
    return out[None]


def solution(mesh):
    return jax.shard_map(
        shards,
        mesh=mesh,
        in_specs=(
            P("fsdp", "dp", None, None),
            P(),
            P(("dp", "fsdp"), None),
            P(),
            P(),
            P(),
            P(("dp", "fsdp"), None),
            P("fsdp", None, None),
            P("fsdp", None, None),
            P("fsdp", None, None),
        ),
        out_specs=P("fsdp", "dp", None, None),
        check_vma=False,
    )
```

```python
import jax
import jax.numpy as jnp
from jax import lax
from jax.experimental import pallas as pl
from jax.experimental.pallas import tpu as pltpu
from jax.sharding import PartitionSpec as P

MESH = pl.DeviceIdType.MESH

D = 1536
KERNEL = 31
MAXLEN = 32
RSLOT = 8
NZ, NY, NX, NC = 8, 4, 4, 2
N_DP = NZ * NY
SHARD_ROWS = 6
BLOCK_ROWS = 24
CHUNK = D // NX
BLOCK_COLS = 3 * CHUNK
PAD = 16

HALF = MAXLEN // 2
PIECES = [(3, None), (1, None), (2, 0), (2, 1)]
ARRIVALS = [0, 7, 1, 6, 2, 5, 3, 4]
ORDER = (0, 3, 1, 2)


def comm_kernel(
    codes, frames_hbm, w_in_hbm, w_out_hbm, gain_hbm, taps_hbm, scale_hbm, shift_hbm, out, full,
    xbuf, wbuf, normed, hidden, window, act, gain, taps, scale, shift, w_sem,
    frames, w_in, w_out, wp, parts, block, staged,
    far0, far1, up2_0, up2_1, dn2_0, dn2_1, up3_0, up3_1, dn3_0, dn3_1, up4_0, up4_1, dn4_0, dn4_1, last0, last1,
    mu3_0, mu3_1, md3_0, md3_1, mu4_0, mu4_1, md4_0, md4_1,
    fy_send, fy_recv, fz_send, fz_recv,
    part_send, part_recv, local_sem,
    zu_send, zu_recv, zd_send, zd_recv,
    yu_send, yu_recv, yd_send, yd_recv,
    xu_send, xu_recv, xd_send, xd_recv,
    core_send, core_recv, lu_send, lu_recv, ld_send, ld_recv,
):
    dp = lax.axis_index("dp")
    fs = lax.axis_index("fsdp")
    z, y = dp // NY, dp % NY
    x, c = fs // NC, fs % NC
    other = 1 - c
    far, last = (far0, far1), (last0, last1)
    two = ((up2_0, up2_1), (dn2_0, dn2_1))
    three = ((up3_0, up3_1), (dn3_0, dn3_1))
    four = ((up4_0, up4_1), (dn4_0, dn4_1))
    merged3 = ((mu3_0, mu3_1), (md3_0, md3_1))
    merged4 = ((mu4_0, mu4_1), (md4_0, md4_1))

    def kept(cc):
        return pl.ds(pl.multiple_of(cc * BLOCK_ROWS, 8), BLOCK_ROWS)

    def dev(zz, yy, xx, cc):
        return (lax.rem(zz, NZ) * NY + lax.rem(yy, NY), lax.rem(xx, NX) * NC + cc)

    sibling = (dp, x * NC + other)
    z_next = (dev(z + 1, y, x, c), dev(z + NZ - 1, y, x, c))
    y_next = (dev(z, y + 1, x, c), dev(z, y + NY - 1, x, c))
    x_next = (dev(z, y, x + 1, c), dev(z, y, x + NX - 1, c))

    barrier = pltpu.get_barrier_semaphore()

    def greet(device):
        pl.semaphore_signal(barrier, inc=1, device_id=device, device_id_type=MESH)

    for k in range(1, NX * NC):
        greet((dp, lax.rem(fs + k, NX * NC)))
    for k in range(1, NY):
        greet(dev(z, y + k, x, c))
    for device in z_next:
        greet(device)

    loads = [
        pltpu.make_async_copy(w_in_hbm, w_in, local_sem.at[2]),
        pltpu.make_async_copy(w_out_hbm, w_out, local_sem.at[3]),
        pltpu.make_async_copy(frames_hbm, frames, local_sem.at[4]),
        pltpu.make_async_copy(gain_hbm, gain, local_sem.at[5]),
        pltpu.make_async_copy(taps_hbm, taps, local_sem.at[6]),
        pltpu.make_async_copy(scale_hbm, scale, local_sem.at[7]),
        pltpu.make_async_copy(shift_hbm, shift, local_sem.at[8]),
    ]
    for load in loads:
        load.start()

    def remote(src, dst, send, recv, device):
        return pltpu.make_async_remote_copy(
            src_ref=src, dst_ref=dst, send_sem=send, recv_sem=recv, device_id=device, device_id_type=MESH
        )

    started = []

    def start(src, dst, s_sem, r_sem, device):
        copy = remote(src, dst, s_sem, r_sem, device)
        copy.start()
        started.append(copy)

    def landed(ref, r_sem):
        remote(ref, ref, fy_send.at[0, 0, 0], r_sem, sibling).wait_recv()

    homes = {
        4: (far, 0), 3: (two[0], 2), 5: (two[1], 2), 2: (three[0], 6), 6: (three[1], 6),
        1: (four[0], 8), 7: (four[1], 8), 0: (last, 16),
    }

    def pick_frames(dz):
        for dy in range(NY):
            slot = codes[0, 6 * RSLOT + dev(z + dz, y + dy, x, c)[0]]
            if dy:
                staged[dz, dy - 1] = frames[slot]
            else:
                refs, first = homes[dz]
                for h in range(2):
                    refs[h][first + y] = frames[slot, h * HALF : (h + 1) * HALF, :]

    def send_frames(dz):
        refs, first = homes[dz]
        for h in range(2):
            for dy in (1, 3, 2):
                start(
                    staged.at[dz, dy - 1, pl.ds(h * HALF, HALF)], refs[h].at[first + y],
                    fy_send.at[dz, dy - 1, h], fy_recv.at[dz, dy - 1, h], dev(z, y + dy, x, c),
                )

    def frames_landed(dz, h):
        refs, first = homes[dz]
        for dy in (1, 3, 2):
            landed(refs[h].at[first + lax.rem(y + NY - dy, NY)], fy_recv.at[dz, dy - 1, h])

    wp[...] = jnp.zeros_like(wp)
    window[...] = jnp.zeros_like(window)
    for load in loads[:2]:
        load.wait()
    for t in range(NX):
        wp[t, 0:SHARD_ROWS, 0:CHUNK] = w_in[:, t * CHUNK : (t + 1) * CHUNK]
        wp[t, 0:SHARD_ROWS, CHUNK : 2 * CHUNK] = w_in[:, D + t * CHUNK : D + (t + 1) * CHUNK]
        wp[t, 0:SHARD_ROWS, 2 * CHUNK : 3 * CHUNK] = w_out[:, t * CHUNK : (t + 1) * CHUNK]
    loads[2].wait()
    pick_frames(4)
    pl.semaphore_wait(barrier, NX * NC + NY)

    slot_here = lax.rem(x, 2) * NC + c
    keeper = x // 2
    for t in range(NX):
        same = jnp.logical_and(x == t, keeper == c)

        @pl.when(jnp.logical_not(same))
        def _():
            remote(wp.at[t], parts.at[slot_here], part_send.at[t], part_recv.at[slot_here], (dp, t * NC + keeper)).start()

        @pl.when(same)
        def _():
            pltpu.make_async_copy(wp.at[t], parts.at[slot_here], local_sem.at[0]).start()

    send_frames(4)
    for dz in (3, 5):
        pick_frames(dz)

    for k in range(4):
        source = c * 4 + k

        @pl.when(source != fs)
        def _():
            landed(parts.at[k], part_recv.at[k])

        @pl.when(source == fs)
        def _():
            pltpu.make_async_copy(wp.at[0], parts.at[k], local_sem.at[0]).wait()

    row = lax.broadcasted_iota(jnp.int32, (BLOCK_ROWS, 32), 0)
    col = lax.broadcasted_iota(jnp.int32, (BLOCK_ROWS, 32), 1)
    pick = (col == (row // SHARD_ROWS) * 8 + lax.rem(row, SHARD_ROWS)).astype(jnp.bfloat16)
    block[...] = jnp.dot(
        pick, parts[...].reshape(32, BLOCK_COLS), preferred_element_type=jnp.float32
    ).astype(jnp.bfloat16)

    own = pltpu.make_async_copy(block, full.at[x, z, y, kept(c)], local_sem.at[1])
    own.start()

    def z_block(xx, dz, yy):
        return full.at[lax.rem(xx, NX), lax.rem(z + dz, NZ), lax.rem(yy, NY), kept(c)]

    def piece(xx, yy, half=None, cc=None):
        rows = slice(None) if half is None else pl.ds(half * 4, 4)
        return full.at[lax.rem(xx, NX), rows, lax.rem(yy, NY), kept(c if cc is None else cc)]

    def most(xx, yy, half=None, cc=None):
        rows = pl.ds(0, NZ - 1) if half is None else pl.ds(half * 4, 4 - half)
        return full.at[lax.rem(xx, NX), rows, lax.rem(yy, NY), kept(c if cc is None else cc)]

    def late(xx, yy, cc=None):
        return full.at[lax.rem(xx, NX), NZ - 1, lax.rem(yy, NY), kept(c if cc is None else cc)]

    def late_start(k):
        ref = late(x + ORDER[k + 1], y)
        start(ref, ref, lu_send.at[k], lu_recv.at[k], y_next[0])
        start(ref, ref, ld_send.at[k], ld_recv.at[k], y_next[1])

    def late_landed(k):
        below, above = late(x + ORDER[k + 1], y + 3), late(x + ORDER[k + 1], y + 1)
        landed(below, lu_recv.at[k])
        landed(above, ld_recv.at[k])
        if k == 1:
            start(above, above, ld_send.at[3], ld_recv.at[3], y_next[1])
        else:
            start(below, below, lu_send.at[3 + k // 2], lu_recv.at[3 + k // 2], y_next[0])
        to_core(20 + 3 * k, below)
        to_core(21 + 3 * k, above)

    def late_far_landed(k):
        ref = late(x + ORDER[k + 1], y + 2)
        landed(ref, ld_recv.at[3] if k == 1 else lu_recv.at[3 + k // 2])
        to_core(22 + 3 * k, ref)

    def spread(i):
        dz = ARRIVALS[i]
        ref = block if i == 0 else z_block(x, dz, y)
        dst = z_block(x, dz, y)
        step = (i + 1) // 2
        if i == 0 or (dz > 4 and step < 4):
            start(ref, dst, zu_send.at[step], zu_recv.at[step], z_next[0])
        if i == 0 or (dz < 4 and step < 3):
            start(ref, dst, zd_send.at[step], zd_recv.at[step], z_next[1])
        start(ref, dst, xu_send.at[i], xu_recv.at[i], x_next[0])
        start(ref, dst, xd_send.at[i], xd_recv.at[i], x_next[1])
        start(ref, dst, yu_send.at[i], yu_recv.at[i], y_next[0])
        start(ref, dst, yd_send.at[i], yd_recv.at[i], y_next[1])

    def z_landed(i):
        dz = ARRIVALS[i]
        step = (i - 1) // 2
        recv = zu_recv if dz >= 4 else zd_recv
        landed(z_block(x, dz, y), recv.at[step])

    def hop(step, h):
        for way in range(2):
            if step == 1:
                src, dst = far[h].at[pl.ds(2 * way, 2)], two[way][h].at[pl.ds(0, 2)]
            elif step == 2:
                src, dst = two[way][h], three[way][h].at[pl.ds(0, 6)]
            elif step == 3:
                src, dst = merged3[way][h], four[way][h].at[pl.ds(0, 8)]
            else:
                src, dst = merged4[way][h], last[h].at[pl.ds(8 * way, 8)]
            start(src, dst, fz_send.at[step - 1, way, h], fz_recv.at[step - 1, way, h], z_next[way])

    def hop_landed(step, h):
        for way in range(2):
            dst = (two[way][h].at[pl.ds(0, 2)], three[way][h].at[pl.ds(0, 6)],
                   four[way][h].at[pl.ds(0, 8)], last[h].at[pl.ds(8 * way, 8)])[step - 1]
            landed(dst, fz_recv.at[step - 1, way, h])

    def merge(step, h):
        for way in range(2):
            index = (1 if step == 3 else 2) if way == 0 else (5 if step == 3 else 4)
            for r in range(RSLOT):
                source = codes[0, index * RSLOT + r] // 64
                zs, ys = source // NY, lax.rem(source, NY)
                away = lax.rem((z - zs if way == 0 else zs - z) + NZ, NZ)
                if step == 3:
                    early = ys - 2 * way
                    early = jnp.where(jnp.logical_and(early >= 0, early < 2), early, 0)
                    at = jnp.where(away == 0, 6 + ys, jnp.where(away == 1, 2 + ys, early))
                    merged3[way][h][r] = three[way][h][at]
                else:
                    at = jnp.where(away == 0, 8 + ys, r)
                    merged4[way][h][r] = four[way][h][at]

    def to_core(sem, ref):
        start(ref, ref, core_send.at[sem], core_recv.at[sem], sibling)

    step_ids = lax.broadcasted_iota(jnp.int32, (MAXLEN, 128), 0)

    def norm(i, carry):
        for h in range(2):
            wide = xbuf[i, h * HALF : (h + 1) * HALF, :].astype(jnp.float32)
            mean = jnp.mean(wide, axis=1, keepdims=True)
            centred = wide - mean
            var = jnp.mean(centred * centred, axis=1, keepdims=True)
            normed[pl.ds(pl.multiple_of(i * MAXLEN + h * HALF, HALF), HALF), :] = (
                centred * lax.rsqrt(var + 1e-05) * gain[...].reshape(1, D)
            ).astype(jnp.bfloat16)
        return carry

    def load_row(dy):
        rows = lax.rem(y + dy, NY)
        far_chunk = full.at[lax.rem(x + ORDER[3], NX)]
        return pltpu.make_async_copy(far_chunk.at[:, rows], wbuf.at[3, :, rows], w_sem.at[3 + dy])

    def load_chunk(i):
        return pltpu.make_async_copy(
            full.at[lax.rem(x + ORDER[i], NX)], wbuf.at[i], w_sem.at[i]
        )

    def chunk(i):
        column = lax.rem(x + ORDER[i], NX) * CHUNK
        if i < 3:
            load_chunk(i).wait()
        else:
            for dy in range(NY):
                load_row(dy).wait()
        hidden[...] = jnp.dot(normed[...], wbuf[i, :, :, :, 0 : 2 * CHUNK].reshape(D, 2 * CHUNK), preferred_element_type=jnp.float32)
        for b in range(CHUNK // 128):
            lane = pl.ds(pl.multiple_of(column + b * 128, 128), 128)
            tap = [jnp.broadcast_to(taps[k : k + 1, lane], (8, 128)) for k in range(KERNEL)]
            mul = jnp.broadcast_to(scale[lane].reshape(1, 128), (16, 128))
            add = jnp.broadcast_to(shift[lane].reshape(1, 128), (16, 128))

            def conv(r, carry):
                base = pl.multiple_of(r * MAXLEN, MAXLEN)
                value = hidden[pl.ds(base, MAXLEN), b * 128 : b * 128 + 128]
                gate = hidden[pl.ds(base, MAXLEN), CHUNK + b * 128 : CHUNK + b * 128 + 128]
                gated = jnp.where(step_ids < lax.rem(codes[0, 3 * RSLOT + r], 64), value * jax.nn.sigmoid(gate), 0.0)
                window[r, PAD : PAD + MAXLEN, :] = gated
                total = [None] * 4
                for first in range(-7, MAXLEN):
                    rows = window[r, PAD + first : PAD + first + 8, :]
                    for t in range(4):
                        k = first + 15 - 8 * t
                        if 0 <= k < KERNEL:
                            term = rows * tap[k]
                            total[t] = term if total[t] is None else total[t] + term
                for pair in range(2):
                    s = jnp.concatenate(total[2 * pair : 2 * pair + 2], axis=0) * mul + add
                    act[pl.ds(pl.multiple_of(base + 16 * pair, 16), 16), lane] = (
                        s * jax.nn.sigmoid(s)
                    ).astype(jnp.bfloat16)
                return carry

            lax.fori_loop(0, RSLOT, conv, 0, unroll=8)

    spread(0)
    for dz in (3, 5):
        send_frames(dz)
    own.wait()
    for i in range(1, 8):
        z_landed(i)
        spread(i)
        if i == 2:
            frames_landed(4, 0)
            hop(1, 0)
        if i == 4:
            frames_landed(4, 1)
            hop(1, 1)
        if i in (5, 6):
            pick_frames((2, 6)[i - 5])
    to_core(0, piece(x, y))
    for dz in (2, 6):
        send_frames(dz)

    for h in range(2):
        hop_landed(1, h)
        frames_landed(3, h)
        frames_landed(5, h)
        hop(2, h)
    for dz in (1, 7, 0):
        pick_frames(dz)

    def x_start(j):
        dy, half = PIECES[j]
        ref = most(x, y + dy, half)
        start(ref, ref, xu_send.at[8 + j], xu_recv.at[8 + j], x_next[0])
        start(ref, ref, xd_send.at[8 + j], xd_recv.at[8 + j], x_next[1])
        to_core(1 + j, piece(x, y + dy, half))

    for i in range(8):
        landed(z_block(x, ARRIVALS[i], y + 3), yu_recv.at[i])
    ref = piece(x, y + 3, 0)
    start(ref, ref, yu_send.at[8], yu_recv.at[8], y_next[0])
    x_start(0)
    for i in range(8):
        landed(z_block(x, ARRIVALS[i], y + 1), yd_recv.at[i])
    ref = piece(x, y + 1, 1)
    start(ref, ref, yd_send.at[8], yd_recv.at[8], y_next[1])
    x_start(1)
    for dz in (1, 7):
        send_frames(dz)

    for i in range(8):
        below, above = z_block(x + 3, ARRIVALS[i], y), z_block(x + 1, ARRIVALS[i], y)
        landed(below, xu_recv.at[i])
        landed(above, xd_recv.at[i])
        if i % 2 == 0:
            start(below, below, xu_send.at[12 + i // 2], xu_recv.at[12 + i // 2], x_next[0])
        else:
            start(above, above, xd_send.at[12 + i // 2], xd_recv.at[12 + i // 2], x_next[1])
    to_core(5, piece(x + 3, y))
    to_core(6, piece(x + 1, y))
    late_start(0)
    late_start(1)
    send_frames(0)

    for h in range(2):
        hop_landed(2, h)
        frames_landed(2, h)
        frames_landed(6, h)
        merge(3, h)
        hop(3, h)

    landed(piece(x, y + 2, 0), yu_recv.at[8])
    x_start(2)
    landed(piece(x, y + 2, 1), yd_recv.at[8])
    x_start(3)

    def x_landed(j):
        dy, half = PIECES[j]
        below, above = most(x + 3, y + dy, half), most(x + 1, y + dy, half)
        landed(below, xu_recv.at[8 + j])
        landed(above, xd_recv.at[8 + j])
        if half in (None, 0):
            ref = most(x + 3, y + dy, 0)
            start(ref, ref, xu_send.at[16 + j], xu_recv.at[16 + j], x_next[0])
        if half in (None, 1):
            ref = most(x + 1, y + dy, 1)
            start(ref, ref, xd_send.at[16 + j], xd_recv.at[16 + j], x_next[1])
        to_core(7 + j, below)
        to_core(11 + j, above)

    def x_far_landed(j):
        dy, half = PIECES[j]
        if half in (None, 0):
            landed(most(x + 2, y + dy, 0), xu_recv.at[16 + j])
        if half in (None, 1):
            landed(most(x + 2, y + dy, 1), xd_recv.at[16 + j])
        to_core(15 + j, most(x + 2, y + dy, half))

    x_landed(0)
    for i in range(8):
        recv = xu_recv if i % 2 == 0 else xd_recv
        landed(z_block(x + 2, ARRIVALS[i], y), recv.at[12 + i // 2])
    to_core(19, piece(x + 2, y))
    late_start(2)

    for h in range(2):
        hop_landed(3, h)
        frames_landed(1, h)
        frames_landed(7, h)
        merge(4, h)
        hop(4, h)
    landed(piece(x, y, None, other), core_recv.at[0])
    for j, (dy, half) in enumerate(PIECES):
        landed(piece(x, y + dy, half, other), core_recv.at[1 + j])
    load_chunk(0).start()
    for k in range(3):
        late_landed(k)
    x_landed(1)
    x_far_landed(0)
    x_landed(2)
    x_far_landed(1)
    for k in range(3):
        late_far_landed(k)
    x_landed(3)

    for load in loads[3:]:
        load.wait()
    for h in range(2):
        hop_landed(4, h)
        frames_landed(0, h)
        for r in range(RSLOT):
            source = codes[0, 3 * RSLOT + r] // 64
            zs, ys = source // NY, lax.rem(source, NY)
            away = lax.rem(z - zs + NZ, NZ)
            above = jnp.logical_or(away > 4, jnp.logical_and(away == 4, ys >= 2))
            at = jnp.where(away == 0, 16 + ys, jnp.where(above, 8 + r, r))
            xbuf[r, h * HALF : (h + 1) * HALF, :] = last[h][at]
    x_far_landed(2)
    lax.fori_loop(0, RSLOT, norm, 0)

    for i, (first, whole) in ((1, (7, 5)), (2, (11, 6))):
        landed(piece(x + ORDER[i], y, None, other), core_recv.at[whole])
        for j, (dy, half) in enumerate(PIECES):
            landed(most(x + ORDER[i], y + dy, half, other), core_recv.at[first + j])
        for j, dy in enumerate((3, 1, 2)):
            landed(late(x + ORDER[i], y + dy, other), core_recv.at[17 + 3 * i + j])
        load_chunk(i).start()
    chunk(0)
    x_far_landed(3)
    chunk(1)
    for j, dy in enumerate((3, 1, 2)):
        landed(late(x + 2, y + dy, other), core_recv.at[26 + j])
    landed(piece(x + 2, y, None, other), core_recv.at[19])
    load_row(0).start()
    for j in range(2):
        dy = PIECES[j][0]
        landed(most(x + 2, y + dy, None, other), core_recv.at[15 + j])
        load_row(dy).start()
    chunk(2)
    for j in range(2, 4):
        landed(most(x + 2, y + 2, PIECES[j][1], other), core_recv.at[15 + j])
    load_row(2).start()
    chunk(3)
    for i in range(NX):
        lane = pl.ds(pl.multiple_of(lax.rem(x + ORDER[i], NX) * CHUNK, 128), CHUNK)
        hidden[:, 0:CHUNK] = jnp.dot(
            act[...], wbuf[i, :, :, :, 2 * CHUNK : 3 * CHUNK].reshape(D, CHUNK), preferred_element_type=jnp.float32
        )

        ids = lax.broadcasted_iota(jnp.int32, (MAXLEN, CHUNK), 0)

        def close(r, carry):
            mixed = xbuf[r, :, lane].astype(jnp.float32) + hidden[
                pl.ds(pl.multiple_of(r * MAXLEN, MAXLEN), MAXLEN), 0:CHUNK
            ]
            out[r, :, lane] = jnp.where(ids < lax.rem(codes[0, 3 * RSLOT + r], 64), mixed, 0.0).astype(jnp.bfloat16)
            return carry

        lax.fori_loop(0, RSLOT, close, 0, unroll=4)

    for t in range(NX):
        same = jnp.logical_and(x == t, keeper == c)

        @pl.when(jnp.logical_not(same))
        def _():
            remote(wp.at[t], parts.at[0], part_send.at[t], part_recv.at[0], sibling).wait_send()

    for copy in started:
        copy.wait_send()


def communicate(codes, frames, w_in, w_out, gain, taps, scale, shift):
    dma = pltpu.SemaphoreType.DMA
    smem = pl.BlockSpec(memory_space=pltpu.SMEM)
    vmem = pl.BlockSpec(memory_space=pltpu.VMEM)
    hbm = pl.BlockSpec(memory_space=pltpu.HBM)

    def slots(n):
        return [pltpu.VMEM((n, HALF, D), jnp.bfloat16)]

    return pl.pallas_call(
        comm_kernel,
        out_shape=(
            jax.ShapeDtypeStruct((RSLOT, MAXLEN, D), jnp.bfloat16),
            jax.ShapeDtypeStruct((NX, NZ, NY, NC * BLOCK_ROWS, BLOCK_COLS), jnp.bfloat16),
        ),
        in_specs=[smem] + [hbm] * 7,
        out_specs=(vmem, pl.BlockSpec(memory_space=pl.ANY)),
        scratch_shapes=[
            pltpu.VMEM((RSLOT, MAXLEN, D), jnp.bfloat16),
            pltpu.VMEM((NX, NZ, NY, NC * BLOCK_ROWS, BLOCK_COLS), jnp.bfloat16),
            pltpu.VMEM((RSLOT * MAXLEN, D), jnp.bfloat16),
            pltpu.VMEM((RSLOT * MAXLEN, 2 * CHUNK), jnp.float32),
            pltpu.VMEM((RSLOT, MAXLEN + 2 * PAD, 128), jnp.float32),
            pltpu.VMEM((RSLOT * MAXLEN, D), jnp.bfloat16),
            pltpu.VMEM((D,), jnp.float32),
            pltpu.VMEM((KERNEL, D), jnp.float32),
            pltpu.VMEM((D,), jnp.float32),
            pltpu.VMEM((D,), jnp.float32),
            dma((NX + 3,)),
            pltpu.VMEM(frames.shape, jnp.bfloat16),
            pltpu.VMEM(w_in.shape, jnp.bfloat16),
            pltpu.VMEM(w_out.shape, jnp.bfloat16),
            pltpu.VMEM((NX, 8, BLOCK_COLS), jnp.bfloat16),
            pltpu.VMEM((4, 8, BLOCK_COLS), jnp.bfloat16),
            pltpu.VMEM((BLOCK_ROWS, BLOCK_COLS), jnp.bfloat16),
            pltpu.VMEM((NZ, NY - 1, MAXLEN, D), jnp.bfloat16),
            *(slots(4) * 2 + slots(6) * 4 + slots(10) * 4 + slots(12) * 4 + slots(20) * 2 + slots(8) * 8),
            dma((NZ, NY - 1, 2)), dma((NZ, NY - 1, 2)), dma((4, 2, 2)), dma((4, 2, 2)),
            dma((4,)), dma((4,)), dma((9,)),
            dma((4,)), dma((4,)), dma((3,)), dma((3,)),
            dma((9,)), dma((9,)), dma((9,)), dma((9,)),
            dma((20,)), dma((20,)), dma((20,)), dma((20,)),
            dma((29,)), dma((29,)), dma((5,)), dma((5,)), dma((4,)), dma((4,)),
        ],
        compiler_params=pltpu.CompilerParams(
            collective_id=0, has_side_effects=True, vmem_limit_bytes=67043328
        ),
        name="exchange",
    )(codes, frames, w_in, w_out, gain, taps, scale, shift)


def table_kernel(tab_len, tab_dest, tab_off, codes, rows):
    dp = lax.axis_index("dp")
    length, dest = tab_len[...], tab_dest[...]
    live = length > 0
    loader = lax.broadcasted_iota(jnp.int32, length.shape, 1)
    slot = lax.broadcasted_iota(jnp.int32, length.shape, 0).astype(jnp.float32)
    key_in = jnp.where(live, dest * RSLOT + tab_off[...] // MAXLEN, -1)
    key_out = jnp.where(jnp.logical_and(live, loader == dp), dest, -1)
    code = (loader * 64 + length).astype(jnp.float32)
    rows[...] = jnp.zeros_like(rows)
    for entry in range(6 * RSLOT + N_DP):
        if entry < 6 * RSLOT:
            target = lax.rem(dp // NY + 3 + NZ - entry // RSLOT, NZ) * NY + dp % NY
            picked = jnp.where(key_in == target * RSLOT + entry % RSLOT, code, 0.0)
        else:
            picked = jnp.where(key_out == entry - 6 * RSLOT, slot, 0.0)
        rows[entry : entry + 1, :] = jnp.sum(picked, axis=0, keepdims=True)
    total = lax.dot_general(
        jnp.ones((8, rows.shape[1]), jnp.float32), rows[...], (((1,), (1,)), ((), ())),
        precision=lax.Precision.HIGHEST, preferred_element_type=jnp.float32,
    )
    codes[...] = (total[0:1] + 0.5).astype(jnp.int32)


def table(tab_len, tab_dest, tab_off):
    vmem = pl.BlockSpec(memory_space=pltpu.VMEM)
    return pl.pallas_call(
        table_kernel,
        out_shape=jax.ShapeDtypeStruct((1, 128), jnp.int32),
        in_specs=[vmem] * 3,
        out_specs=vmem,
        scratch_shapes=[pltpu.VMEM((128, tab_len.shape[1]), jnp.float32)],
        name="table",
    )(tab_len, tab_dest, tab_off)


def shards(frames, ln_gain, w_in, depth_kernel, bn_scale, bn_shift, w_out, lengths, destinations, offsets):
    tab_len, tab_dest, tab_off = lengths[0], destinations[0], offsets[0]
    codes = table(tab_len.T, tab_dest.T, tab_off.T)
    out, _ = communicate(codes, frames[0], w_in, w_out, ln_gain, depth_kernel, bn_scale, bn_shift)
    return out[None]


def solution(mesh):
    return jax.shard_map(
        shards,
        mesh=mesh,
        in_specs=(
            P("fsdp", "dp", None, None),
            P(),
            P(("dp", "fsdp"), None),
            P(),
            P(),
            P(),
            P(("dp", "fsdp"), None),
            P("fsdp", None, None),
            P("fsdp", None, None),
            P("fsdp", None, None),
        ),
        out_specs=P("fsdp", "dp", None, None),
        check_vma=False,
    )
```

```python
import jax
import jax.numpy as jnp
from jax import lax
from jax.experimental import pallas as pl
from jax.experimental.pallas import tpu as pltpu
from jax.sharding import PartitionSpec as P

MESH = pl.DeviceIdType.MESH

D = 1536
KERNEL = 31
MAXLEN = 32
RSLOT = 8
NZ, NY, NX, NC = 8, 4, 4, 2
N_DP = NZ * NY
SHARD_ROWS = 6
BLOCK_ROWS = 24
CHUNK = D // NX
BLOCK_COLS = 3 * CHUNK
PAD = 16

HALF = MAXLEN // 2
PIECES = [(3, None), (1, None), (2, 0), (2, 1)]
ARRIVALS = [0, 7, 1, 6, 2, 5, 3, 4]
ORDER = (0, 3, 1, 2)


def comm_kernel(
    codes, frames_hbm, w_in_hbm, w_out_hbm, gain_hbm, taps_hbm, scale_hbm, shift_hbm, out, full,
    xbuf, wbuf, normed, hidden, window, act, gain, taps, scale, shift, w_sem,
    frames, w_in, w_out, wp, parts, block, staged,
    far0, far1, up2_0, up2_1, dn2_0, dn2_1, up3_0, up3_1, dn3_0, dn3_1, up4_0, up4_1, dn4_0, dn4_1, last0, last1,
    mu3_0, mu3_1, md3_0, md3_1, mu4_0, mu4_1, md4_0, md4_1,
    fy_send, fy_recv, fz_send, fz_recv,
    part_send, part_recv, local_sem,
    zu_send, zu_recv, zd_send, zd_recv,
    yu_send, yu_recv, yd_send, yd_recv,
    xu_send, xu_recv, xd_send, xd_recv,
    core_send, core_recv, lu_send, lu_recv, ld_send, ld_recv,
):
    dp = lax.axis_index("dp")
    fs = lax.axis_index("fsdp")
    z, y = dp // NY, dp % NY
    x, c = fs // NC, fs % NC
    other = 1 - c
    far, last = (far0, far1), (last0, last1)
    two = ((up2_0, up2_1), (dn2_0, dn2_1))
    three = ((up3_0, up3_1), (dn3_0, dn3_1))
    four = ((up4_0, up4_1), (dn4_0, dn4_1))
    merged3 = ((mu3_0, mu3_1), (md3_0, md3_1))
    merged4 = ((mu4_0, mu4_1), (md4_0, md4_1))

    def kept(cc):
        return pl.ds(pl.multiple_of(cc * BLOCK_ROWS, 8), BLOCK_ROWS)

    def dev(zz, yy, xx, cc):
        return (lax.rem(zz, NZ) * NY + lax.rem(yy, NY), lax.rem(xx, NX) * NC + cc)

    sibling = (dp, x * NC + other)
    z_next = (dev(z + 1, y, x, c), dev(z + NZ - 1, y, x, c))
    y_next = (dev(z, y + 1, x, c), dev(z, y + NY - 1, x, c))
    x_next = (dev(z, y, x + 1, c), dev(z, y, x + NX - 1, c))

    barrier = pltpu.get_barrier_semaphore()

    def greet(device):
        pl.semaphore_signal(barrier, inc=1, device_id=device, device_id_type=MESH)

    for k in range(1, NX * NC):
        greet((dp, lax.rem(fs + k, NX * NC)))
    for k in range(1, NY):
        greet(dev(z, y + k, x, c))
    for device in z_next:
        greet(device)

    loads = [
        pltpu.make_async_copy(w_in_hbm, w_in, local_sem.at[2]),
        pltpu.make_async_copy(w_out_hbm, w_out, local_sem.at[3]),
        pltpu.make_async_copy(frames_hbm, frames, local_sem.at[4]),
        pltpu.make_async_copy(gain_hbm, gain, local_sem.at[5]),
        pltpu.make_async_copy(taps_hbm, taps, local_sem.at[6]),
        pltpu.make_async_copy(scale_hbm, scale, local_sem.at[7]),
        pltpu.make_async_copy(shift_hbm, shift, local_sem.at[8]),
    ]
    for load in loads:
        load.start()

    def remote(src, dst, send, recv, device):
        return pltpu.make_async_remote_copy(
            src_ref=src, dst_ref=dst, send_sem=send, recv_sem=recv, device_id=device, device_id_type=MESH
        )

    started = []

    def start(src, dst, s_sem, r_sem, device):
        copy = remote(src, dst, s_sem, r_sem, device)
        copy.start()
        started.append(copy)

    def landed(ref, r_sem):
        remote(ref, ref, fy_send.at[0, 0, 0], r_sem, sibling).wait_recv()

    homes = {
        4: (far, 0), 3: (two[0], 2), 5: (two[1], 2), 2: (three[0], 6), 6: (three[1], 6),
        1: (four[0], 8), 7: (four[1], 8), 0: (last, 16),
    }

    def pick_frames(dz):
        for dy in range(NY):
            slot = codes[0, 6 * RSLOT + dev(z + dz, y + dy, x, c)[0]]
            if dy:
                staged[dz, dy - 1] = frames[slot]
            else:
                refs, first = homes[dz]
                for h in range(2):
                    refs[h][first + y] = frames[slot, h * HALF : (h + 1) * HALF, :]

    def send_frames(dz):
        refs, first = homes[dz]
        for h in range(2):
            for dy in (1, 3, 2):
                start(
                    staged.at[dz, dy - 1, pl.ds(h * HALF, HALF)], refs[h].at[first + y],
                    fy_send.at[dz, dy - 1, h], fy_recv.at[dz, dy - 1, h], dev(z, y + dy, x, c),
                )

    def frames_landed(dz, h):
        refs, first = homes[dz]
        for dy in (1, 3, 2):
            landed(refs[h].at[first + lax.rem(y + NY - dy, NY)], fy_recv.at[dz, dy - 1, h])

    wp[...] = jnp.zeros_like(wp)
    window[...] = jnp.zeros_like(window)
    for load in loads[:2]:
        load.wait()
    for t in range(NX):
        wp[t, 0:SHARD_ROWS, 0:CHUNK] = w_in[:, t * CHUNK : (t + 1) * CHUNK]
        wp[t, 0:SHARD_ROWS, CHUNK : 2 * CHUNK] = w_in[:, D + t * CHUNK : D + (t + 1) * CHUNK]
        wp[t, 0:SHARD_ROWS, 2 * CHUNK : 3 * CHUNK] = w_out[:, t * CHUNK : (t + 1) * CHUNK]
    loads[2].wait()
    pick_frames(4)
    pl.semaphore_wait(barrier, NX * NC + NY)

    slot_here = lax.rem(x, 2) * NC + c
    keeper = x // 2
    for t in range(NX):
        same = jnp.logical_and(x == t, keeper == c)

        @pl.when(jnp.logical_not(same))
        def _():
            remote(wp.at[t], parts.at[slot_here], part_send.at[t], part_recv.at[slot_here], (dp, t * NC + keeper)).start()

        @pl.when(same)
        def _():
            pltpu.make_async_copy(wp.at[t], parts.at[slot_here], local_sem.at[0]).start()

    send_frames(4)
    for dz in (3, 5):
        pick_frames(dz)

    for k in range(4):
        source = c * 4 + k

        @pl.when(source != fs)
        def _():
            landed(parts.at[k], part_recv.at[k])

        @pl.when(source == fs)
        def _():
            pltpu.make_async_copy(wp.at[0], parts.at[k], local_sem.at[0]).wait()

    row = lax.broadcasted_iota(jnp.int32, (BLOCK_ROWS, 32), 0)
    col = lax.broadcasted_iota(jnp.int32, (BLOCK_ROWS, 32), 1)
    pick = (col == (row // SHARD_ROWS) * 8 + lax.rem(row, SHARD_ROWS)).astype(jnp.bfloat16)
    block[...] = jnp.dot(
        pick, parts[...].reshape(32, BLOCK_COLS), preferred_element_type=jnp.float32
    ).astype(jnp.bfloat16)

    own = pltpu.make_async_copy(block, full.at[x, z, y, kept(c)], local_sem.at[1])
    own.start()

    def z_block(xx, dz, yy):
        return full.at[lax.rem(xx, NX), lax.rem(z + dz, NZ), lax.rem(yy, NY), kept(c)]

    def piece(xx, yy, half=None, cc=None):
        rows = slice(None) if half is None else pl.ds(half * 4, 4)
        return full.at[lax.rem(xx, NX), rows, lax.rem(yy, NY), kept(c if cc is None else cc)]

    def most(xx, yy, half=None, cc=None):
        rows = pl.ds(0, NZ - 1) if half is None else pl.ds(half * 4, 4 - half)
        return full.at[lax.rem(xx, NX), rows, lax.rem(yy, NY), kept(c if cc is None else cc)]

    def late(xx, yy, cc=None):
        return full.at[lax.rem(xx, NX), NZ - 1, lax.rem(yy, NY), kept(c if cc is None else cc)]

    def late_start(k):
        ref = late(x + ORDER[k + 1], y)
        start(ref, ref, lu_send.at[k], lu_recv.at[k], y_next[0])
        start(ref, ref, ld_send.at[k], ld_recv.at[k], y_next[1])

    def late_landed(k):
        below, above = late(x + ORDER[k + 1], y + 3), late(x + ORDER[k + 1], y + 1)
        landed(below, lu_recv.at[k])
        landed(above, ld_recv.at[k])
        if k == 1:
            start(above, above, ld_send.at[3], ld_recv.at[3], y_next[1])
        else:
            start(below, below, lu_send.at[3 + k // 2], lu_recv.at[3 + k // 2], y_next[0])
        to_core(20 + 3 * k, below)
        to_core(21 + 3 * k, above)

    def late_far_landed(k):
        ref = late(x + ORDER[k + 1], y + 2)
        landed(ref, ld_recv.at[3] if k == 1 else lu_recv.at[3 + k // 2])
        to_core(22 + 3 * k, ref)

    def spread(i):
        dz = ARRIVALS[i]
        ref = block if i == 0 else z_block(x, dz, y)
        dst = z_block(x, dz, y)
        step = (i + 1) // 2
        if i == 0 or (dz > 4 and step < 4):
            start(ref, dst, zu_send.at[step], zu_recv.at[step], z_next[0])
        if i == 0 or (dz < 4 and step < 3):
            start(ref, dst, zd_send.at[step], zd_recv.at[step], z_next[1])
        start(ref, dst, xu_send.at[i], xu_recv.at[i], x_next[0])
        start(ref, dst, xd_send.at[i], xd_recv.at[i], x_next[1])
        start(ref, dst, yu_send.at[i], yu_recv.at[i], y_next[0])
        start(ref, dst, yd_send.at[i], yd_recv.at[i], y_next[1])

    def z_landed(i):
        dz = ARRIVALS[i]
        step = (i - 1) // 2
        recv = zu_recv if dz >= 4 else zd_recv
        landed(z_block(x, dz, y), recv.at[step])

    def hop(step, h):
        for way in range(2):
            if step == 1:
                src, dst = far[h].at[pl.ds(2 * way, 2)], two[way][h].at[pl.ds(0, 2)]
            elif step == 2:
                src, dst = two[way][h], three[way][h].at[pl.ds(0, 6)]
            elif step == 3:
                src, dst = merged3[way][h], four[way][h].at[pl.ds(0, 8)]
            else:
                src, dst = merged4[way][h], last[h].at[pl.ds(8 * way, 8)]
            start(src, dst, fz_send.at[step - 1, way, h], fz_recv.at[step - 1, way, h], z_next[way])

    def hop_landed(step, h):
        for way in range(2):
            dst = (two[way][h].at[pl.ds(0, 2)], three[way][h].at[pl.ds(0, 6)],
                   four[way][h].at[pl.ds(0, 8)], last[h].at[pl.ds(8 * way, 8)])[step - 1]
            landed(dst, fz_recv.at[step - 1, way, h])

    def merge(step, h):
        for way in range(2):
            index = (1 if step == 3 else 2) if way == 0 else (5 if step == 3 else 4)
            for r in range(RSLOT):
                source = codes[0, index * RSLOT + r] // 64
                zs, ys = source // NY, lax.rem(source, NY)
                away = lax.rem((z - zs if way == 0 else zs - z) + NZ, NZ)
                if step == 3:
                    early = ys - 2 * way
                    early = jnp.where(jnp.logical_and(early >= 0, early < 2), early, 0)
                    at = jnp.where(away == 0, 6 + ys, jnp.where(away == 1, 2 + ys, early))
                    merged3[way][h][r] = three[way][h][at]
                else:
                    at = jnp.where(away == 0, 8 + ys, r)
                    merged4[way][h][r] = four[way][h][at]

    def to_core(sem, ref):
        start(ref, ref, core_send.at[sem], core_recv.at[sem], sibling)

    step_ids = lax.broadcasted_iota(jnp.int32, (MAXLEN, 128), 0)

    def norm(i, carry):
        for h in range(2):
            wide = xbuf[i, h * HALF : (h + 1) * HALF, :].astype(jnp.float32)
            mean = jnp.mean(wide, axis=1, keepdims=True)
            centred = wide - mean
            var = jnp.mean(centred * centred, axis=1, keepdims=True)
            normed[pl.ds(pl.multiple_of(i * MAXLEN + h * HALF, HALF), HALF), :] = (
                centred * lax.rsqrt(var + 1e-05) * gain[...].reshape(1, D)
            ).astype(jnp.bfloat16)
        return carry

    def load_row(dy):
        rows = lax.rem(y + dy, NY)
        far_chunk = full.at[lax.rem(x + ORDER[3], NX)]
        return pltpu.make_async_copy(far_chunk.at[:, rows], wbuf.at[3, :, rows], w_sem.at[3 + dy])

    def load_chunk(i):
        return pltpu.make_async_copy(
            full.at[lax.rem(x + ORDER[i], NX)], wbuf.at[i], w_sem.at[i]
        )

    def chunk(i):
        column = lax.rem(x + ORDER[i], NX) * CHUNK
        if i < 3:
            load_chunk(i).wait()
        else:
            for dy in range(NY):
                load_row(dy).wait()
        hidden[...] = jnp.dot(normed[...], wbuf[i, :, :, :, 0 : 2 * CHUNK].reshape(D, 2 * CHUNK), preferred_element_type=jnp.float32)
        for b in range(CHUNK // 128):
            lane = pl.ds(pl.multiple_of(column + b * 128, 128), 128)
            tap = [jnp.broadcast_to(taps[k : k + 1, lane], (8, 128)) for k in range(KERNEL)]
            mul = jnp.broadcast_to(scale[lane].reshape(1, 128), (16, 128))
            add = jnp.broadcast_to(shift[lane].reshape(1, 128), (16, 128))

            def conv(r, carry):
                base = pl.multiple_of(r * MAXLEN, MAXLEN)
                value = hidden[pl.ds(base, MAXLEN), b * 128 : b * 128 + 128]
                gate = hidden[pl.ds(base, MAXLEN), CHUNK + b * 128 : CHUNK + b * 128 + 128]
                gated = jnp.where(step_ids < lax.rem(codes[0, 3 * RSLOT + r], 64), value * jax.nn.sigmoid(gate), 0.0)
                window[r, PAD : PAD + MAXLEN, :] = gated
                total = [None] * 4
                for first in range(-7, MAXLEN):
                    rows = window[r, PAD + first : PAD + first + 8, :]
                    for t in range(4):
                        k = first + 15 - 8 * t
                        if 0 <= k < KERNEL:
                            term = rows * tap[k]
                            total[t] = term if total[t] is None else total[t] + term
                for pair in range(2):
                    s = jnp.concatenate(total[2 * pair : 2 * pair + 2], axis=0) * mul + add
                    act[pl.ds(pl.multiple_of(base + 16 * pair, 16), 16), lane] = (
                        s * jax.nn.sigmoid(s)
                    ).astype(jnp.bfloat16)
                return carry

            lax.fori_loop(0, RSLOT, conv, 0, unroll=8)

    spread(0)
    for dz in (3, 5):
        send_frames(dz)
    own.wait()
    for i in range(1, 8):
        z_landed(i)
        spread(i)
        if i == 2:
            frames_landed(4, 0)
            hop(1, 0)
        if i == 4:
            frames_landed(4, 1)
            hop(1, 1)
        if i in (5, 6):
            pick_frames((2, 6)[i - 5])
    to_core(0, piece(x, y))
    for dz in (2, 6):
        send_frames(dz)

    for h in range(2):
        hop_landed(1, h)
        frames_landed(3, h)
        frames_landed(5, h)
        hop(2, h)
    for dz in (1, 7, 0):
        pick_frames(dz)

    def x_start(j):
        dy, half = PIECES[j]
        ref = most(x, y + dy, half)
        start(ref, ref, xu_send.at[8 + j], xu_recv.at[8 + j], x_next[0])
        start(ref, ref, xd_send.at[8 + j], xd_recv.at[8 + j], x_next[1])
        to_core(1 + j, piece(x, y + dy, half))

    for i in range(8):
        landed(z_block(x, ARRIVALS[i], y + 3), yu_recv.at[i])
    ref = piece(x, y + 3, 0)
    start(ref, ref, yu_send.at[8], yu_recv.at[8], y_next[0])
    x_start(0)
    for i in range(8):
        landed(z_block(x, ARRIVALS[i], y + 1), yd_recv.at[i])
    ref = piece(x, y + 1, 1)
    start(ref, ref, yd_send.at[8], yd_recv.at[8], y_next[1])
    x_start(1)
    for dz in (1, 7):
        send_frames(dz)

    for h in range(2):
        hop_landed(2, h)
        frames_landed(2, h)
        frames_landed(6, h)
        merge(3, h)
        hop(3, h)

    for i in range(8):
        below, above = z_block(x + 3, ARRIVALS[i], y), z_block(x + 1, ARRIVALS[i], y)
        landed(below, xu_recv.at[i])
        landed(above, xd_recv.at[i])
        if i % 2 == 0:
            start(below, below, xu_send.at[12 + i // 2], xu_recv.at[12 + i // 2], x_next[0])
        else:
            start(above, above, xd_send.at[12 + i // 2], xd_recv.at[12 + i // 2], x_next[1])
    to_core(5, piece(x + 3, y))
    to_core(6, piece(x + 1, y))
    late_start(0)
    late_start(1)
    send_frames(0)

    landed(piece(x, y + 2, 0), yu_recv.at[8])
    x_start(2)
    landed(piece(x, y + 2, 1), yd_recv.at[8])
    x_start(3)

    def x_landed(j):
        dy, half = PIECES[j]
        below, above = most(x + 3, y + dy, half), most(x + 1, y + dy, half)
        landed(below, xu_recv.at[8 + j])
        landed(above, xd_recv.at[8 + j])
        if half in (None, 0):
            ref = most(x + 3, y + dy, 0)
            start(ref, ref, xu_send.at[16 + j], xu_recv.at[16 + j], x_next[0])
        if half in (None, 1):
            ref = most(x + 1, y + dy, 1)
            start(ref, ref, xd_send.at[16 + j], xd_recv.at[16 + j], x_next[1])
        to_core(7 + j, below)
        to_core(11 + j, above)

    def x_far_landed(j):
        dy, half = PIECES[j]
        if half in (None, 0):
            landed(most(x + 2, y + dy, 0), xu_recv.at[16 + j])
        if half in (None, 1):
            landed(most(x + 2, y + dy, 1), xd_recv.at[16 + j])
        to_core(15 + j, most(x + 2, y + dy, half))

    x_landed(0)
    for i in range(8):
        recv = xu_recv if i % 2 == 0 else xd_recv
        landed(z_block(x + 2, ARRIVALS[i], y), recv.at[12 + i // 2])
    to_core(19, piece(x + 2, y))
    late_start(2)

    for h in range(2):
        hop_landed(3, h)
        frames_landed(1, h)
        frames_landed(7, h)
        merge(4, h)
        hop(4, h)
    landed(piece(x, y, None, other), core_recv.at[0])
    for j, (dy, half) in enumerate(PIECES):
        landed(piece(x, y + dy, half, other), core_recv.at[1 + j])
    load_chunk(0).start()
    for k in range(3):
        late_landed(k)
    x_landed(1)
    x_far_landed(0)
    x_landed(2)
    x_far_landed(1)
    for k in range(3):
        late_far_landed(k)
    x_landed(3)

    for load in loads[3:]:
        load.wait()
    for h in range(2):
        hop_landed(4, h)
        frames_landed(0, h)
        for r in range(RSLOT):
            source = codes[0, 3 * RSLOT + r] // 64
            zs, ys = source // NY, lax.rem(source, NY)
            away = lax.rem(z - zs + NZ, NZ)
            above = jnp.logical_or(away > 4, jnp.logical_and(away == 4, ys >= 2))
            at = jnp.where(away == 0, 16 + ys, jnp.where(above, 8 + r, r))
            xbuf[r, h * HALF : (h + 1) * HALF, :] = last[h][at]
    x_far_landed(2)
    lax.fori_loop(0, RSLOT, norm, 0)

    for i, (first, whole) in ((1, (7, 5)), (2, (11, 6))):
        landed(piece(x + ORDER[i], y, None, other), core_recv.at[whole])
        for j, (dy, half) in enumerate(PIECES):
            landed(most(x + ORDER[i], y + dy, half, other), core_recv.at[first + j])
        for j, dy in enumerate((3, 1, 2)):
            landed(late(x + ORDER[i], y + dy, other), core_recv.at[17 + 3 * i + j])
        load_chunk(i).start()
    chunk(0)
    x_far_landed(3)
    chunk(1)
    for j, dy in enumerate((3, 1, 2)):
        landed(late(x + 2, y + dy, other), core_recv.at[26 + j])
    landed(piece(x + 2, y, None, other), core_recv.at[19])
    load_row(0).start()
    for j in range(2):
        dy = PIECES[j][0]
        landed(most(x + 2, y + dy, None, other), core_recv.at[15 + j])
        load_row(dy).start()
    chunk(2)
    for j in range(2, 4):
        landed(most(x + 2, y + 2, PIECES[j][1], other), core_recv.at[15 + j])
    load_row(2).start()
    chunk(3)
    for i in range(NX):
        lane = pl.ds(pl.multiple_of(lax.rem(x + ORDER[i], NX) * CHUNK, 128), CHUNK)
        hidden[:, 0:CHUNK] = jnp.dot(
            act[...], wbuf[i, :, :, :, 2 * CHUNK : 3 * CHUNK].reshape(D, CHUNK), preferred_element_type=jnp.float32
        )

        ids = lax.broadcasted_iota(jnp.int32, (MAXLEN, CHUNK), 0)

        def close(r, carry):
            mixed = xbuf[r, :, lane].astype(jnp.float32) + hidden[
                pl.ds(pl.multiple_of(r * MAXLEN, MAXLEN), MAXLEN), 0:CHUNK
            ]
            out[r, :, lane] = jnp.where(ids < lax.rem(codes[0, 3 * RSLOT + r], 64), mixed, 0.0).astype(jnp.bfloat16)
            return carry

        lax.fori_loop(0, RSLOT, close, 0, unroll=4)

    for t in range(NX):
        same = jnp.logical_and(x == t, keeper == c)

        @pl.when(jnp.logical_not(same))
        def _():
            remote(wp.at[t], parts.at[0], part_send.at[t], part_recv.at[0], sibling).wait_send()

    for copy in started:
        copy.wait_send()


def communicate(codes, frames, w_in, w_out, gain, taps, scale, shift):
    dma = pltpu.SemaphoreType.DMA
    smem = pl.BlockSpec(memory_space=pltpu.SMEM)
    vmem = pl.BlockSpec(memory_space=pltpu.VMEM)
    hbm = pl.BlockSpec(memory_space=pltpu.HBM)

    def slots(n):
        return [pltpu.VMEM((n, HALF, D), jnp.bfloat16)]

    return pl.pallas_call(
        comm_kernel,
        out_shape=(
            jax.ShapeDtypeStruct((RSLOT, MAXLEN, D), jnp.bfloat16),
            jax.ShapeDtypeStruct((NX, NZ, NY, NC * BLOCK_ROWS, BLOCK_COLS), jnp.bfloat16),
        ),
        in_specs=[smem] + [hbm] * 7,
        out_specs=(vmem, pl.BlockSpec(memory_space=pl.ANY)),
        scratch_shapes=[
            pltpu.VMEM((RSLOT, MAXLEN, D), jnp.bfloat16),
            pltpu.VMEM((NX, NZ, NY, NC * BLOCK_ROWS, BLOCK_COLS), jnp.bfloat16),
            pltpu.VMEM((RSLOT * MAXLEN, D), jnp.bfloat16),
            pltpu.VMEM((RSLOT * MAXLEN, 2 * CHUNK), jnp.float32),
            pltpu.VMEM((RSLOT, MAXLEN + 2 * PAD, 128), jnp.float32),
            pltpu.VMEM((RSLOT * MAXLEN, D), jnp.bfloat16),
            pltpu.VMEM((D,), jnp.float32),
            pltpu.VMEM((KERNEL, D), jnp.float32),
            pltpu.VMEM((D,), jnp.float32),
            pltpu.VMEM((D,), jnp.float32),
            dma((NX + 3,)),
            pltpu.VMEM(frames.shape, jnp.bfloat16),
            pltpu.VMEM(w_in.shape, jnp.bfloat16),
            pltpu.VMEM(w_out.shape, jnp.bfloat16),
            pltpu.VMEM((NX, 8, BLOCK_COLS), jnp.bfloat16),
            pltpu.VMEM((4, 8, BLOCK_COLS), jnp.bfloat16),
            pltpu.VMEM((BLOCK_ROWS, BLOCK_COLS), jnp.bfloat16),
            pltpu.VMEM((NZ, NY - 1, MAXLEN, D), jnp.bfloat16),
            *(slots(4) * 2 + slots(6) * 4 + slots(10) * 4 + slots(12) * 4 + slots(20) * 2 + slots(8) * 8),
            dma((NZ, NY - 1, 2)), dma((NZ, NY - 1, 2)), dma((4, 2, 2)), dma((4, 2, 2)),
            dma((4,)), dma((4,)), dma((9,)),
            dma((4,)), dma((4,)), dma((3,)), dma((3,)),
            dma((9,)), dma((9,)), dma((9,)), dma((9,)),
            dma((20,)), dma((20,)), dma((20,)), dma((20,)),
            dma((29,)), dma((29,)), dma((5,)), dma((5,)), dma((4,)), dma((4,)),
        ],
        compiler_params=pltpu.CompilerParams(
            collective_id=0, has_side_effects=True, vmem_limit_bytes=67043328
        ),
        name="exchange",
    )(codes, frames, w_in, w_out, gain, taps, scale, shift)


def table_kernel(tab_len, tab_dest, tab_off, codes, rows):
    dp = lax.axis_index("dp")
    length, dest = tab_len[...], tab_dest[...]
    live = length > 0
    loader = lax.broadcasted_iota(jnp.int32, length.shape, 1)
    slot = lax.broadcasted_iota(jnp.int32, length.shape, 0).astype(jnp.float32)
    key_in = jnp.where(live, dest * RSLOT + tab_off[...] // MAXLEN, -1)
    key_out = jnp.where(jnp.logical_and(live, loader == dp), dest, -1)
    code = (loader * 64 + length).astype(jnp.float32)
    rows[...] = jnp.zeros_like(rows)
    for entry in range(6 * RSLOT + N_DP):
        if entry < 6 * RSLOT:
            target = lax.rem(dp // NY + 3 + NZ - entry // RSLOT, NZ) * NY + dp % NY
            picked = jnp.where(key_in == target * RSLOT + entry % RSLOT, code, 0.0)
        else:
            picked = jnp.where(key_out == entry - 6 * RSLOT, slot, 0.0)
        rows[entry : entry + 1, :] = jnp.sum(picked, axis=0, keepdims=True)
    total = lax.dot_general(
        jnp.ones((8, rows.shape[1]), jnp.float32), rows[...], (((1,), (1,)), ((), ())),
        precision=lax.Precision.HIGHEST, preferred_element_type=jnp.float32,
    )
    codes[...] = (total[0:1] + 0.5).astype(jnp.int32)


def table(tab_len, tab_dest, tab_off):
    vmem = pl.BlockSpec(memory_space=pltpu.VMEM)
    return pl.pallas_call(
        table_kernel,
        out_shape=jax.ShapeDtypeStruct((1, 128), jnp.int32),
        in_specs=[vmem] * 3,
        out_specs=vmem,
        scratch_shapes=[pltpu.VMEM((128, tab_len.shape[1]), jnp.float32)],
        name="table",
    )(tab_len, tab_dest, tab_off)


def shards(frames, ln_gain, w_in, depth_kernel, bn_scale, bn_shift, w_out, lengths, destinations, offsets):
    tab_len, tab_dest, tab_off = lengths[0], destinations[0], offsets[0]
    codes = table(tab_len.T, tab_dest.T, tab_off.T)
    out, _ = communicate(codes, frames[0], w_in, w_out, ln_gain, depth_kernel, bn_scale, bn_shift)
    return out[None]


def solution(mesh):
    return jax.shard_map(
        shards,
        mesh=mesh,
        in_specs=(
            P("fsdp", "dp", None, None),
            P(),
            P(("dp", "fsdp"), None),
            P(),
            P(),
            P(),
            P(("dp", "fsdp"), None),
            P("fsdp", None, None),
            P("fsdp", None, None),
            P("fsdp", None, None),
        ),
        out_specs=P("fsdp", "dp", None, None),
        check_vma=False,
    )
```
